128 devices in a mesh: fsdp: 4 (over y_lo, core), ctx: 8 (over y_hi, z), tp: 4 (over x).
Axes of the slice: x: 4, y: 4 (y_hi: 2, y_lo: 2; y = y_hi * 2 + y_lo), z: 4, core: 2. Of those that a mesh axis runs over, the one named last changes fastest.
Arguments:
- layer_input: bfloat16 [16, 2048, 768], P('fsdp', 'ctx'), may hold values from -6 to 6
- segment_ids: int32 [16, 2048], P('fsdp', 'ctx'), may hold values from 0 to 3, never falling along the last dimension, each value on 1 to 1280 neighbouring positions
- proj_weight: bfloat16 [3, 768, 768], P(None, 'fsdp', 'tp'), may hold values from -0.21875 to 0.21875
- proj_bias: bfloat16 [2, 768], P(None, 'tp'), may hold values from -3 to 3
- out_weight: bfloat16 [768, 768], P('tp', 'fsdp'), may hold values from -2.5 to 2.5
- out_bias: bfloat16 [768], P('fsdp'), may hold values from -3 to 3
- first_gain: bfloat16 [768], P('fsdp'), may hold values from 0.099609375 to 1.8984375
- first_shift: bfloat16 [768], P('fsdp'), may hold values from -2 to 2
- up_weight: bfloat16 [768, 3072], P('fsdp', 'tp'), may hold values from -0.21875 to 0.21875
- up_bias: bfloat16 [3072], P('tp'), may hold values from -3 to 3
- down_weight: bfloat16 [3072, 768], P('tp', 'fsdp'), may hold values from -0.15625 to 0.15625
- down_bias: bfloat16 [768], P('fsdp'), may hold values from -2 to 2
- second_gain: bfloat16 [768], P('fsdp'), may hold values from 0.099609375 to 1.8984375
- second_shift: bfloat16 [768], P('fsdp'), may hold values from -2 to 2
- cotangent: bfloat16 [16, 2048, 768], P('fsdp', 'ctx'), may hold values from -6 to 6
Outputs:
- layer_output: bfloat16 [16, 2048, 768], P('fsdp', 'ctx')
- input_grad: float32 [16, 2048, 768], P('fsdp', 'ctx')
- proj_grad: float32 [3, 768, 768], P(None, ('fsdp', 'ctx'), 'tp')
- proj_bias_grad: float32 [2, 768], P(None, 'tp')
- out_grad: float32 [768, 768], P('tp', ('fsdp', 'ctx'))
- out_bias_grad: float32 [768], P(('fsdp', 'ctx'))
- first_gain_grad: float32 [768], P(('fsdp', 'ctx'))
- first_shift_grad: float32 [768], P(('fsdp', 'ctx'))
- up_grad: float32 [768, 3072], P(('fsdp', 'ctx'), 'tp')
- up_bias_grad: float32 [3072], P('tp')
- down_grad: float32 [3072, 768], P('tp', ('fsdp', 'ctx'))
- down_bias_grad: float32 [768], P(('fsdp', 'ctx'))
- second_gain_grad: float32 [768], P(('fsdp', 'ctx'))
- second_shift_grad: float32 [768], P(('fsdp', 'ctx'))
The draws below stay inside these ranges and needn't reach their ends.
Inputs may be any that keep to these rules, and one draw needn't show every extreme that they name: `segment_ids`: ids never fall along a sequence; every document spans 1 to 1280 positions, and one in each sequence spans exactly 1280.
All inputs are finite; a program needn't handle non-finite values.
Results may differ from the reference program's by a relative error of at most 0.039.
Values may be sent and summed in bfloat16 or wider, within the bound.
A program may use at most 192 MiB of HBM per device.

```python
import math
import jax
import jax.numpy as jnp
import numpy as np
from jax import lax

D = 768
HEADS = 12
HEAD_DIM = 64
FF = 3072
SEQ_LEN = 2048
DOCS = 4
LONGEST = 1280
NSEQ = 16


def levels(own_key, shape, shards, low, high):
    level, own = 1.0, jax.random.fold_in(own_key, 6)
    for dim, shards_of in shards:
        heights = jnp.exp(jax.random.uniform(jax.random.fold_in(own, dim), (shards_of,), jnp.float32, low / len(shards), high / len(shards)))
        level = level * jnp.repeat(heights, shape[dim] // shards_of).reshape([-1 if axis == dim else 1 for axis in range(len(shape))])
    return level


def length_profile(number_of, total, limit, slope):
    portions = [(1 << 20) // math.isqrt(standing ** slope) + 1 for standing in range(2, number_of + 1)]
    rest, counts = total - limit - (number_of - 1), [1] * (number_of - 1)
    while rest > 0:
        candidates = [i for i in range(number_of - 1) if counts[i] < limit]
        whole, left = sum([portions[i] for i in candidates]), rest
        for i in candidates:
            more = min(limit - counts[i], max(1, left * portions[i] // whole), rest)
            counts[i] = counts[i] + more
            rest = rest - more
    return np.array([limit] + counts)


def ragged_sizes(stream_key, number_of, total, bound, skew):
    if number_of == 2:
        one = jax.random.randint(stream_key, (), max(1, total - bound), min(bound, total - 1) + 1)
        return jnp.stack([one, total - one])
    sizes = jnp.asarray(length_profile(number_of, total, bound, skew), jnp.int32)
    twos = (number_of - 1) // 2
    donor, receiver = sizes[1:1 + 2 * twos:2], sizes[2:2 + 2 * twos:2]
    slack = jnp.minimum(donor - 1, bound - receiver)
    shifted = jax.random.randint(jax.random.fold_in(stream_key, 1), (twos,), 0, 1 << 20) % (slack + 1)
    sizes = sizes.at[1:1 + 2 * twos:2].set(donor - shifted).at[2:2 + 2 * twos:2].set(receiver + shifted)
    return sizes[jax.random.permutation(jax.random.fold_in(stream_key, 2), number_of)]


def scatter_about(stream_key, shape, scale, reach, shards=(), dtype=jnp.bfloat16):
    array = jax.random.normal(stream_key, shape, jnp.float32) * scale
    if len(shards) > 0:
        array = levels(stream_key, shape, shards, -0.22, 0.18) * array
    return jnp.clip(array, min=-reach, max=reach).astype(dtype)


def setup_inputs(seed: int = 0) -> dict:
    streams_of = jax.random.split(jax.random.key(seed), 16)
    return {
        "layer_input": scatter_about(streams_of[0], (NSEQ, SEQ_LEN, D), 1.0, 6.0, ((0, 4), (1, 8))),
        "segment_ids": jax.vmap(lambda own: jnp.searchsorted(jnp.cumsum(ragged_sizes(own, DOCS, SEQ_LEN, LONGEST, 0)), jnp.arange(SEQ_LEN), side="right"))(jax.random.split(streams_of[1], NSEQ)).reshape((NSEQ, SEQ_LEN)).astype(jnp.int32),
        "proj_weight": scatter_about(streams_of[2], (3, D, D), D ** -0.5, 0.21875, ((1, 4), (2, 4))),
        "proj_bias": scatter_about(streams_of[3], (2, D), 0.5, 3.0, ((1, 4),)),
        "out_weight": scatter_about(streams_of[4], (D, D), (max(D // 128, 2)) ** -0.5, 2.5, ((0, 4), (1, 4))),
        "out_bias": scatter_about(streams_of[5], (D,), 0.5, 3.0, ((0, 4),)),
        "first_gain": jnp.clip(1.0 + 0.18 * jax.random.normal(streams_of[6], (D,), jnp.float32), 0.099609375, 1.8984375).astype(jnp.bfloat16),
        "first_shift": scatter_about(streams_of[7], (D,), 0.3, 2.0, ((0, 4),)),
        "up_weight": scatter_about(streams_of[8], (D, FF), D ** -0.5, 0.21875, ((0, 4), (1, 4))),
        "up_bias": scatter_about(streams_of[9], (FF,), 0.5, 3.0, ((0, 4),)),
        "down_weight": scatter_about(streams_of[10], (FF, D), (FF // 2) ** -0.5, 0.15625, ((0, 4), (1, 4))),
        "down_bias": scatter_about(streams_of[11], (D,), 0.3, 2.0, ((0, 4),)),
        "second_gain": jnp.clip(1.0 + 0.18 * jax.random.normal(streams_of[12], (D,), jnp.float32), 0.099609375, 1.8984375).astype(jnp.bfloat16),
        "second_shift": scatter_about(streams_of[13], (D,), 0.3, 2.0, ((0, 4),)),
        "cotangent": scatter_about(streams_of[14], (NSEQ, SEQ_LEN, D), 1.0, 6.0, ((0, 4), (1, 8))),
    }


@jax.custom_vjp
def low(v):
    return lax.optimization_barrier(v.astype(jnp.bfloat16)).astype(jnp.float32)

@jax.custom_vjp
def low_back(v):
    return v

def low_keep(v):
    return (low(v), None)

def low_pass(kept, grad):
    return (grad,)

def back_keep(v):
    return (v, None)

def back_low(kept, grad):
    return (low(grad),)
low.defvjp(low_keep, low_pass)
low_back.defvjp(back_keep, back_low)
norm_eps = 1e-12
highest = lax.Precision.HIGHEST

def layer_norm(values_in, gain, shift):
    centre = lax.optimization_barrier(jnp.mean(values_in, axis=-1, keepdims=True))
    centred = values_in - centre
    spread = lax.optimization_barrier(jnp.mean(centred * centred, axis=-1, keepdims=True))
    return centred * lax.rsqrt(spread + norm_eps) * gain + shift

def matmul(left, right):
    return jnp.dot(left, right, precision=highest)

def attention_block(queries, key_rows, value_rows, query_docs, key_docs):
    raw_scores = jnp.einsum('qhd,khd->hqk', queries, key_rows, precision=highest) * HEAD_DIM ** (-0.5)
    scores = low_back(raw_scores)
    same_doc = query_docs[None, :, None] == key_docs[None, None, :]
    attn_probs = jax.nn.softmax(jnp.where(same_doc, scores, -1e+30), axis=-1)
    return jnp.einsum('hqk,khd->qhd', low(attn_probs), value_rows, precision=highest)

def forward(seq_input, seq_docs, params):
    proj_full, proj_shift, out_full, out_shift, gain_one, shift_one, up_full, up_shift, down_full, down_shift, gain_two, shift_two = params
    length = seq_input.shape[0]
    input_low = low(seq_input)
    proj_pre = low_back(jnp.einsum('ld,tdc->tlc', input_low, proj_full, precision=highest))
    queries = low(proj_pre[0] + proj_shift[0]).reshape(length, HEADS, HEAD_DIM)
    key_rows = low(proj_pre[1]).reshape(length, HEADS, HEAD_DIM)
    value_rows = low(proj_pre[2] + proj_shift[1]).reshape(length, HEADS, HEAD_DIM)
    block_len = min(512, length)

    def one_block(block_part):
        return attention_block(block_part[0], key_rows, value_rows, block_part[1], seq_docs)
    attended = lax.map(jax.checkpoint(one_block), (queries.reshape(length // block_len, block_len, HEADS, HEAD_DIM), seq_docs.reshape(length // block_len, block_len)))
    context = low_back(low(attended.reshape(length, D)))
    first_sum = seq_input + low_back(matmul(context, out_full)) + out_shift
    first_norm = layer_norm(first_sum, gain_one, shift_one)
    up_pre = low_back(matmul(low(first_norm), up_full)) + up_shift
    activated = low_back(low(jax.nn.gelu(up_pre, approximate=False)))
    second_sum = first_norm + low_back(matmul(activated, down_full)) + down_shift
    return layer_norm(second_sum, gain_two, shift_two)

def reference(layer_input, segment_ids, proj_weight, proj_bias, out_weight, out_bias, first_gain, first_shift, up_weight, up_bias, down_weight, down_bias, second_gain, second_shift, cotangent):
    params = tuple((weight_in.astype(jnp.float32) for weight_in in (proj_weight, proj_bias, out_weight, out_bias, first_gain, first_shift, up_weight, up_bias, down_weight, down_bias, second_gain, second_shift)))

    def seq_step(totals, seq_item):
        seq_input, seq_docs, seq_cot = seq_item
        seq_output, pullback = jax.vjp(lambda inputs_f, params_f: forward(inputs_f, seq_docs, params_f), seq_input.astype(jnp.float32), params)
        grad_input, grad_params = pullback(seq_cot.astype(jnp.float32))
        totals = jax.tree.map(jnp.add, totals, grad_params)
        return (totals, (seq_output.astype(jnp.bfloat16), grad_input))
    zero_grads = jax.tree.map(jnp.zeros_like, params)
    totals, (outputs, input_grads) = lax.scan(seq_step, zero_grads, (layer_input, segment_ids, cotangent))
    return (outputs, input_grads, totals[0], totals[1], totals[2], totals[3], totals[4], totals[5], totals[6], totals[7], totals[8], totals[9], totals[10], totals[11])
```

```python
import functools
import math

import jax
import jax.numpy as jnp
import numpy as np
from jax import lax
from jax.experimental import pallas as pl
from jax.experimental.pallas import tpu as pltpu
from jax.sharding import PartitionSpec as P

HEAD_DIM = 64
NORM_EPS = 1e-12
MESH = pl.DeviceIdType.MESH
bf=jnp.bfloat16; f32=jnp.float32

class Place:
    def __init__(self):
        self.x=lax.axis_index("tp"); f=lax.axis_index("fsdp"); c=lax.axis_index("ctx")
        self.yl=f//2; self.core=f%2; self.yh=c//4; self.z=c%4
        self.y=self.yh*2+self.yl
    def px(self,k):
        q=(self.x+k)%4
        return {"tp":q}, q
    def pz(self,k):
        q=(self.z+k)%4
        return {"ctx":self.yh*4+q}, q
    def py(self,k):
        q=(self.y+k)%4
        return {"fsdp":(q%2)*2+self.core,"ctx":(q//2)*4+self.z}, (q%2,q//2)
    def sib(self):
        return {"fsdp":self.yl*2+1-self.core}

def greet(devs):
    bar=pltpu.get_barrier_semaphore()
    for d in devs: pl.semaphore_signal(bar,inc=1,device_id=d,device_id_type=MESH)
    pl.semaphore_wait(bar,len(devs))

def rcopy(src,dst,ss,rs,dev):
    return pltpu.make_async_remote_copy(src_ref=src,dst_ref=dst,send_sem=ss,recv_sem=rs,device_id=dev,device_id_type=MESH)

def gather_kernel(pk,vec,W,V,ss,rs,ls):
    p=Place(); x,yl,core,yh,z=p.x,p.yl,p.core,p.yh,p.z
    nb={"fsdp":(1-yl)*2+core}
    greet([p.px(k)[0] for k in (1,2,3)]+[p.pz(k)[0] for k in (1,2,3)]+[p.py(k)[0] for k in (1,2,3)]+[nb_dev(p) for nb_dev in (lambda q:q.sib(),)])
    n=[0]; sent=[]
    def sem():
        n[0]+=1; return n[0]-1
    def send(src,dst,dev):
        i=sem(); c=rcopy(src,dst,ss.at[i],rs.at[i],dev); c.start(); sent.append(c); return c
    own=pltpu.make_async_copy(pk,W.at[:,x,yl,core],ls.at[0]); own.start()
    ownv=pltpu.make_async_copy(vec,V.at[x,yl,core],ls.at[1]); ownv.start()
    half=pl.ds(pl.multiple_of(yh*96,8),96); quar=pl.ds(pl.multiple_of(z*48,8),48)
    nbd,_=p.py(1)
    a0=send(pk.at[0],W.at[0,x,yl,core],nb)
    av=send(vec,V.at[x,yl,core],nb)
    a2=send(pk.at[2,quar],W.at[2,x,yl,core,quar],nb)
    b1=[send(pk.at[1,half],W.at[1,x,yl,core,half],p.px(k)[0]) for k in (1,2,3)]
    b2=[send(pk.at[2,quar],W.at[2,x,yl,core,quar],p.px(k)[0]) for k in (1,2,3)]
    b0=[send(pk.at[0],W.at[0,x,yl,core],p.px(k)[0]) for k in (1,2,3)]
    bv=[send(vec,V.at[x,yl,core],p.px(k)[0]) for k in (1,2,3)]
    c1=[send(pk.at[1,half],W.at[1,x,yl,core,half],p.py(k)[0]) for k in (1,3)]
    d=[send(pk.at[j],W.at[j,x,yl,core],p.sib()) for j in range(3)]
    dv=[send(vec,V.at[x,yl,core],p.sib())]
    a2.wait_recv()
    b2n=[send(W.at[2,x,1-yl,core,quar],W.at[2,x,1-yl,core,quar],p.px(k)[0]) for k in (1,2,3)]
    c2=[send(W.at[2,x,1-yl,core,quar],W.at[2,x,1-yl,core,quar],p.pz(k)[0]) for k in (1,2,3)]
    a0.wait_recv(); av.wait_recv()
    b0n=[send(W.at[0,x,1-yl,core],W.at[0,x,1-yl,core],p.px(k)[0]) for k in (1,2,3)]
    bvn=[send(V.at[x,1-yl,core],V.at[x,1-yl,core],p.px(k)[0]) for k in (1,2,3)]
    d.append(send(W.at[0,x,1-yl,core],W.at[0,x,1-yl,core],p.sib()))
    dv.append(send(V.at[x,1-yl,core],V.at[x,1-yl,core],p.sib()))
    c1n=[]; c2n=[]
    for k in (1,2,3):
        t=(x-k+4)%4
        b1[k-1].wait_recv()
        c1n.append([send(W.at[1,t,yl,core,half],W.at[1,t,yl,core,half],p.py(j)[0]) for j in (1,2,3)])
        b2[k-1].wait_recv()
        c2n.append([send(W.at[2,t,yl,core,quar],W.at[2,t,yl,core,quar],p.pz(j)[0]) for j in (1,2,3)])
    for k in (1,2,3):
        t=(x-k+4)%4
        b2n[k-1].wait_recv()
        c2n.append([send(W.at[2,t,1-yl,core,quar],W.at[2,t,1-yl,core,quar],p.pz(j)[0]) for j in (1,2,3)])
    for k in (1,2,3):
        t=(x-k+4)%4
        b0[k-1].wait_recv(); bv[k-1].wait_recv()
        d.append(send(W.at[0,t,yl,core],W.at[0,t,yl,core],p.sib()))
        dv.append(send(V.at[t,yl,core],V.at[t,yl,core],p.sib()))
    for c in c2: c.wait_recv()
    d.append(send(W.at[2,x,1-yl,core],W.at[2,x,1-yl,core],p.sib()))
    for c in c1: c.wait_recv()
    d.append(send(W.at[1,x,1-yl,core],W.at[1,x,1-yl,core],p.sib()))
    for k in (1,2,3):
        t=(x-k+4)%4
        for c in c1n[k-1]: c.wait_recv()
        d.append(send(W.at[1,t],W.at[1,t],p.sib()) if False else send(W.at[1,t,:,core],W.at[1,t,:,core],p.sib()))
        for c in c2n[k-1]: c.wait_recv()
        d.append(send(W.at[2,t,yl,core],W.at[2,t,yl,core],p.sib()))
    for k in (1,2,3):
        t=(x-k+4)%4
        b0n[k-1].wait_recv(); bvn[k-1].wait_recv()
        d.append(send(W.at[0,t,1-yl,core],W.at[0,t,1-yl,core],p.sib()))
        dv.append(send(V.at[t,1-yl,core],V.at[t,1-yl,core],p.sib()))
        for c in c2n[2+k]: c.wait_recv()
        d.append(send(W.at[2,t,1-yl,core],W.at[2,t,1-yl,core],p.sib()))
    for c in d+dv: c.wait_recv()
    for c in sent: c.wait_send()
    own.wait(); ownv.wait()
NS_G=96
def gather_weights(pk,vec,cid):
    return pl.pallas_call(gather_kernel,out_shape=(jax.ShapeDtypeStruct((3,4,2,2,192,768),bf),jax.ShapeDtypeStruct((4,2,2,8,768),bf)),
      in_specs=[pl.BlockSpec(memory_space=pl.ANY)]*2,out_specs=[pl.BlockSpec(memory_space=pl.ANY)]*2,
      scratch_shapes=[pltpu.SemaphoreType.DMA((NS_G,)),pltpu.SemaphoreType.DMA((NS_G,)),pltpu.SemaphoreType.DMA((2,))],
      compiler_params=pltpu.CompilerParams(collective_id=cid,has_side_effects=True))(pk,vec)

DIMS = {"x": (4,), "y": (2, 2), "z": (4,)}
ORDER = ("xyz", "yzx", "zxy")


def shape_of(axes):
    return sum([DIMS[d] for d in "xyz" if d in axes], ())


def split_index(i, shape):
    out = []
    for s in reversed(shape):
        out.insert(0, i % s)
        i = i // s
    return tuple(out)


def pick(ref, axis, q, left):
    at = []
    for d in "xyz":
        if d in left:
            at += list(q if d == "y" else (q,)) if d == axis else [slice(None)] * len(DIMS[d])
    return ref.at[tuple(at)]


def total(dst, first, others, shape):
    count = math.prod(shape)

    @pl.loop(0, count)
    def _(i):
        at = split_index(i, shape)
        a = first[at].astype(f32)
        for o in others:
            a = a + o[at].astype(f32)
        dst[at] = a.astype(dst.dtype)


def reduce_kernel(g0, g1, g2, vin, R, V, acc, cor, *refs):
    s1, r1, s2, r2 = refs[0:3], refs[3:6], refs[6:9], refs[9:12]
    r3, vr, vt, ss, rs, ls = refs[12:]
    p = Place()
    x, yl, core, yh, z = p.x, p.yl, p.core, p.yh, p.z
    peers = {"x": p.px, "y": p.py, "z": p.pz}
    here = {"x": x, "y": (yl, yh), "z": z}
    greet([peers[a](k)[0] for a in "xyz" for k in (1, 2, 3)] + [p.sib()])
    sent = []

    def send(src, dst, dev):
        i = len(sent)
        c = rcopy(src, dst, ss.at[i], rs.at[i], dev)
        c.start()
        sent.append(c)
        return c

    g = [g0, g1, g2]
    turn = (1, 2, 0)
    cv = send(vin, vr.at[0, 0], p.sib())
    cc, ll = {}, {}
    for k in turn:
        cc[k] = send(g[k].at[:, :, 1 - core], cor.at[k], p.sib())
        ll[k] = pltpu.make_async_copy(g[k].at[:, :, core], acc.at[k], ls.at[k])
        ll[k].start()
    cv.wait_recv()
    vt[0] = vin[...] + vr[0, 0]

    def vsend(i, a):
        return [send(vt.at[i], vr.at[i + 1, j - 1], peers[a](j)[0]) for j in (1, 2, 3)]

    def vsum(i, cs):
        for c in cs:
            c.wait_recv()
        return vt[i] + vr[i + 1, 0] + vr[i + 1, 1] + vr[i + 1, 2]

    vx = vsend(0, "x")
    st1, st2, st3 = {}, {}, {}
    for k in turn:
        cc[k].wait_recv()
        ll[k].wait()
        total(acc.at[k], acc.at[k], [cor.at[k]], shape_of("xyz"))
        a = ORDER[k][0]
        st1[k] = [send(pick(acc.at[k], a, peers[a](j)[1], "xyz"), r1[k].at[j - 1], peers[a](j)[0]) for j in (1, 2, 3)]
    vt[1] = vsum(0, vx)
    vy = vsend(1, "y")
    for k in turn:
        a, b, _ = ORDER[k]
        left = [d for d in "xyz" if d != a]
        for c in st1[k]:
            c.wait_recv()
        total(s1[k], pick(acc.at[k], a, here[a], "xyz"), [r1[k].at[j] for j in range(3)], shape_of(left))
        st2[k] = [send(pick(s1[k], b, peers[b](j)[1], left), r2[k].at[j - 1], peers[b](j)[0]) for j in (1, 2, 3)]
    vt[2] = vsum(1, vy)
    vz = vsend(2, "z")
    for k in turn:
        a, b, d = ORDER[k]
        left = [e for e in "xyz" if e != a]
        for c in st2[k]:
            c.wait_recv()
        total(s2[k], pick(s1[k], b, here[b], left), [r2[k].at[j] for j in range(3)], shape_of(d))
        st3[k] = [send(pick(s2[k], d, peers[d](j)[1], d), r3.at[k, j - 1], peers[d](j)[0]) for j in (1, 2, 3)]
    V[...] = vsum(2, vz)
    for k in turn:
        d = ORDER[k][2]
        for c in st3[k]:
            c.wait_recv()
        m = pick(s2[k], d, here[d], d)[...].astype(f32)
        for j in range(3):
            m = m + r3[k, j].astype(f32)
        R[k] = m
    for c in sent:
        c.wait_send()


def reduce_grads(g0, g1, g2, vin, cid):
    vm = pltpu.VMEM
    sh = (4, 2, 2, 2, 4, 24, 768)
    first = [shape_of([d for d in "xyz" if d != o[0]]) for o in ORDER]
    second = [shape_of(o[2]) for o in ORDER]
    scratch = (
        [vm((3, *shape_of("xyz"), 24, 768), bf)] * 2
        + [vm((*s, 24, 768), bf) for s in first]
        + [vm((3, *s, 24, 768), bf) for s in first]
        + [vm((*s, 24, 768), bf) for s in second]
        + [vm((3, *s, 24, 768), bf) for s in second]
        + [vm((3, 3, 24, 768), bf), vm((4, 3) + vin.shape, f32), vm((3,) + vin.shape, f32)]
        + [pltpu.SemaphoreType.DMA((48,)), pltpu.SemaphoreType.DMA((48,)), pltpu.SemaphoreType.DMA((3,))]
    )
    return pl.pallas_call(
        reduce_kernel,
        out_shape=(jax.ShapeDtypeStruct((3, 24, 768), f32), jax.ShapeDtypeStruct(vin.shape, f32)),
        in_specs=[pl.BlockSpec(memory_space=pl.ANY)] * 3 + [pl.BlockSpec(memory_space=vm)],
        out_specs=[pl.BlockSpec(memory_space=vm)] * 2,
        scratch_shapes=scratch,
        compiler_params=pltpu.CompilerParams(collective_id=cid, has_side_effects=True, vmem_limit_bytes=56 << 20),
    )(g0.reshape(sh), g1.reshape(sh), g2.reshape(sh), vin)


SQ = HEAD_DIM ** -0.5
FAR = float(2.0 ** 100)
BLK = 256


def nt(a, b):
    return lax.dot_general(a, b, (((1,), (1,)), ((), ())), preferred_element_type=f32)


def nn(a, b):
    return jnp.dot(a, b, preferred_element_type=f32)


def params(cid=None, mb=48):
    return pltpu.CompilerParams(collective_id=cid, has_side_effects=cid is not None, vmem_limit_bytes=mb << 20)


def qkv_kernel(x, w, b, o):
    r = (nn(x[...], w[0]) + b[0]).astype(bf)
    o[0] = r[:, :384]
    o[1] = jnp.concatenate([r[:, 384:576], r[:, 192:384]], axis=1)


def project(x, w, b):
    return pl.pallas_call(
        qkv_kernel,
        grid=(4,),
        out_shape=jax.ShapeDtypeStruct((8, BLK, 384), bf),
        in_specs=[
            pl.BlockSpec((BLK, 768), lambda t: (0, 0)),
            pl.BlockSpec((1, 768, 768), lambda t: (t, 0, 0)),
            pl.BlockSpec((1, 1, 768), lambda t: (t, 0, 0)),
        ],
        out_specs=pl.BlockSpec((2, BLK, 384), lambda t: (t, 0, 0)),
        compiler_params=params(),
    )(x, w, b)


def swap_kernel(pairs, *refs):
    ins, outs = refs[:pairs], refs[pairs : 2 * pairs]
    ss, rs, ls = refs[2 * pairs :]
    c = lax.axis_index("ctx")
    greet([{"ctx": (c + k) % 8} for k in range(1, 8)])
    sent, own = [], []
    for k in range(1, 8):
        q = (c + k) % 8
        for i in range(pairs):
            src = ins[i].at[q] if ins[i].shape == outs[i].shape else ins[i]
            cp = rcopy(src, outs[i].at[c], ss.at[i, k], rs.at[i, k], {"ctx": q})
            cp.start()
            sent.append(cp)
    for i in range(pairs):
        src = ins[i].at[c] if ins[i].shape == outs[i].shape else ins[i]
        cp = pltpu.make_async_copy(src, outs[i].at[c], ls.at[i])
        cp.start()
        own.append(cp)
    for cp in own + sent:
        cp.wait()


def swap(arrays, outs, cid):
    n = len(arrays)
    sems = [pltpu.SemaphoreType.DMA((n, 8))] * 2 + [pltpu.SemaphoreType.DMA((n,))]
    return pl.pallas_call(
        functools.partial(swap_kernel, n),
        out_shape=tuple(jax.ShapeDtypeStruct(s, a.dtype) for s, a in zip(outs, arrays)),
        in_specs=[pl.BlockSpec(memory_space=pl.ANY)] * n,
        out_specs=[pl.BlockSpec(memory_space=pl.ANY)] * n,
        scratch_shapes=sems,
        compiler_params=params(cid),
    )(*arrays)


def spread(r, aug, qa, ka, h):
    q = r[:, :, h * 192 : h * 192 + 64].reshape(2048, 64)
    k = r[:, :, h * 192 + 64 : h * 192 + 128].reshape(2048, 64)
    qa[h] = jnp.concatenate([q * bf(SQ), aug[:, 64:]], axis=1)
    ka[h] = jnp.concatenate([k, aug[:, :64]], axis=1)


def reach(edge, i, low, high):
    lo, hi = jnp.int32(0), jnp.int32(0)
    for j in range(8):
        lo = lo + (edge[1, j] < edge[0, i]).astype(jnp.int32)
        hi = hi + (edge[0, j] <= edge[1, i]).astype(jnp.int32)
    return lo, hi


def attend_kernel(edge, r, aug, msg, lse, ct, qa, ka, vt):
    par = lax.axis_index("ctx") % 2
    for h in range(2):
        spread(r, aug, qa, ka, h)
        v = r[:, :, h * 192 + 128 : h * 192 + 192].reshape(2048, 64)
        vt[h] = v.astype(f32).T.astype(bf)
    lse[...] = jnp.zeros_like(lse)
    ct[...] = jnp.zeros_like(ct)
    msg[...] = jnp.zeros_like(msg)

    def one(h, i):
        at = pl.ds(pl.multiple_of(i * BLK, BLK), BLK)
        q = qa[h, at]
        lo, hi = reach(edge, i, 0, 8)

        def body(j, carry):
            m, l, acc = carry
            to = pl.ds(pl.multiple_of(j * BLK, BLK), BLK)
            s = nt(ka[h, to], q)
            mj = jnp.maximum(m, jnp.max(s, axis=0, keepdims=True))
            p = jnp.exp(s - mj)
            alpha = jnp.exp(m - mj)
            l = l * alpha + jnp.sum(p, axis=0, keepdims=True)
            acc = acc * alpha + nn(vt[h, :, to], p.astype(bf))
            return mj, l, acc

        m, l, acc = lax.fori_loop(
            lo, hi, body, (jnp.full((1, BLK), -3e38, f32), jnp.zeros((1, BLK), f32), jnp.zeros((64, BLK), f32))
        )
        c = acc / l
        lse[h * 8 + i] = jnp.broadcast_to(m + jnp.log(l), (8, BLK))
        ct[h, :, at] = c
        msg[i, :, h * 64 : h * 64 + 64] = c.T.astype(bf)

    @pl.loop(0, 8)
    def _(i):
        one(0, i)

    @pl.loop(0, 4)
    def _(i):
        one(1, 2 * i + par)


def attend(edge, r, aug):
    vm = pltpu.VMEM
    return pl.pallas_call(
        attend_kernel,
        out_shape=(
            jax.ShapeDtypeStruct((8, BLK, 128), bf),
            jax.ShapeDtypeStruct((16, 8, BLK), f32),
            jax.ShapeDtypeStruct((2, 64, 2048), f32),
        ),
        in_specs=[pl.BlockSpec(memory_space=pltpu.SMEM)] + [pl.BlockSpec(memory_space=vm)] * 2,
        out_specs=[pl.BlockSpec(memory_space=vm)] * 3,
        scratch_shapes=[vm((2, 2048, 128), bf), vm((2, 2048, 128), bf), vm((2, 64, 2048), bf)],
        compiler_params=params(),
    )(edge, r, aug)


def unattend_kernel(edge, r, aug, dc, lse, ct, out, qa, ka, kt, delta, dqt, dk, dv):
    par = lax.axis_index("ctx") % 2
    for h in range(2):
        spread(r, aug, qa, ka, h)
        k = r[:, :, h * 192 + 64 : h * 192 + 128].reshape(2048, 64)
        kt[h] = k.astype(f32).T.astype(bf)
        g = dc[:, :, h * 64 : h * 64 + 64].reshape(2048, 64).astype(f32).T
        d = jnp.sum(g * ct[h], axis=0, keepdims=True)
        for i in range(8):
            delta[h * 8 + i] = jnp.broadcast_to(d[:, i * BLK : i * BLK + BLK], (8, BLK))
    dqt[...] = jnp.zeros_like(dqt)

    def one(h, j):
        to = pl.ds(pl.multiple_of(j * BLK, BLK), BLK)
        lo, hi = reach(edge, j, 0, 8)
        if h == 1:
            lo = (lo - par + 1) // 2
            hi = (hi - par + 1) // 2
        dk[...] = jnp.zeros_like(dk)
        dv[...] = jnp.zeros_like(dv)
        kj = ka[h, to]
        vj = r[j, :, h * 192 + 128 : h * 192 + 192]
        ktj = kt[h, :, to]

        def body(n, _):
            i = n if h == 0 else 2 * n + par
            at = pl.ds(pl.multiple_of(i * BLK, BLK), BLK)
            q = qa[h, at]
            g = dc[i, :, h * 64 : h * 64 + 64]
            p = jnp.exp(nt(kj, q) - lse[h * 8 + i, :1])
            dp = nt(vj, g)
            ds = (p * (dp - delta[h * 8 + i, :1])).astype(bf)
            dv[...] += nn(p.astype(bf), g)
            dk[...] += nn(ds, q)
            dqt[h, :, at] += nn(ktj, ds)
            return 0

        lax.fori_loop(lo, hi, body, 0)
        out[j, :, h * 192 + 64 : h * 192 + 128] = dk[:, :64].astype(bf)
        out[j, :, h * 192 + 128 : h * 192 + 192] = dv[...].astype(bf)

    @pl.loop(0, 8)
    def _(j):
        one(0, j)
        one(1, j)

    for h in range(2):
        dq = (dqt[h] * SQ).T.astype(bf)
        for i in range(8):
            out[i, :, h * 192 : h * 192 + 64] = dq[i * BLK : i * BLK + BLK]


def unattend(edge, r, aug, dc, lse, ct):
    vm = pltpu.VMEM
    return pl.pallas_call(
        unattend_kernel,
        out_shape=jax.ShapeDtypeStruct((8, BLK, 384), bf),
        in_specs=[pl.BlockSpec(memory_space=pltpu.SMEM)] + [pl.BlockSpec(memory_space=vm)] * 5,
        out_specs=pl.BlockSpec(memory_space=vm),
        scratch_shapes=[
            vm((2, 2048, 128), bf),
            vm((2, 2048, 128), bf),
            vm((2, 64, 2048), bf),
            vm((16, 8, BLK), f32),
            vm((2, 64, 2048), f32),
            vm((BLK, 128), f32),
            vm((BLK, 64), f32),
        ],
        compiler_params=params(),
    )(edge, r, aug, dc, lse, ct)


def norm_of(v):
    d = v - jnp.mean(v, axis=-1, keepdims=True)
    s = lax.rsqrt(jnp.mean(d * d, axis=-1, keepdims=True) + NORM_EPS)
    return d * s, s


def norm_back(g, xhat, s, gain):
    e = g * gain
    return s * (e - jnp.mean(e, axis=-1, keepdims=True) - xhat * jnp.mean(e * xhat, axis=-1, keepdims=True))


def down_sum(v):
    return jnp.sum(v, axis=0, keepdims=True)


def rows_kernel(w, cm, x, cot, pv, lo, dh1, gup, gdn, go, dcm, sums, wv, wo, zs, cdf, act, gs, ls, os):
    loads = []
    for k in range(3):
        for t in range(4):
            cp = pltpu.make_async_copy(w.at[k, t], wv.at[k * 4 + t], ls.at[k * 4 + t])
            cp.start()
            loads.append(cp)
    attn = jnp.zeros((BLK, 768), f32)
    for t in range(4):
        loads[t].wait()
        o = wv[t, :, 576:768]
        wo[2 * t] = o[:, :128]
        wo[2 * t + 1] = jnp.concatenate([o[:, 128:], o[:, 64:128]], axis=1)
        attn = attn + nt(cm[2 * t], wo[2 * t]) + nt(cm[2 * t + 1], wo[2 * t + 1])
    h1 = x[...].astype(f32) + attn + pv[0:1]
    xh1, s1 = norm_of(h1)
    y1 = xh1 * pv[2:3] + pv[3:4]
    y1b = y1.astype(bf)
    ffn = jnp.zeros((BLK, 768), f32)
    for t in range(4):
        loads[4 + t].wait()
        z = nn(y1b, wv[4 + t]) + pv[8 + t : 9 + t]
        c = 0.5 * (1.0 + lax.erf(z * (2.0 ** -0.5)))
        zs[t] = z
        cdf[t] = c
        a = (z * c).astype(bf)
        act[t] = a
        loads[8 + t].wait()
        ffn = ffn + nt(a, wv[8 + t])
    xh2, s2 = norm_of(y1 + ffn + pv[1:2])
    lo[...] = (xh2 * pv[4:5] + pv[5:6]).astype(bf)
    g = cot[...].astype(f32)
    sums[4:5] = down_sum(g * xh2)
    sums[5:6] = down_sum(g)
    dh2 = norm_back(g, xh2, s2, pv[4:5])
    sums[1:2] = down_sum(dh2)
    dh2b = dh2.astype(bf)
    dh2t = dh2.T.astype(bf)
    y1t = y1.T.astype(bf)
    dy1 = dh2
    outs = []
    for t in range(4):
        da = nn(dh2b, wv[8 + t]).astype(bf).astype(f32)
        z = zs[t]
        dz = da * (cdf[t] + z * (jnp.exp(-0.5 * z * z) * ((2.0 * math.pi) ** -0.5)))
        sums[8 + t : 9 + t] = down_sum(dz)
        dzb = dz.astype(bf)
        if t >= 1:
            outs[2 * t - 2].wait()
            outs[2 * t - 1].wait()
        gs[0] = nn(dh2t, act[t]).astype(bf)
        cp = pltpu.make_async_copy(gs.at[0], gdn.at[t], os.at[0])
        cp.start()
        outs.append(cp)
        gs[1] = nn(y1t, dzb).astype(bf)
        cp = pltpu.make_async_copy(gs.at[1], gup.at[t], os.at[1])
        cp.start()
        outs.append(cp)
        dy1 = dy1 + nt(dzb, wv[4 + t])
    sums[2:3] = down_sum(dy1 * xh1)
    sums[3:4] = down_sum(dy1)
    d1 = norm_back(dy1, xh1, s1, pv[2:3])
    dh1[...] = d1
    sums[0:1] = down_sum(d1)
    d1b = d1.astype(bf)
    d1t = d1.T.astype(bf)
    for t in range(4):
        ga = nn(d1t, cm[2 * t])
        gb = nn(d1t, cm[2 * t + 1])
        go[t] = jnp.concatenate([ga[:, :64], ga[:, 64:] + gb[:, 64:], gb[:, :64]], axis=1).astype(bf)
        dcm[2 * t] = nn(d1b, wo[2 * t]).astype(bf)
        dcm[2 * t + 1] = nn(d1b, wo[2 * t + 1]).astype(bf)
    outs[6].wait()
    outs[7].wait()


def rows(w, cm, x, cot, pv):
    vm = pltpu.VMEM
    sd = jax.ShapeDtypeStruct
    anywhere = pl.BlockSpec(memory_space=pl.ANY)
    here = pl.BlockSpec(memory_space=vm)
    return pl.pallas_call(
        rows_kernel,
        out_shape=(
            sd((BLK, 768), bf),
            sd((BLK, 768), f32),
            sd((4, 768, 768), bf),
            sd((4, 768, 768), bf),
            sd((4, 768, 192), bf),
            sd((8, BLK, 128), bf),
            sd((16, 768), f32),
        ),
        in_specs=[anywhere] + [here] * 4,
        out_specs=[here, here, anywhere, anywhere, here, here, here],
        scratch_shapes=[
            vm((12, 768, 768), bf),
            vm((8, 768, 128), bf),
            vm((4, BLK, 768), f32),
            vm((4, BLK, 768), f32),
            vm((4, BLK, 768), bf),
            vm((2, 768, 768), bf),
            pltpu.SemaphoreType.DMA((12,)),
            pltpu.SemaphoreType.DMA((2,)),
        ],
        compiler_params=params(mb=56),
    )(w, cm, x, cot, pv)


def last_kernel(d, x, dh1, w, go, g, ig, pb, xt, acc):
    t = pl.program_id(0)

    @pl.when(t == 0)
    def _():
        xt[...] = x[...].astype(f32).T.astype(bf)
        acc[...] = dh1[...]

    a, b = d[0].astype(f32), d[1].astype(f32)
    pre = jnp.concatenate([a[:, :192], a[:, 192:] + b[:, 192:], b[:, :192]], axis=1)
    pb[0] = jnp.broadcast_to(down_sum(pre), (8, 576))
    pre = pre.astype(bf)
    g[0] = jnp.concatenate([nn(xt[...], pre).astype(bf), go[0]], axis=1)
    acc[...] += nt(pre, w[0, :, :576])
    ig[...] = acc[...].astype(bf)


def last(d, x, dh1, w, go):
    sd = jax.ShapeDtypeStruct
    return pl.pallas_call(
        last_kernel,
        grid=(4,),
        out_shape=(sd((4, 768, 768), bf), sd((BLK, 768), bf), sd((4, 8, 576), f32)),
        in_specs=[
            pl.BlockSpec((2, BLK, 384), lambda t: (t, 0, 0)),
            pl.BlockSpec((BLK, 768), lambda t: (0, 0)),
            pl.BlockSpec((BLK, 768), lambda t: (0, 0)),
            pl.BlockSpec((1, 768, 768), lambda t: (t, 0, 0)),
            pl.BlockSpec((1, 768, 192), lambda t: (t, 0, 0)),
        ],
        out_specs=[
            pl.BlockSpec((1, 768, 768), lambda t: (t, 0, 0)),
            pl.BlockSpec((BLK, 768), lambda t: (0, 0)),
            pl.BlockSpec((1, 8, 576), lambda t: (t, 0, 0)),
        ],
        scratch_shapes=[pltpu.VMEM((768, BLK), bf), pltpu.VMEM((BLK, 768), f32)],
        compiler_params=params(),
    )(d, x, dh1, w, go)


def share_kernel(a, o, ss, rs, ls):
    x = lax.axis_index("tp")
    greet([{"tp": (x + k) % 4} for k in (1, 2, 3)])
    sent = []
    for k in (1, 2, 3):
        cp = rcopy(a, o.at[x], ss.at[k], rs.at[k], {"tp": (x + k) % 4})
        cp.start()
        sent.append(cp)
    own = pltpu.make_async_copy(a, o.at[x], ls)
    own.start()
    own.wait()
    for cp in sent:
        cp.wait()


def share(a, cid):
    return pl.pallas_call(
        share_kernel,
        out_shape=jax.ShapeDtypeStruct((4, *a.shape), a.dtype),
        in_specs=[pl.BlockSpec(memory_space=pl.ANY)],
        out_specs=pl.BlockSpec(memory_space=pl.ANY),
        scratch_shapes=[pltpu.SemaphoreType.DMA((4,)), pltpu.SemaphoreType.DMA((4,)), pltpu.SemaphoreType.DMA],
        compiler_params=params(cid),
    )(a)


def shards(
    layer_input,
    segment_ids,
    proj_weight,
    proj_bias,
    out_weight,
    out_bias,
    first_gain,
    first_shift,
    up_weight,
    up_bias,
    down_weight,
    down_bias,
    second_gain,
    second_shift,
    cotangent,
):
    tp = lax.axis_index("tp")
    turn = np.array([0, 2, 1])
    qkv = proj_weight.reshape(3, 192, 3, 64).transpose(1, 2, 0, 3)[:, turn].reshape(192, 576)
    out_turned = out_weight.T.reshape(192, 3, 64)[:, turn].reshape(192, 192)
    pk = jnp.stack([jnp.concatenate([qkv, out_turned], axis=1), up_weight, down_weight.T])
    pb = proj_bias.reshape(2, 3, 64)[:, turn]
    pb = jnp.stack([pb[0], jnp.zeros_like(pb[0]), pb[1]], axis=1).reshape(576)
    vec = jnp.stack(
        [
            up_bias,
            jnp.pad(pb, (0, 192)),
            jnp.concatenate([out_bias, down_bias, first_gain, first_shift]),
            jnp.pad(jnp.concatenate([second_gain, second_shift]), (0, 384)),
        ]
    )
    vec = jnp.pad(vec, ((0, 4), (0, 0)))
    w, v = gather_weights(pk, vec, 1)
    w = w.reshape(3, 4, 768, 768)
    v = v.astype(f32)
    four = v[0, :, :, 2].reshape(4, 4, 192).transpose(1, 0, 2).reshape(4, 768)
    two = v[0, :, :, 3, :384].reshape(4, 2, 192).transpose(1, 0, 2).reshape(2, 768)
    pv = jnp.concatenate([four, two, jnp.zeros((2, 768), f32), v[:, 0, 0, 0], jnp.zeros((4, 768), f32)])
    x = lax.dynamic_index_in_dim(layer_input, tp, 0, keepdims=False)
    cot = lax.dynamic_index_in_dim(cotangent, tp, 0, keepdims=False)
    seg = lax.dynamic_index_in_dim(segment_ids, tp, 0, keepdims=False)
    seg = jnp.pad(seg.reshape(2, 128), ((0, 6), (0, 0)))
    m = project(x, w[0], v[:, 0, 0, 1][:, None])
    r, segs = swap((m, seg), ((8, BLK, 384), (8, 8, 128)), 2)
    segs = segs[:, :2].reshape(8, BLK)
    edge = jnp.stack([segs[:, 0], segs[:, -1]])
    col = segs.reshape(2048, 1)
    lane = lax.broadcasted_iota(jnp.int32, (1, 64), 1)
    same = col == lane
    aug = jnp.concatenate(
        [jnp.where(same | (lane > 3), 0.0, 1.0).astype(bf), jnp.where(same, -FAR, 0.0).astype(bf)], axis=1
    )
    cmsg, lse, ct = attend(edge, r, aug)
    (cm,) = swap((cmsg,), ((8, BLK, 128),), 3)
    lo, dh1, gup, gdn, go, dcm, sums = rows(w, cm, x, cot, pv)
    layer_output = lax.all_gather(lo, "tp", axis=0)
    (dc,) = swap((dcm,), ((8, BLK, 128),), 4)
    dmsg = unattend(edge, r, aug, dc, lse, ct)
    (d,) = swap((dmsg,), ((8, BLK, 384),), 5)
    gpo, ig, pbs = last(d, x, dh1, w[0], go)
    input_grad = share(ig, 6).astype(f32)
    vin = jnp.concatenate([sums[:6].reshape(36, 128), sums[8:12].reshape(24, 128), pbs[:, 0].reshape(18, 128)])
    vin = jnp.pad(vin, ((0, 2), (0, 0)))
    red, vs = reduce_grads(gpo, gup, gdn, vin, 7)
    g0 = red[0]
    gq = g0[:, :576].reshape(24, 3, 3, 64)[:, turn].transpose(2, 0, 1, 3).reshape(3, 24, 192)
    gout = g0[:, 576:].reshape(24, 3, 64)[:, turn].reshape(24, 192).T
    fc = lax.axis_index(("fsdp", "ctx"))
    six = lax.dynamic_index_in_dim(vs[:36].reshape(6, 32, 24), fc, 1, keepdims=False)
    upb = lax.dynamic_index_in_dim(vs[36:60].reshape(4, 768), tp, 0, keepdims=False)
    pbq = lax.dynamic_index_in_dim(vs[60:78].reshape(4, 3, 3, 64), tp, 0, keepdims=False)
    pbg = pbq[turn][:, np.array([0, 2])].transpose(1, 0, 2).reshape(2, 192)
    return (
        layer_output,
        input_grad,
        gq,
        pbg,
        gout,
        six[0],
        six[2],
        six[3],
        red[1],
        upb,
        red[2].T,
        six[1],
        six[4],
        six[5],
    )


def solution(mesh):
    placed = (
        P("fsdp", "ctx", None),
        P("fsdp", "ctx"),
        P(None, "fsdp", "tp"),
        P(None, "tp"),
        P("tp", "fsdp"),
        P("fsdp"),
        P("fsdp"),
        P("fsdp"),
        P("fsdp", "tp"),
        P("tp"),
        P("tp", "fsdp"),
        P("fsdp"),
        P("fsdp"),
        P("fsdp"),
        P("fsdp", "ctx", None),
    )
    return jax.shard_map(
        shards,
        mesh=mesh,
        in_specs=placed,
        out_specs=(
            P("fsdp", "ctx", None),
            P("fsdp", "ctx", None),
            P(None, ("fsdp", "ctx"), "tp"),
            P(None, "tp"),
            P("tp", ("fsdp", "ctx")),
            P(("fsdp", "ctx")),
            P(("fsdp", "ctx")),
            P(("fsdp", "ctx")),
            P(("fsdp", "ctx"), "tp"),
            P("tp"),
            P("tp", ("fsdp", "ctx")),
            P(("fsdp", "ctx")),
            P(("fsdp", "ctx")),
            P(("fsdp", "ctx")),
        ),
        check_vma=False,
    )
```

```python
import functools
import math

import jax
import jax.numpy as jnp
from jax import lax
from jax.experimental import pallas as pl
from jax.experimental.pallas import tpu as pltpu
from jax.sharding import PartitionSpec as P

HEAD_DIM = 64
NORM_EPS = 1e-12

MESH = pl.DeviceIdType.MESH
bf=jnp.bfloat16; f32=jnp.float32

class Place:
    def __init__(self):
        self.x=lax.axis_index("tp"); f=lax.axis_index("fsdp"); c=lax.axis_index("ctx")
        self.yl=f//2; self.core=f%2; self.yh=c//4; self.z=c%4
        self.y=self.yh*2+self.yl
    def px(self,k):
        q=(self.x+k)%4
        return {"tp":q}, q
    def pz(self,k):
        q=(self.z+k)%4
        return {"ctx":self.yh*4+q}, q
    def py(self,k):
        q=(self.y+k)%4
        return {"fsdp":(q%2)*2+self.core,"ctx":(q//2)*4+self.z}, (q%2,q//2)
    def sib(self):
        return {"fsdp":self.yl*2+1-self.core}

def greet(devs):
    bar=pltpu.get_barrier_semaphore()
    for d in devs: pl.semaphore_signal(bar,inc=1,device_id=d,device_id_type=MESH)
    pl.semaphore_wait(bar,len(devs))

def rcopy(src,dst,ss,rs,dev):
    return pltpu.make_async_remote_copy(src_ref=src,dst_ref=dst,send_sem=ss,recv_sem=rs,device_id=dev,device_id_type=MESH)


DIMS = {"x": (4,), "y": (2, 2), "z": (4,)}
ORDER = ("xyz", "yzx", "zxy")


def shape_of(axes):
    return sum([DIMS[d] for d in "xyz" if d in axes], ())


def split_index(i, shape):
    out = []
    for s in reversed(shape):
        out.insert(0, i % s)
        i = i // s
    return tuple(out)


def pick(ref, axis, q, left):
    at = []
    for d in "xyz":
        if d in left:
            at += list(q if d == "y" else (q,)) if d == axis else [slice(None)] * len(DIMS[d])
    return ref.at[tuple(at)]


def total(dst, first, others, shape):
    count = math.prod(shape)

    @pl.loop(0, count)
    def _(i):
        at = split_index(i, shape)
        a = first[at].astype(f32)
        for o in others:
            a = a + o[at].astype(f32)
        dst[at] = a.astype(dst.dtype)


SQ = HEAD_DIM ** -0.5
FAR = float(2.0 ** 100)
BLK = 256


def nt(a, b):
    return lax.dot_general(a, b, (((1,), (1,)), ((), ())), preferred_element_type=f32)


def nn(a, b):
    return jnp.dot(a, b, preferred_element_type=f32)


def params(cid=None, mb=48):
    return pltpu.CompilerParams(collective_id=cid, has_side_effects=cid is not None, vmem_limit_bytes=mb << 20)


class Sender:
    def __init__(self, ss, rs):
        self.ss, self.rs, self.all = ss, rs, []

    def __call__(self, src, dst, dev):
        i = len(self.all)
        c = rcopy(src, dst, self.ss.at[i], self.rs.at[i], dev)
        c.start()
        self.all.append(c)
        return c


AXES = (1, 2, 3)


class Spread:
    def __init__(self, p, send, own, to, rx, ry, rz):
        self.p, self.send, self.own, self.to = p, send, own, to
        self.rx, self.ry, self.rz = rx, ry, rz
        self.half = ry[0] + pl.multiple_of(p.yh * (ry[1] // 2), 8), ry[1] // 2
        self.quarter = rz[0] + pl.multiple_of(p.z * (rz[1] // 4), 8), rz[1] // 4

    def rows(self, what):
        a, n = what
        return pl.ds(a if isinstance(a, int) else pl.multiple_of(a, 8), n)

    def out(self, t, yl, what):
        return self.to.at[t, yl, self.p.core, self.rows(what)]

    def pass_on(self, t, yl, what, devs):
        return [self.send(self.out(t, yl, what), self.out(t, yl, what), d) for d in devs]

    def start(self):
        p = self.p
        nb = {"fsdp": (1 - p.yl) * 2 + p.core}
        mine = lambda what: self.own.at[self.rows(what)]
        push = lambda what, devs: [self.send(mine(what), self.out(p.x, p.yl, what), d) for d in devs]
        xs = [p.px(k)[0] for k in AXES]
        self.nz = push(self.quarter, [nb])[0] if self.rz[1] else None
        self.nx = push(self.rx, [nb])[0]
        self.xy = push(self.half, xs)
        self.xz = push(self.quarter, xs)
        self.yy = push(self.half, [p.py(k)[0] for k in (1, 3)])

    def second(self):
        p = self.p
        xs = [p.px(k)[0] for k in AXES]
        ys = [p.py(k)[0] for k in AXES]
        zs = [p.pz(k)[0] for k in AXES]
        self.nz.wait_recv()
        self.xz2 = self.pass_on(p.x, 1 - p.yl, self.quarter, xs)
        self.zz = self.pass_on(p.x, 1 - p.yl, self.quarter, zs)
        self.xx = [self.send(self.own.at[self.rows(self.rx)], self.out(p.x, p.yl, self.rx), d) for d in xs]
        self.nx.wait_recv()
        self.xx2 = self.pass_on(p.x, 1 - p.yl, self.rx, xs)
        for k in AXES:
            t = (p.x + 4 - k) % 4
            self.xy[k - 1].wait_recv()
            self.yy += self.pass_on(t, p.yl, self.half, ys)
            self.xz[k - 1].wait_recv()
            self.zz += self.pass_on(t, p.yl, self.quarter, zs)
        for k in AXES:
            t = (p.x + 4 - k) % 4
            self.xz2[k - 1].wait_recv()
            self.zz += self.pass_on(t, 1 - p.yl, self.quarter, zs)

    def finish(self):
        for c in self.yy + self.zz + self.xx + self.xx2:
            c.wait_recv()


def front_kernel(p0, p1, p2, vec, xs, seg, W, V, R, S, po, m, x, ss, rs, ls):
    p = Place()
    c = lax.axis_index("ctx")
    core, sib = p.core, p.sib()
    ctx = [{"ctx": (c + k) % 8} for k in range(1, 8)]
    greet([p.px(k)[0] for k in AXES] + [p.py(k)[0] for k in (1, 3)] + ctx + [sib])
    send = Sender(ss, rs)
    own = pltpu.make_async_copy(p0, po.at[p.x, p.yl, core], ls.at[0])
    mine = pltpu.make_async_copy(vec, V.at[p.x, p.yl, core], ls.at[1])
    rows = pltpu.make_async_copy(xs.at[p.x], x, ls.at[2])
    up = pltpu.make_async_copy(p1, W.at[1, p.x, p.yl, core], ls.at[4])
    down = pltpu.make_async_copy(p2, W.at[2, p.x, p.yl, core], ls.at[5])
    for cp in (own, mine, rows, up, down):
        cp.start()
    nb = {"fsdp": (1 - p.yl) * 2 + core}
    first = Spread(p, send, p0, po, (0, 64), (64, 64), (128, 64))
    first.start()
    vn = send(vec, V.at[p.x, p.yl, core], nb)
    vx = [send(vec, V.at[p.x, p.yl, core], p.px(k)[0]) for k in AXES]
    sg = [send(seg, S.at[c], d) for d in ctx]
    sgo = pltpu.make_async_copy(seg, S.at[c], ls.at[3])
    sgo.start()
    d0 = [send(p0, po.at[p.x, p.yl, core], sib)]
    dv = [send(vec, V.at[p.x, p.yl, core], sib)]
    first.second()
    vn.wait_recv()
    vx += [send(V.at[p.x, 1 - p.yl, core], V.at[p.x, 1 - p.yl, core], p.px(k)[0]) for k in AXES]
    bulk = [
        Spread(p, send, p1, W.at[1], (0, 96), (96, 64), (160, 32)),
        Spread(p, send, p2, W.at[2], (0, 64), (64, 64), (128, 64)),
    ]
    for b in bulk:
        b.start()
    first.finish()
    for cp in vx:
        cp.wait_recv()
    own.wait()
    mine.wait()
    d0.append(send(po.at[p.x, 1 - p.yl, core], po.at[p.x, 1 - p.yl, core], sib))
    dv.append(send(V.at[p.x, 1 - p.yl, core], V.at[p.x, 1 - p.yl, core], sib))
    for k in AXES:
        t = (p.x + k) % 4
        d0.append(send(po.at[t, :, core], po.at[t, :, core], sib))
        dv.append(send(V.at[t, :, core], V.at[t, :, core], sib))
    for b in bulk:
        b.second()
    for cp in d0 + dv:
        cp.wait_recv()
    rows.wait()
    back = pltpu.make_async_copy(po, W.at[0], ls.at[0])
    back.start()

    @pl.loop(0, 4)
    def _(t):
        b = V[t, 0, 0, 1:2].astype(f32)
        r = (nn(x[...], po[t].reshape(768, 768)) + b).astype(bf)
        m[2 * t] = r[:, :384]
        m[2 * t + 1] = jnp.concatenate([r[:, 384:576], r[:, 192:384]], axis=1)

    sw = [send(m.at[(c + k) % 8], R.at[c], {"ctx": (c + k) % 8}) for k in range(1, 8)]
    swo = pltpu.make_async_copy(m.at[c], R.at[c], ls.at[2])
    swo.start()
    for b in bulk:
        b.finish()
    up.wait()
    down.wait()
    dw = []
    for k in range(4):
        t = (p.x + k) % 4
        dw.append(send(W.at[pl.ds(1, 2), t, :, core], W.at[pl.ds(1, 2), t, :, core], sib))
    for cp in sg + sw + dw:
        cp.wait_recv()
    for cp in send.all:
        cp.wait_send()
    for cp in (back, swo, sgo):
        cp.wait()


def front(p0, p1, p2, vec, xs, seg, cid):
    sd = jax.ShapeDtypeStruct
    vm = pltpu.VMEM
    anywhere, here = pl.BlockSpec(memory_space=pl.ANY), pl.BlockSpec(memory_space=vm)
    count = 192
    return pl.pallas_call(
        front_kernel,
        out_shape=(
            sd((3, 4, 2, 2, 192, 768), bf),
            sd((4, 2, 2, 8, 768), bf),
            sd((8, BLK, 384), bf),
            sd((8, 2, 128), jnp.int32),
        ),
        in_specs=[anywhere] * 6,
        out_specs=[anywhere, here, anywhere, anywhere],
        scratch_shapes=[
            vm((4, 2, 2, 192, 768), bf),
            vm((8, BLK, 384), bf),
            vm((BLK, 768), bf),
            pltpu.SemaphoreType.DMA((count,)),
            pltpu.SemaphoreType.DMA((count,)),
            pltpu.SemaphoreType.DMA((6,)),
        ],
        compiler_params=params(cid),
    )(p0, p1, p2, vec, xs, seg)


LONG = 2048 + BLK
SAFE = 120.0 / SQ
FWD = 8
BWD = 4


def blocks(edge, lst, par, unit):
    n = jnp.int32(0)
    for h in range(2):
        for i in range(8 if h == 0 else 4):
            qi = i if h == 0 else 2 * i + par
            lo, hi = jnp.int32(0), jnp.int32(0)
            for j in range(8):
                lo = lo + (edge[j, 1, 127] < edge[qi, 0, 0]).astype(jnp.int32)
                hi = hi + (edge[j, 0, 0] <= edge[qi, 1, 127]).astype(jnp.int32)

            def put(j, n):
                lst[n] = (h * 8 + qi) * 16 + j
                return n + 1

            n = lax.fori_loop(lo, hi, put, n)
    for k in range(unit - 1):
        lst[n + k] = 8
    return (n + unit - 1) // unit


def triple(code):
    j = code % 16
    i = (code // 16) % 8
    return code // 128, pl.ds(pl.multiple_of(i * BLK, BLK), BLK), pl.ds(pl.multiple_of(j * BLK, BLK), BLK), i


def lanes():
    return lax.broadcasted_iota(jnp.int32, (1, 128), 1)


def three(v, at, lane):
    a = v.astype(bf).astype(f32)
    b = (v - a).astype(bf).astype(f32)
    c = v - a - b
    return jnp.where(lane == at, a, jnp.where(lane == at + 1, b, jnp.where(lane == at + 2, c, 0.0))).astype(bf)


def flat(r, k):
    return r[:, :, 128 * k : 128 * k + 128].reshape(2048, 128)


def turned(v):
    return v.astype(f32).T.astype(bf)


def one_lane(h, lane):
    return lane == (72 if h == 0 else 8)


def doc_rows(docs):
    seg = jnp.concatenate([docs[j, i : i + 1] for j in range(8) for i in range(2)] + [jnp.full((1, BLK), -1)], axis=1)
    row = lax.broadcasted_iota(jnp.int32, (64, 1), 0)
    return seg, jnp.where(((row < 4) & (row != seg)) | ((row >= 8) & (row < 11)), 1.0, 0.0)


def attend_kernel(edge, docs, r, msg, acc, qa, kt, va, top, lst):
    par = lax.axis_index("ctx") % 2
    lane = lanes()
    count = blocks(edge, lst, par, FWD)
    seg, augk = doc_rows(docs)
    row = lax.broadcasted_iota(jnp.int32, (128, 1), 0) - 64
    augq = jnp.where(row == seg[:, :2048], -FAR, 0.0).T.astype(bf)
    augk = augk.astype(bf)
    vv = flat(r, 1)
    safe = jnp.bool_(True)
    for h in range(2):
        qk = flat(r, 2 * h)
        qa[h] = jnp.where(lane < 64, qk * bf(SQ), augq)
        kt[h, :64, :2048] = turned(qk)[64:]
        kt[h, :64, 2048:] = jnp.zeros((64, BLK), bf)
        kt[h, 64:] = augk
        va[h, :2048] = jnp.where((lane < 64) if h == 0 else (lane >= 64), vv, one_lane(h, lane).astype(bf))
        va[h, 2048:] = jnp.zeros((BLK, 128), bf)
        f = qk.astype(f32)
        safe = safe & (jnp.max(jnp.sum(f * f, axis=1, keepdims=True)) < SAFE)
    acc[...] = jnp.zeros_like(acc)

    @pl.when(jnp.logical_not(safe))
    def _():
        top[...] = jnp.full_like(top, -3e38)

        @pl.loop(0, count * FWD)
        def _(n):
            h, at, to, i = triple(lst[n])
            s = jnp.max(nn(qa[h, at], kt[h, :, to]), axis=1, keepdims=True)
            top[h, at] = jnp.maximum(top[h, at], s)

        for h in range(2):
            for i in range(8):
                at = slice(i * BLK, i * BLK + BLK)
                qa[h, at] = qa[h, at] + three(-top[h, at, :1], 72, lane)

    @pl.loop(0, count)
    def _(n):
        got = []
        for u in range(FWD):
            h, at, to, _ = triple(lst[n * FWD + u])
            p = jnp.exp(nn(qa[h, at], kt[h, :, to])).astype(bf)
            got.append((h, at, nn(p, va[h, to])))
        for h, at, o in got:
            acc[h, at] += o

    for i in range(8):
        at = slice(i * BLK, i * BLK + BLK)
        a = acc[0, at] * (1.0 / acc[0, at, 72:73])
        b = acc[1, at] * (1.0 / acc[1, at, 8:9])
        b = jnp.where(par == i % 2, b, 0.0)
        msg[i] = jnp.where(lane < 64, a, b).astype(bf)


def attend(docs, r):
    vm = pltpu.VMEM
    sd = jax.ShapeDtypeStruct
    return pl.pallas_call(
        attend_kernel,
        out_shape=(sd((8, BLK, 128), bf), sd((2, 2048, 128), f32), sd((2, 2048, 128), bf)),
        in_specs=[pl.BlockSpec(memory_space=pltpu.SMEM)] + [pl.BlockSpec(memory_space=vm)] * 2,
        out_specs=[pl.BlockSpec(memory_space=vm)] * 3,
        scratch_shapes=[
            vm((2, 128, LONG), bf),
            vm((2, LONG, 128), bf),
            vm((2, 2048, 128), f32),
            pltpu.SMEM((128,), jnp.int32),
        ],
        compiler_params=params(),
    )(docs, docs, r)


def unattend_kernel(edge, docs, r, dc, acc, qa, out, ka, va, kt, ga, gz, qz, dkv, dqt, lst):
    par = lax.axis_index("ctx") % 2
    lane = lanes()
    count = blocks(edge, lst, par, BWD)
    vv, gg = flat(r, 1), flat(dc, 0)
    tops = doc_rows(docs)[1].T.astype(bf)
    for h in range(2):
        qk = flat(r, 2 * h)
        low = (lane < 64) if h == 0 else (lane >= 64)
        at = 72 if h == 0 else 8
        kt[h, :, :2048] = turned(qk)[64:]
        kt[h, :, 2048:] = jnp.zeros((64, BLK), bf)
        ka[h, :2048] = jnp.concatenate([qk[:, 64:], tops[:2048]], axis=1)
        ka[h, 2048:] = jnp.concatenate([jnp.zeros((BLK, 64), bf), tops[2048:]], axis=1)
        ones = ((lane >= at) & (lane < at + 3)).astype(bf)
        va[h, :2048] = jnp.where(low, vv, ones)
        va[h, 2048:] = jnp.zeros((BLK, 128), bf)
        inv = 1.0 / acc[h, :, at : at + 1]
        g = jnp.where(low, gg.astype(f32), 0.0)
        g = (g * inv).astype(bf)
        delta = jnp.sum(g.astype(f32) * acc[h], axis=1, keepdims=True) * inv
        gz[h] = g
        ga[h] = g + three(-delta, at, lane)
        q = jnp.where(lane < 64, qa[h], bf(0))
        qz[h] = pltpu.roll(q.astype(f32), 64, 1).astype(bf) if h == 0 else q
    dqt[...] = jnp.zeros_like(dqt)
    dkv[...] = jnp.zeros_like(dkv)

    @pl.loop(0, count)
    def _(n):
        got = []
        for u in range(BWD):
            h, at, to, _ = triple(lst[n * BWD + u])
            p = jnp.exp(nt(ka[h, to], qa[h, at]))
            ds = (p * nt(va[h, to], ga[h, at])).astype(bf)
            kv = nn(p.astype(bf), gz[h, at]) + nn(ds, qz[h, at])
            got.append((h, at, to, kv, nn(kt[h, :, to], ds)))
        for h, at, to, kv, dq in got:
            dkv[h, to] += kv
            dqt[h, :, at] += dq

    for i in range(8):
        a = slice(i * BLK, i * BLK + BLK)
        q0, q1 = [jnp.concatenate([(dqt[h, :, a] * SQ).T] * 2, axis=1) for h in range(2)]
        q1 = jnp.where(par == i % 2, q1, 0.0)
        kv0, kv1 = dkv[0, a], dkv[1, a]
        out[i, :, :128] = jnp.where(lane < 64, q0, kv0).astype(bf)
        out[i, :, 128:256] = jnp.where(lane < 64, kv0, kv1).astype(bf)
        out[i, :, 256:] = jnp.where(lane < 64, q1, pltpu.roll(kv1, 64, 1)).astype(bf)


def unattend(docs, r, dc, acc, qa):
    vm = pltpu.VMEM
    return pl.pallas_call(
        unattend_kernel,
        out_shape=jax.ShapeDtypeStruct((8, BLK, 384), bf),
        in_specs=[pl.BlockSpec(memory_space=pltpu.SMEM)] + [pl.BlockSpec(memory_space=vm)] * 5,
        out_specs=pl.BlockSpec(memory_space=vm),
        scratch_shapes=[
            vm((2, LONG, 128), bf),
            vm((2, LONG, 128), bf),
            vm((2, 64, LONG), bf),
            vm((2, 2048, 128), bf),
            vm((2, 2048, 128), bf),
            vm((2, 2048, 128), bf),
            vm((2, LONG, 128), f32),
            vm((2, 64, 2048), f32),
            pltpu.SMEM((128,), jnp.int32),
        ],
        compiler_params=params(),
    )(docs, docs, r, dc, acc, qa)


class Reducer:
    def __init__(self, p, send, order, refs):
        self.p, self.send, self.order = p, send, order
        self.acc, self.cor, self.r1, self.s1, self.r2, self.s2, self.r3 = refs
        self.peers = {"x": p.px, "y": p.py, "z": p.pz}
        self.here = {"x": p.x, "y": (p.yl, p.yh), "z": p.z}
        self.left = [[d for d in "xyz" if d not in order[:n]] for n in range(3)]

    def begin(self, src, sem=None):
        self.c0 = self.send(src.at[:, :, 1 - self.p.core], self.cor, self.p.sib())
        self.own = None
        if sem is not None:
            self.own = pltpu.make_async_copy(src.at[:, :, self.p.core], self.acc, sem)
            self.own.start()

    def scatter(self, src, into, n):
        a = self.order[n]
        return [
            self.send(pick(src, a, self.peers[a](j)[1], self.left[n]), into.at[j - 1], self.peers[a](j)[0]) for j in AXES
        ]

    def first(self):
        self.c0.wait_recv()
        if self.own is not None:
            self.own.wait()
        total(self.acc, self.acc, [self.cor], shape_of("xyz"))
        self.c1 = self.scatter(self.acc, self.r1, 0)

    def gathered(self, copies, out, src, got, n):
        for c in copies:
            c.wait_recv()
        a = self.order[n]
        total(out, pick(src, a, self.here[a], self.left[n]), [got.at[j] for j in range(3)], shape_of(self.left[n + 1]))

    def second(self):
        self.gathered(self.c1, self.s1, self.acc, self.r1, 0)
        self.c2 = self.scatter(self.s1, self.r2, 1)

    def third(self):
        self.gathered(self.c2, self.s2, self.s1, self.r2, 1)
        self.c3 = self.scatter(self.s2, self.r3, 2)

    def result(self):
        for c in self.c3:
            c.wait_recv()
        a = self.order[2]
        m = pick(self.s2, a, self.here[a], self.left[2])[...].astype(f32)
        for j in range(3):
            m = m + self.r3[j].astype(f32)
        return m


def reducer_scratch(order, n):
    vm = pltpu.VMEM
    one, two = shape_of([d for d in "xyz" if d != order[0]]), shape_of(order[2])
    whole = (*shape_of("xyz"), 24, n)
    shapes = [whole, whole, (3, *one, 24, n), (*one, 24, n), (3, *two, 24, n), (*two, 24, n), (3, 24, n)]
    return [vm(s, bf) for s in shapes]


MID = ("yzx", "zyx")


def norm_of(v):
    d = v - jnp.mean(v, axis=-1, keepdims=True)
    s = lax.rsqrt(jnp.mean(d * d, axis=-1, keepdims=True) + NORM_EPS)
    return d * s, s


def norm_back(g, xhat, s, gain):
    e = g * gain
    return s * (e - jnp.mean(e, axis=-1, keepdims=True) - xhat * jnp.mean(e * xhat, axis=-1, keepdims=True))


def down_sum(v):
    return jnp.sum(v, axis=0, keepdims=True)


def store_pieces(g, t, a, b):
    for i in range(32):
        at = (t, i // 16, i // 8 % 2, i // 4 % 2, i % 4)
        piece = g[24 * i : 24 * i + 24].astype(bf)
        a[at] = piece[:, :384]
        b[at] = piece[:, 384:]


def mid_kernel(w, cms, xs, cots, vec, LO, dh1, gup, go, DC, sums, o0, o1, *refs):
    red = [[*refs[3 * i : 3 * i + 3], (o0, o1)[i], None, None, None] for i in range(2)]
    refs = refs[6:]
    cm, wv, wo, zs, cdf, act, gs, ga, gb, lob, dcm, x, cot, ss, rs, ls, os = refs
    p = Place()
    c = lax.axis_index("ctx")
    ctx = [{"ctx": (c + k) % 8} for k in range(1, 8)]
    greet([p.px(k)[0] for k in AXES] + [p.py(k)[0] for k in (1, 3)] + ctx + [p.sib()])
    send = Sender(ss, rs)
    sw = [send(cms.at[(c + k) % 8], cm.at[c], {"ctx": (c + k) % 8}) for k in range(1, 8)]
    swo = pltpu.make_async_copy(cms.at[c], cm.at[c], ls.at[12])
    swo.start()
    ins = [pltpu.make_async_copy(a.at[p.x], b, ls.at[n]) for a, b, n in ((xs, x, 13), (cots, cot, 14))]
    loads = []
    for k in range(3):
        for t in range(4):
            cp = pltpu.make_async_copy(w.at[k, t], wv.at[k * 4 + t], ls.at[k * 4 + t])
            cp.start()
            loads.append(cp)
    for cp in ins:
        cp.start()
    fours = [vec[0, f // 2, f % 2].astype(f32) for f in range(4)]
    pv = [
        jnp.concatenate([f[2 + i // 4 : 3 + i // 4, 192 * (i % 4) : 192 * (i % 4) + 192] for f in fours], axis=1)
        for i in range(6)
    ]
    for t in range(4):
        loads[t].wait()
        o = wv[t, :, 576:768]
        wo[2 * t] = o[:, :128]
        wo[2 * t + 1] = jnp.concatenate([o[:, 128:], o[:, 64:128]], axis=1)
    swo.wait()
    for cp in ins:
        cp.wait()
    for cp in sw:
        cp.wait_recv()
    attn = jnp.zeros((BLK, 768), f32)
    for j in range(8):
        attn = attn + nt(cm[j], wo[j])
    h1 = x[...].astype(f32) + attn + pv[0]
    xh1, s1 = norm_of(h1)
    y1 = xh1 * pv[2] + pv[3]
    y1b = y1.astype(bf)
    ffn = jnp.zeros((BLK, 768), f32)
    for t in range(4):
        loads[4 + t].wait()
        z = nn(y1b, wv[4 + t]) + vec[t, 0, 0, 0:1].astype(f32)
        e = 0.5 * (1.0 + lax.erf(z * (2.0**-0.5)))
        zs[t] = z
        cdf[t] = e
        a = (z * e).astype(bf)
        act[t] = a
        loads[8 + t].wait()
        ffn = ffn + nt(a, wv[8 + t])
    xh2, s2 = norm_of(y1 + ffn + pv[1])
    lob[...] = (xh2 * pv[4] + pv[5]).astype(bf)
    los = [send(lob, LO.at[p.x], p.px(k)[0]) for k in AXES]
    loo = pltpu.make_async_copy(lob, LO.at[p.x], ls.at[12])
    loo.start()
    g = cot[...].astype(f32)
    sums[4:5] = down_sum(g * xh2)
    sums[5:6] = down_sum(g)
    dh2 = norm_back(g, xh2, s2, pv[4])
    sums[1:2] = down_sum(dh2)
    dh2b = dh2.astype(bf)
    dh2t = dh2.T.astype(bf)
    y1t = y1.T.astype(bf)
    for t in range(4):
        store_pieces(nn(dh2t, act[t]), t, ga, gb)
    parts = [Reducer(p, send, o, r) for o, r in zip(MID, red)]
    parts[0].begin(ga, ls.at[0])
    parts[1].begin(gb, ls.at[1])
    dy1 = dh2
    outs = []
    for t in range(4):
        da = nn(dh2b, wv[8 + t]).astype(bf).astype(f32)
        z = zs[t]
        dz = da * (cdf[t] + z * (jnp.exp(-0.5 * z * z) * ((2.0 * math.pi) ** -0.5)))
        sums[8 + t : 9 + t] = down_sum(dz)
        dzb = dz.astype(bf)
        if t >= 2:
            outs[t - 2].wait()
        gs[t % 2] = nn(y1t, dzb).astype(bf)
        cp = pltpu.make_async_copy(gs.at[t % 2], gup.at[t], os.at[t % 2])
        cp.start()
        outs.append(cp)
        dy1 = dy1 + nt(dzb, wv[4 + t])
        if t == 0:
            for part in parts:
                part.first()
    sums[2:3] = down_sum(dy1 * xh1)
    sums[3:4] = down_sum(dy1)
    d1 = norm_back(dy1, xh1, s1, pv[2])
    dh1[...] = d1
    sums[0:1] = down_sum(d1)
    d1b = d1.astype(bf)
    d1t = d1.T.astype(bf)
    for j in range(8):
        dcm[j] = nn(d1b, wo[j]).astype(bf)
    sw = [send(dcm.at[(c + k) % 8], DC.at[c], {"ctx": (c + k) % 8}) for k in range(1, 8)]
    swo = pltpu.make_async_copy(dcm.at[c], DC.at[c], ls.at[2])
    swo.start()
    for t in range(4):
        a, b = nn(d1t, cm[2 * t]), nn(d1t, cm[2 * t + 1])
        go[t] = jnp.concatenate([a[:, :64], a[:, 64:] + b[:, 64:], b[:, :64]], axis=1).astype(bf)
    for part in parts:
        part.gathered(part.c1, part.s1, part.acc, part.r1, 0)
    for cp in los + sw:
        cp.wait_recv()
    for cp in outs[2:] + [swo, loo]:
        cp.wait()
    for cp in send.all:
        cp.wait_send()


def middle(w, cms, xs, cots, vec, cid):
    vm = pltpu.VMEM
    sd = jax.ShapeDtypeStruct
    anywhere, here = pl.BlockSpec(memory_space=pl.ANY), pl.BlockSpec(memory_space=vm)
    left = [shape_of([d for d in "xyz" if d != o[0]]) for o in MID]
    seven = (4, 2, 2, 2, 4, 24)
    return pl.pallas_call(
        mid_kernel,
        out_shape=(
            sd((4, BLK, 768), bf),
            sd((BLK, 768), f32),
            sd((4, 768, 768), bf),
            sd((4, 768, 192), bf),
            sd((8, BLK, 128), bf),
            sd((16, 768), f32),
            sd((*left[0], 24, 384), bf),
            sd((*left[1], 24, 384), bf),
        ),
        in_specs=[anywhere] * 4 + [here],
        out_specs=[anywhere, here, anywhere, here, anywhere, here, here, here],
        scratch_shapes=sum([reducer_scratch(o, 384)[:3] for o in MID], [])
        + [
            vm((8, BLK, 128), bf),
            vm((12, 768, 768), bf),
            vm((8, 768, 128), bf),
            vm((4, BLK, 768), f32),
            vm((4, BLK, 768), f32),
            vm((4, BLK, 768), bf),
            vm((2, 768, 768), bf),
            vm((*seven, 384), bf),
            vm((*seven, 384), bf),
            vm((BLK, 768), bf),
            vm((8, BLK, 128), bf),
            vm((BLK, 768), bf),
            vm((BLK, 768), bf),
            pltpu.SemaphoreType.DMA((40,)),
            pltpu.SemaphoreType.DMA((40,)),
            pltpu.SemaphoreType.DMA((15,)),
            pltpu.SemaphoreType.DMA((2,)),
        ],
        compiler_params=params(cid, 60),
    )(w, cms, xs, cots, vec)


TAIL = ("xyz", "yzx", "zyx")
TAILN = (768, 384, 384)


def tail_kernel(dm, xs, dh1, w, go, gup, vin, n0, n1, R1, R0, R2, V, IG, *refs):
    red, refs = [refs[7 * i : 7 * i + 7] for i in range(3)], refs[21:]
    more, refs = [[None] * 3 + [(n0, n1)[i], *refs[3 * i : 3 * i + 3]] for i in range(2)], refs[6:]
    x, d, wv, ga, gb, igb, igr, acc, vt, vr, ss, rs, ls = refs
    p = Place()
    c = lax.axis_index("ctx")
    core, sib = p.core, p.sib()
    ctx = [{"ctx": (c + k) % 8} for k in range(1, 8)]
    peers = {"x": p.px, "y": p.py, "z": p.pz}
    greet([p.px(k)[0] for k in AXES] + [p.py(k)[0] for k in (1, 3)] + ctx + [sib])
    send = Sender(ss, rs)
    parts = [Reducer(p, send, o, r) for o, r in zip(TAIL, red)]
    parts += [Reducer(p, send, o, r) for o, r in zip(MID, more)]
    parts[0].begin(gup, ls.at[0])
    sw = [send(dm.at[(c + k) % 8], d.at[c], {"ctx": (c + k) % 8}) for k in range(1, 8)]
    swo = pltpu.make_async_copy(dm.at[c], d.at[c], ls.at[1])
    load = pltpu.make_async_copy(w.at[0], wv, ls.at[2])
    swo.start()
    rows = pltpu.make_async_copy(xs.at[p.x], x, ls.at[3])
    rows.start()
    load.start()
    parts[0].first()
    for q in (3, 4):
        parts[q].c2 = parts[q].scatter(parts[q].s1, parts[q].r2, 1)
    rows.wait()
    xt = x[...].astype(f32).T.astype(bf)
    acc[...] = dh1[...]
    swo.wait()
    load.wait()
    for cp in sw:
        cp.wait_recv()
    vt[0, :60] = vin[:60]
    for t in range(4):
        a, b = d[2 * t].astype(f32), d[2 * t + 1].astype(f32)
        pre = jnp.concatenate([a[:, :192], a[:, 192:] + b[:, 192:], b[:, :192]], axis=1)
        sums = jnp.concatenate([down_sum(pre), jnp.zeros((1, 64), f32)], axis=1)
        for k in range(5):
            vt[0, 60 + 5 * t + k : 61 + 5 * t + k] = sums[:, 128 * k : 128 * k + 128]
        pre = pre.astype(bf)
        g = jnp.concatenate([nn(xt, pre), go[t].astype(f32)], axis=1)
        store_pieces(g, t, ga, gb)
        acc[...] += nt(pre, wv[t, :, :576])
    parts[1].begin(ga, ls.at[0])
    parts[2].begin(gb, ls.at[1])
    igb[...] = acc[...].astype(bf)
    igr[p.x] = igb[...]
    ig = [send(igb, igr.at[p.x], p.px(k)[0]) for k in AXES]
    cv = send(vt.at[0], vr.at[0, 0], sib)
    parts[1].first()
    parts[2].first()
    cv.wait_recv()
    vt[1] = vt[0] + vr[0, 0]

    def vsend(i, a):
        return [send(vt.at[i], vr.at[i, j - 1], peers[a](j)[0]) for j in AXES]

    def vsum(i, cs):
        for cp in cs:
            cp.wait_recv()
        return vt[i] + vr[i, 0] + vr[i, 1] + vr[i, 2]

    v1 = vsend(1, "z")
    for q in (3, 4):
        parts[q].third()
    parts[0].second()
    vt[2] = vsum(1, v1)
    v2 = vsend(2, "y")
    for q in (1, 2):
        parts[q].second()
    vt[3] = vsum(2, v2)
    v3 = vsend(3, "x")
    for q in (0, 1, 2):
        parts[q].third()
    V[...] = vsum(3, v3)
    for cp in ig:
        cp.wait_recv()
    IG[...] = igr[...].astype(f32)
    R1[...] = parts[0].result()
    R2[:, :384] = parts[3].result()
    R2[:, 384:] = parts[4].result()
    R0[:, :384] = parts[1].result()
    R0[:, 384:] = parts[2].result()
    for cp in send.all:
        cp.wait_send()


def finale(dm, xs, dh1, w, go, gup, vin, n0, n1, cid):
    vm = pltpu.VMEM
    sd = jax.ShapeDtypeStruct
    anywhere, here = pl.BlockSpec(memory_space=pl.ANY), pl.BlockSpec(memory_space=vm)
    scratch = sum([reducer_scratch(o, n) for o, n in zip(TAIL, TAILN)], [])
    scratch += sum([reducer_scratch(o, 384)[4:] for o in MID], [])
    seven = (4, 2, 2, 2, 4, 24)
    return pl.pallas_call(
        tail_kernel,
        out_shape=(sd((24, 768), f32), sd((24, 768), f32), sd((24, 768), f32), sd((80, 128), f32), sd((4, BLK, 768), f32)),
        in_specs=[anywhere, anywhere, here, anywhere, here, anywhere, here, here, here],
        out_specs=[here] * 5,
        scratch_shapes=scratch
        + [
            vm((BLK, 768), bf),
            vm((8, BLK, 384), bf),
            vm((4, 768, 768), bf),
            vm((*seven, 384), bf),
            vm((*seven, 384), bf),
            vm((BLK, 768), bf),
            vm((4, BLK, 768), bf),
            vm((BLK, 768), f32),
            vm((4, 80, 128), f32),
            vm((4, 3, 80, 128), f32),
            pltpu.SemaphoreType.DMA((64,)),
            pltpu.SemaphoreType.DMA((64,)),
            pltpu.SemaphoreType.DMA((4,)),
        ],
        compiler_params=params(cid, 60),
    )(dm, xs, dh1, w, go, gup.reshape(*seven, 768), vin, n0, n1)


NINE = ((0, 0), (1, 0), (2, 0), (2, 2), (0, 2), (1, 2), (0, 1), (1, 1), (2, 1))
TURN = (0, 2, 1)


def shards(
    layer_input,
    segment_ids,
    proj_weight,
    proj_bias,
    out_weight,
    out_bias,
    first_gain,
    first_shift,
    up_weight,
    up_bias,
    down_weight,
    down_bias,
    second_gain,
    second_shift,
    cotangent,
):
    tp = lax.axis_index("tp")
    out_t = out_weight.T

    def head(h):
        return slice(64 * h, 64 * h + 64)

    p0 = jnp.concatenate([proj_weight[k, :, head(h)] for k, h in NINE] + [out_t[:, head(h)] for h in TURN], axis=1)
    none = jnp.zeros((64,), bf)
    pb = jnp.concatenate([none if k == 1 else proj_bias[k // 2, head(h)] for k, h in NINE] + [none] * 3)
    vec = jnp.concatenate(
        [up_bias, pb, out_bias, down_bias, first_gain, first_shift, second_gain, second_shift, jnp.zeros((3456,), bf)]
    ).reshape(8, 768)
    seg = lax.dynamic_index_in_dim(segment_ids, tp, 0, keepdims=False).reshape(2, 128)
    w, vec, r, docs = front(p0, up_weight, down_weight.T, vec, layer_input, seg, 1)
    w = w.reshape(3, 4, 768, 768)
    cmsg, acc, qa = attend(docs, r)
    layer_output, dh1, gup, go, dc, sums, n0, n1 = middle(w, cmsg, layer_input, cotangent, vec, 2)
    dmsg = unattend(docs, r, dc, acc, qa)
    vin = jnp.concatenate([sums[:6].reshape(36, 128), sums[8:12].reshape(24, 128), jnp.zeros((20, 128), f32)])
    r1, r0, r2, vs, input_grad = finale(dmsg, layer_input, dh1, w, go, gup, vin, n0, n1, 3)
    at = {kh: i for i, kh in enumerate(NINE)}
    proj = jnp.stack([jnp.concatenate([r0[:, head(at[k, h])] for h in range(3)], axis=1) for k in range(3)])
    out_grad = jnp.concatenate([r0[:, head(9 + TURN[h])] for h in range(3)], axis=1).T
    fc = lax.axis_index(("fsdp", "ctx"))
    six = lax.dynamic_index_in_dim(vs[:36].reshape(6, 32, 24), fc, 1, keepdims=False)
    upb = lax.dynamic_index_in_dim(vs[36:60].reshape(4, 768), tp, 0, keepdims=False)
    pbs = lax.dynamic_index_in_dim(vs[60:80].reshape(4, 640), tp, 0, keepdims=False)
    pbg = jnp.stack([jnp.concatenate([pbs[head(at[k, h])] for h in range(3)]) for k in (0, 2)])
    return (
        layer_output,
        input_grad,
        proj,
        pbg,
        out_grad,
        six[0],
        six[2],
        six[3],
        r1,
        upb,
        r2.T,
        six[1],
        six[4],
        six[5],
    )


def solution(mesh):
    placed = (
        P("fsdp", "ctx", None),
        P("fsdp", "ctx"),
        P(None, "fsdp", "tp"),
        P(None, "tp"),
        P("tp", "fsdp"),
        P("fsdp"),
        P("fsdp"),
        P("fsdp"),
        P("fsdp", "tp"),
        P("tp"),
        P("tp", "fsdp"),
        P("fsdp"),
        P("fsdp"),
        P("fsdp"),
        P("fsdp", "ctx", None),
    )
    return jax.shard_map(
        shards,
        mesh=mesh,
        in_specs=placed,
        out_specs=(
            P("fsdp", "ctx", None),
            P("fsdp", "ctx", None),
            P(None, ("fsdp", "ctx"), "tp"),
            P(None, "tp"),
            P("tp", ("fsdp", "ctx")),
            P(("fsdp", "ctx")),
            P(("fsdp", "ctx")),
            P(("fsdp", "ctx")),
            P(("fsdp", "ctx"), "tp"),
            P("tp"),
            P("tp", ("fsdp", "ctx")),
            P(("fsdp", "ctx")),
            P(("fsdp", "ctx")),
            P(("fsdp", "ctx")),
        ),
        check_vma=False,
    )
```

```python
import functools
import math

import jax
import jax.numpy as jnp
from jax import lax
from jax.experimental import pallas as pl
from jax.experimental.pallas import tpu as pltpu
from jax.sharding import PartitionSpec as P

HEAD_DIM = 64
NORM_EPS = 1e-12

MESH = pl.DeviceIdType.MESH
bf=jnp.bfloat16; f32=jnp.float32

class Place:
    def __init__(self):
        self.x=lax.axis_index("tp"); f=lax.axis_index("fsdp"); c=lax.axis_index("ctx")
        self.yl=f//2; self.core=f%2; self.yh=c//4; self.z=c%4
        self.y=self.yh*2+self.yl
    def px(self,k):
        q=(self.x+k)%4
        return {"tp":q}, q
    def pz(self,k):
        q=(self.z+k)%4
        return {"ctx":self.yh*4+q}, q
    def py(self,k):
        q=(self.y+k)%4
        return {"fsdp":(q%2)*2+self.core,"ctx":(q//2)*4+self.z}, (q%2,q//2)
    def sib(self):
        return {"fsdp":self.yl*2+1-self.core}

def greet(devs):
    bar=pltpu.get_barrier_semaphore()
    for d in devs: pl.semaphore_signal(bar,inc=1,device_id=d,device_id_type=MESH)
    pl.semaphore_wait(bar,len(devs))

def rcopy(src,dst,ss,rs,dev):
    return pltpu.make_async_remote_copy(src_ref=src,dst_ref=dst,send_sem=ss,recv_sem=rs,device_id=dev,device_id_type=MESH)


DIMS = {"x": (4,), "y": (2, 2), "z": (4,)}
ORDER = ("xyz", "yzx", "zxy")


def shape_of(axes):
    return sum([DIMS[d] for d in "xyz" if d in axes], ())


def split_index(i, shape):
    out = []
    for s in reversed(shape):
        out.insert(0, i % s)
        i = i // s
    return tuple(out)


def pick(ref, axis, q, left):
    at = []
    for d in "xyz":
        if d in left:
            at += list(q if d == "y" else (q,)) if d == axis else [slice(None)] * len(DIMS[d])
    return ref.at[tuple(at)]


def total(dst, first, others, shape):
    outer = shape[: max(0, len(shape) - 2)] if len(shape) != 2 or shape == (4, 4) else ()
    outer = shape[:1] if shape == (4, 4) else outer

    def block(at):
        at = at + (Ellipsis,)
        if len(others) == 1:
            dst[at] = first[at] + others[0][at]
        else:
            a = first[at].astype(f32)
            for o in others:
                a = a + o[at].astype(f32)
            dst[at] = a.astype(dst.dtype)

    if outer:

        @pl.loop(0, math.prod(outer))
        def _(i):
            block(split_index(i, outer))
    else:
        block(())


SQ = HEAD_DIM ** -0.5
FAR = float(2.0 ** 100)
BLK = 256


def nt(a, b):
    return lax.dot_general(a, b, (((1,), (1,)), ((), ())), preferred_element_type=f32)


def nn(a, b):
    return jnp.dot(a, b, preferred_element_type=f32)


def params(cid=None, mb=48):
    return pltpu.CompilerParams(collective_id=cid, has_side_effects=cid is not None, vmem_limit_bytes=mb << 20)


NINE = ((0, 0), (1, 0), (2, 0), (2, 2), (0, 2), (1, 2), (0, 1), (1, 1), (2, 1))
AT = {kh: i for i, kh in enumerate(NINE)}
TURN = (0, 2, 1)
TAILMB, MIDMB, FRONTMB = 48, 50, 48


def head(h):
    return slice(64 * h, 64 * h + 64)


class Sender:
    def __init__(self, ss, rs):
        self.ss, self.rs, self.all = ss, rs, []

    def __call__(self, src, dst, dev):
        i = len(self.all)
        c = rcopy(src, dst, self.ss.at[i], self.rs.at[i], dev)
        c.start()
        self.all.append(c)
        return c


AXES = (1, 2, 3)


class Spread:
    def __init__(self, p, send, own, to, rx, ry, rz):
        self.p, self.send, self.own, self.to = p, send, own, to
        self.rx, self.ry, self.rz = rx, ry, rz
        self.half = ry[0] + pl.multiple_of(p.yh * (ry[1] // 2), 8), ry[1] // 2
        self.quarter = rz[0] + pl.multiple_of(p.z * (rz[1] // 4), 8), rz[1] // 4

    def rows(self, what):
        a, n = what
        return pl.ds(a if isinstance(a, int) else pl.multiple_of(a, 8), n)

    def out(self, t, yl, what):
        return self.to.at[t, yl, self.p.core, self.rows(what)]

    def pass_on(self, t, yl, what, devs):
        return [self.send(self.out(t, yl, what), self.out(t, yl, what), d) for d in devs]

    def start(self):
        p = self.p
        nb = {"fsdp": (1 - p.yl) * 2 + p.core}
        mine = lambda what: self.own.at[self.rows(what)]
        push = lambda what, devs: [self.send(mine(what), self.out(p.x, p.yl, what), d) for d in devs]
        xs = [p.px(k)[0] for k in AXES]
        self.nz = push(self.quarter, [nb])[0] if self.rz[1] else None
        self.nx = push(self.rx, [nb])[0]
        self.xy = push(self.half, xs)
        self.xz = push(self.quarter, xs)
        self.yy = push(self.half, [p.py(k)[0] for k in (1, 3)])

    def second(self):
        p = self.p
        xs = [p.px(k)[0] for k in AXES]
        ys = [p.py(k)[0] for k in AXES]
        zs = [p.pz(k)[0] for k in AXES]
        self.nz.wait_recv()
        self.xz2 = self.pass_on(p.x, 1 - p.yl, self.quarter, xs)
        self.zz = self.pass_on(p.x, 1 - p.yl, self.quarter, zs)
        self.xx = [self.send(self.own.at[self.rows(self.rx)], self.out(p.x, p.yl, self.rx), d) for d in xs]
        self.nx.wait_recv()
        self.xx2 = self.pass_on(p.x, 1 - p.yl, self.rx, xs)
        for k in AXES:
            t = (p.x + 4 - k) % 4
            self.xy[k - 1].wait_recv()
            self.yy += self.pass_on(t, p.yl, self.half, ys)
            self.xz[k - 1].wait_recv()
            self.zz += self.pass_on(t, p.yl, self.quarter, zs)
        for k in AXES:
            t = (p.x + 4 - k) % 4
            self.xz2[k - 1].wait_recv()
            self.zz += self.pass_on(t, 1 - p.yl, self.quarter, zs)

    def finish(self):
        for c in self.yy + self.zz + self.xx + self.xx2:
            c.wait_recv()


def front_kernel(p0, p1, p2, vec, xs, seg, W, V, R, S, po, m, x, ss, rs, ls):
    p = Place()
    c = lax.axis_index("ctx")
    core, sib = p.core, p.sib()
    ctx = [{"ctx": (c + k) % 8} for k in range(1, 8)]
    greet([p.px(k)[0] for k in AXES] + [p.py(k)[0] for k in (1, 3)] + ctx + [sib])
    send = Sender(ss, rs)
    own = pltpu.make_async_copy(p0, po.at[p.x, p.yl, core], ls.at[0])
    mine = pltpu.make_async_copy(vec, V.at[p.x, p.yl, core], ls.at[1])
    rows = pltpu.make_async_copy(xs.at[p.x], x, ls.at[2])
    up = pltpu.make_async_copy(p1, W.at[1, p.x, p.yl, core], ls.at[4])
    down = pltpu.make_async_copy(p2, W.at[2, p.x, p.yl, core], ls.at[5])
    for cp in (own, mine, rows, up, down):
        cp.start()
    nb = {"fsdp": (1 - p.yl) * 2 + core}
    first = Spread(p, send, p0, po, (0, 64), (64, 64), (128, 64))
    first.start()
    vn = send(vec, V.at[p.x, p.yl, core], nb)
    vx = [send(vec, V.at[p.x, p.yl, core], p.px(k)[0]) for k in AXES]
    sg = [send(seg, S.at[c], d) for d in ctx]
    sgo = pltpu.make_async_copy(seg, S.at[c], ls.at[3])
    sgo.start()
    d0 = [send(p0, po.at[p.x, p.yl, core], sib)]
    dv = [send(vec, V.at[p.x, p.yl, core], sib)]
    first.second()
    vn.wait_recv()
    vx += [send(V.at[p.x, 1 - p.yl, core], V.at[p.x, 1 - p.yl, core], p.px(k)[0]) for k in AXES]
    bulk = [
        Spread(p, send, p1, W.at[1], (0, 96), (96, 64), (160, 32)),
        Spread(p, send, p2, W.at[2], (0, 64), (64, 64), (128, 64)),
    ]
    for b in bulk:
        b.start()
    first.finish()
    for cp in vx:
        cp.wait_recv()
    own.wait()
    mine.wait()
    d0.append(send(po.at[p.x, 1 - p.yl, core], po.at[p.x, 1 - p.yl, core], sib))
    dv.append(send(V.at[p.x, 1 - p.yl, core], V.at[p.x, 1 - p.yl, core], sib))
    for k in AXES:
        t = (p.x + k) % 4
        d0.append(send(po.at[t, :, core], po.at[t, :, core], sib))
        dv.append(send(V.at[t, :, core], V.at[t, :, core], sib))
    for b in bulk:
        b.second()
    for cp in d0 + dv:
        cp.wait_recv()
    rows.wait()
    back = pltpu.make_async_copy(po, W.at[0], ls.at[0])
    back.start()

    @pl.loop(0, 4)
    def _(t):
        qv = V[t, 0, 0].astype(f32)
        b = [jnp.zeros((1, 64), f32) if k == 1 else qv[6 + k // 2 : 7 + k // 2, head(h)] for k, h in NINE]
        b = jnp.concatenate(b + [jnp.zeros((1, 192), f32)], axis=1)
        r = (nn(x[...], po[t].reshape(768, 768)) + b).astype(bf)
        m[2 * t] = r[:, :384]
        m[2 * t + 1] = jnp.concatenate([r[:, 384:576], r[:, 192:384]], axis=1)

    sw = [send(m.at[(c + k) % 8], R.at[c], {"ctx": (c + k) % 8}) for k in range(1, 8)]
    swo = pltpu.make_async_copy(m.at[c], R.at[c], ls.at[2])
    swo.start()
    for b in bulk:
        b.finish()
    up.wait()
    down.wait()
    dw = []
    for k in range(4):
        t = (p.x + k) % 4
        dw.append(send(W.at[pl.ds(1, 2), t, :, core], W.at[pl.ds(1, 2), t, :, core], sib))
    for cp in sg + sw + dw:
        cp.wait_recv()
    for cp in send.all:
        cp.wait_send()
    for cp in (back, swo, sgo):
        cp.wait()


def front(p0, p1, p2, vec, xs, seg, cid):
    sd = jax.ShapeDtypeStruct
    vm = pltpu.VMEM
    anywhere, here = pl.BlockSpec(memory_space=pl.ANY), pl.BlockSpec(memory_space=vm)
    count = 192
    return pl.pallas_call(
        front_kernel,
        out_shape=(
            sd((3, 4, 2, 2, 192, 768), bf),
            sd((4, 2, 2, 16, 192), bf),
            sd((8, BLK, 384), bf),
            sd((8, 2, 128), jnp.int32),
        ),
        in_specs=[here] * 3 + [anywhere] * 3,
        out_specs=[anywhere, here, anywhere, anywhere],
        scratch_shapes=[
            vm((4, 2, 2, 192, 768), bf),
            vm((8, BLK, 384), bf),
            vm((BLK, 768), bf),
            pltpu.SemaphoreType.DMA((count,)),
            pltpu.SemaphoreType.DMA((count,)),
            pltpu.SemaphoreType.DMA((6,)),
        ],
        compiler_params=params(cid),
    )(p0, p1, p2, vec, xs, seg)


LONG = 2048 + BLK
SAFE = 120.0 / SQ
FWD = 8
BWD = 4


def blocks(edge, lst, par, unit):
    n = jnp.int32(0)
    for h in range(2):
        for i in range(8 if h == 0 else 4):
            qi = i if h == 0 else 2 * i + par
            lo, hi = jnp.int32(0), jnp.int32(0)
            for j in range(8):
                lo = lo + (edge[j, 1, 127] < edge[qi, 0, 0]).astype(jnp.int32)
                hi = hi + (edge[j, 0, 0] <= edge[qi, 1, 127]).astype(jnp.int32)

            def put(j, n):
                lst[n] = (h * 8 + qi) * 16 + j
                return n + 1

            n = lax.fori_loop(lo, hi, put, n)
    for k in range(unit - 1):
        lst[n + k] = 8
    return (n + unit - 1) // unit


def triple(code):
    j = code % 16
    i = (code // 16) % 8
    return code // 128, pl.ds(pl.multiple_of(i * BLK, BLK), BLK), pl.ds(pl.multiple_of(j * BLK, BLK), BLK), i


def lanes():
    return lax.broadcasted_iota(jnp.int32, (1, 128), 1)


def three(v, at, lane):
    a = v.astype(bf).astype(f32)
    b = (v - a).astype(bf).astype(f32)
    c = v - a - b
    return jnp.where(lane == at, a, jnp.where(lane == at + 1, b, jnp.where(lane == at + 2, c, 0.0))).astype(bf)


def flat(r, k):
    return r[:, :, 128 * k : 128 * k + 128].reshape(2048, 128)


def turned(v):
    return v.astype(f32).T.astype(bf)


def one_lane(h, lane):
    return lane == (72 if h == 0 else 8)


def doc_rows(docs):
    seg = jnp.concatenate([docs[j, i : i + 1] for j in range(8) for i in range(2)] + [jnp.full((1, BLK), -1)], axis=1)
    row = lax.broadcasted_iota(jnp.int32, (64, 1), 0)
    return seg, jnp.where(((row < 4) & (row != seg)) | ((row >= 8) & (row < 11)), 1.0, 0.0)


def attend_kernel(edge, docs, r, msg, acc, qa, kt, va, top, lst):
    par = lax.axis_index("ctx") % 2
    lane = lanes()
    count = blocks(edge, lst, par, FWD)
    seg, augk = doc_rows(docs)
    row = lax.broadcasted_iota(jnp.int32, (128, 1), 0) - 64
    augq = jnp.where(row == seg[:, :2048], -FAR, 0.0).T.astype(bf)
    augk = augk.astype(bf)
    vv = flat(r, 1)
    safe = jnp.bool_(True)
    for h in range(2):
        qk = flat(r, 2 * h)
        qa[h] = jnp.where(lane < 64, qk * bf(SQ), augq)
        kt[h, :64, :2048] = turned(qk)[64:]
        kt[h, :64, 2048:] = jnp.zeros((64, BLK), bf)
        kt[h, 64:] = augk
        va[h, :2048] = jnp.where((lane < 64) if h == 0 else (lane >= 64), vv, one_lane(h, lane).astype(bf))
        va[h, 2048:] = jnp.zeros((BLK, 128), bf)
        f = qk.astype(f32)
        safe = safe & (jnp.max(jnp.sum(f * f, axis=1, keepdims=True)) < SAFE)
    acc[...] = jnp.zeros_like(acc)

    @pl.when(jnp.logical_not(safe))
    def _():
        top[...] = jnp.full_like(top, -3e38)

        @pl.loop(0, count * FWD)
        def _(n):
            h, at, to, i = triple(lst[n])
            s = jnp.max(nn(qa[h, at], kt[h, :, to]), axis=1, keepdims=True)
            top[h, at] = jnp.maximum(top[h, at], s)

        for h in range(2):
            for i in range(8):
                at = slice(i * BLK, i * BLK + BLK)
                qa[h, at] = qa[h, at] + three(-top[h, at, :1], 72, lane)

    @pl.loop(0, count)
    def _(n):
        tr = [triple(lst[n * FWD + u]) for u in range(FWD)]
        ps = [nn(qa[h, at], kt[h, :, to]) for h, at, to, _ in tr]
        ps = [jnp.exp(p).astype(bf) for p in ps]
        got = [(h, at, nn(p, va[h, to])) for p, (h, at, to, _) in zip(ps, tr)]
        for h, at, o in got:
            acc[h, at] += o

    for i in range(8):
        at = slice(i * BLK, i * BLK + BLK)
        a = acc[0, at] * (1.0 / acc[0, at, 72:73])
        b = acc[1, at] * (1.0 / acc[1, at, 8:9])
        b = jnp.where(par == i % 2, b, 0.0)
        msg[i] = jnp.where(lane < 64, a, b).astype(bf)


def attend(docs, r):
    vm = pltpu.VMEM
    sd = jax.ShapeDtypeStruct
    return pl.pallas_call(
        attend_kernel,
        out_shape=(sd((8, BLK, 128), bf), sd((2, 2048, 128), f32), sd((2, 2048, 128), bf)),
        in_specs=[pl.BlockSpec(memory_space=pltpu.SMEM)] + [pl.BlockSpec(memory_space=vm)] * 2,
        out_specs=[pl.BlockSpec(memory_space=vm)] * 3,
        scratch_shapes=[
            vm((2, 128, LONG), bf),
            vm((2, LONG, 128), bf),
            vm((2, 2048, 128), f32),
            pltpu.SMEM((128,), jnp.int32),
        ],
        compiler_params=params(),
    )(docs, docs, r)


def unattend_kernel(edge, docs, r, dc, acc, qa, out, ka, va, kt, ga, gz, qz, dkv, dqt, lst):
    par = lax.axis_index("ctx") % 2
    lane = lanes()
    count = blocks(edge, lst, par, BWD)
    vv, gg = flat(r, 1), flat(dc, 0)
    tops = doc_rows(docs)[1].T.astype(bf)
    for h in range(2):
        qk = flat(r, 2 * h)
        low = (lane < 64) if h == 0 else (lane >= 64)
        at = 72 if h == 0 else 8
        kt[h, :, :2048] = turned(qk)[64:]
        kt[h, :, 2048:] = jnp.zeros((64, BLK), bf)
        ka[h, :2048] = jnp.concatenate([qk[:, 64:], tops[:2048]], axis=1)
        ka[h, 2048:] = jnp.concatenate([jnp.zeros((BLK, 64), bf), tops[2048:]], axis=1)
        ones = ((lane >= at) & (lane < at + 3)).astype(bf)
        va[h, :2048] = jnp.where(low, vv, ones)
        va[h, 2048:] = jnp.zeros((BLK, 128), bf)
        inv = 1.0 / acc[h, :, at : at + 1]
        g = jnp.where(low, gg.astype(f32), 0.0)
        g = (g * inv).astype(bf)
        delta = jnp.sum(g.astype(f32) * acc[h], axis=1, keepdims=True) * inv
        gz[h] = g
        ga[h] = g + three(-delta, at, lane)
        q = jnp.where(lane < 64, qa[h], bf(0))
        qz[h] = pltpu.roll(q.astype(f32), 64, 1).astype(bf) if h == 0 else q
    dqt[...] = jnp.zeros_like(dqt)
    dkv[...] = jnp.zeros_like(dkv)

    @pl.loop(0, count)
    def _(n):
        tr = [triple(lst[n * BWD + u]) for u in range(BWD)]
        ps = [nt(ka[h, to], qa[h, at]) for h, at, to, _ in tr]
        dp = [nt(va[h, to], ga[h, at]) for h, at, to, _ in tr]
        ps = [jnp.exp(p) for p in ps]
        ds = [(p * d).astype(bf) for p, d in zip(ps, dp)]
        ps = [p.astype(bf) for p in ps]
        kv = [nn(p, gz[h, at]) + nn(d, qz[h, at]) for p, d, (h, at, to, _) in zip(ps, ds, tr)]
        dq = [nn(kt[h, :, to], d) for d, (h, at, to, _) in zip(ds, tr)]
        got = [(h, at, to, a, b) for a, b, (h, at, to, _) in zip(kv, dq, tr)]
        for h, at, to, kv, dq in got:
            dkv[h, to] += kv
            dqt[h, :, at] += dq

    for i in range(8):
        a = slice(i * BLK, i * BLK + BLK)
        q0, q1 = [jnp.concatenate([(dqt[h, :, a] * SQ).T] * 2, axis=1) for h in range(2)]
        q1 = jnp.where(par == i % 2, q1, 0.0)
        kv0, kv1 = dkv[0, a], dkv[1, a]
        out[i, :, :128] = jnp.where(lane < 64, q0, kv0).astype(bf)
        out[i, :, 128:256] = jnp.where(lane < 64, kv0, kv1).astype(bf)
        out[i, :, 256:] = jnp.where(lane < 64, q1, pltpu.roll(kv1, 64, 1)).astype(bf)


def unattend(docs, r, dc, acc, qa):
    vm = pltpu.VMEM
    return pl.pallas_call(
        unattend_kernel,
        out_shape=jax.ShapeDtypeStruct((8, BLK, 384), bf),
        in_specs=[pl.BlockSpec(memory_space=pltpu.SMEM)] + [pl.BlockSpec(memory_space=vm)] * 5,
        out_specs=pl.BlockSpec(memory_space=vm),
        scratch_shapes=[
            vm((2, LONG, 128), bf),
            vm((2, LONG, 128), bf),
            vm((2, 64, LONG), bf),
            vm((2, 2048, 128), bf),
            vm((2, 2048, 128), bf),
            vm((2, 2048, 128), bf),
            vm((2, LONG, 128), f32),
            vm((2, 64, 2048), f32),
            pltpu.SMEM((128,), jnp.int32),
        ],
        compiler_params=params(),
    )(docs, docs, r, dc, acc, qa)


class Reducer:
    def __init__(self, p, send, order, refs):
        self.p, self.send, self.order = p, send, order
        self.acc, self.cor, self.r1, self.s1, self.r2, self.s2, self.r3 = refs
        self.peers = {"x": p.px, "y": p.py, "z": p.pz}
        self.here = {"x": p.x, "y": (p.yl, p.yh), "z": p.z}
        self.left = [[d for d in "xyz" if d not in order[:n]] for n in range(3)]

    def begin(self, src, sem):
        self.c0 = [self.send(src.at[:, :, 1 - self.p.core], self.cor, self.p.sib())]
        self.own = pltpu.make_async_copy(src.at[:, :, self.p.core], self.acc, sem)
        self.own.start()
        self.mine = self.acc

    def begin_at(self, src, t):
        self.c0 = ([] if t == 0 else self.c0) + [self.send(src.at[t, :, 1 - self.p.core], self.cor.at[t], self.p.sib())]
        self.own, self.mine = None, src.at[:, :, self.p.core]

    def scatter(self, src, into, n):
        a = self.order[n]
        return [
            self.send(pick(src, a, self.peers[a](j)[1], self.left[n]), into.at[j - 1], self.peers[a](j)[0]) for j in AXES
        ]

    def first(self):
        for c in self.c0:
            c.wait_recv()
        if self.own is not None:
            self.own.wait()
        total(self.acc, self.mine, [self.cor], shape_of("xyz"))
        self.c1 = self.scatter(self.acc, self.r1, 0)

    def gathered(self, copies, out, src, got, n):
        for c in copies:
            c.wait_recv()
        a = self.order[n]
        total(out, pick(src, a, self.here[a], self.left[n]), [got.at[j] for j in range(3)], shape_of(self.left[n + 1]))

    def second(self):
        self.gathered(self.c1, self.s1, self.acc, self.r1, 0)
        self.c2 = self.scatter(self.s1, self.r2, 1)

    def third(self):
        self.gathered(self.c2, self.s2, self.s1, self.r2, 1)
        self.c3 = self.scatter(self.s2, self.r3, 2)

    def result(self):
        for c in self.c3:
            c.wait_recv()
        a = self.order[2]
        m = pick(self.s2, a, self.here[a], self.left[2])[...].astype(f32)
        for j in range(3):
            m = m + self.r3[j].astype(f32)
        return m


def reducer_scratch(order, n):
    vm = pltpu.VMEM
    one, two = shape_of([d for d in "xyz" if d != order[0]]), shape_of(order[2])
    whole = (*shape_of("xyz"), 24, n)
    shapes = [whole, whole, (3, *one, 24, n), (*one, 24, n), (3, *two, 24, n), (*two, 24, n), (3, 24, n)]
    return [vm(s, bf) for s in shapes]


MID = ("yzx", "zyx")


def norm_of(v):
    d = v - jnp.mean(v, axis=-1, keepdims=True)
    s = lax.rsqrt(jnp.mean(d * d, axis=-1, keepdims=True) + NORM_EPS)
    return d * s, s


def norm_back(g, xhat, s, gain):
    e = g * gain
    return s * (e - jnp.mean(e, axis=-1, keepdims=True) - xhat * jnp.mean(e * xhat, axis=-1, keepdims=True))


def down_sum(v):
    return jnp.sum(v, axis=0, keepdims=True)


def store_pieces(g, t, a, b):
    for i in range(32):
        at = (t, i // 16, i // 8 % 2, i // 4 % 2, i % 4)
        piece = g[24 * i : 24 * i + 24].astype(bf)
        a[at] = piece[:, :384]
        b[at] = piece[:, 384:]


def mid_kernel(w, cms, xs, cots, vec, LO, dh1, gup, go, DC, sums, o0, o1, *refs):
    red = [[*refs[3 * i : 3 * i + 3], (o0, o1)[i], None, None, None] for i in range(2)]
    refs = refs[6:]
    cm, wv, wo, zs, cdf, act, gs, ga, gb, lob, dcm, x, cot, ss, rs, ls, os = refs
    p = Place()
    c = lax.axis_index("ctx")
    ctx = [{"ctx": (c + k) % 8} for k in range(1, 8)]
    greet([p.px(k)[0] for k in AXES] + [p.py(k)[0] for k in (1, 3)] + ctx + [p.sib()])
    send = Sender(ss, rs)

    def put(i, row):
        for k in range(6):
            sums[6 * i + k : 6 * i + k + 1] = row[:, 128 * k : 128 * k + 128]

    sw = [send(cms.at[(c + k) % 8], cm.at[c], {"ctx": (c + k) % 8}) for k in range(1, 8)]
    swo = pltpu.make_async_copy(cms.at[c], cm.at[c], ls.at[12])
    swo.start()
    ins = [pltpu.make_async_copy(a.at[p.x], b, ls.at[n]) for a, b, n in ((xs, x, 13), (cots, cot, 14))]
    loads = []
    for k in range(3):
        for t in range(4):
            cp = pltpu.make_async_copy(w.at[k, t], wv.at[k * 4 + t], ls.at[k * 4 + t])
            cp.start()
            loads.append(cp)
    for cp in ins:
        cp.start()
    fours = [vec[0, f // 2, f % 2].astype(f32) for f in range(4)]
    pv = [jnp.concatenate([f[i : i + 1] for f in fours], axis=1) for i in range(6)]
    for t in range(4):
        loads[t].wait()
        o = wv[t, :, 576:768]
        wo[2 * t] = o[:, :128]
        wo[2 * t + 1] = jnp.concatenate([o[:, 128:], o[:, 64:128]], axis=1)
    swo.wait()
    for cp in ins:
        cp.wait()
    for cp in sw:
        cp.wait_recv()
    attn = jnp.zeros((BLK, 768), f32)
    for j in range(8):
        attn = attn + nt(cm[j], wo[j])
    h1 = x[...].astype(f32) + attn + pv[0]
    xh1, s1 = norm_of(h1)
    y1 = xh1 * pv[2] + pv[3]
    y1b = y1.astype(bf)
    ffn = jnp.zeros((BLK, 768), f32)
    for t in range(4):
        loads[4 + t].wait()
        z = nn(y1b, wv[4 + t]) + jnp.concatenate([vec[t, 0, 0, 8 + k : 9 + k].astype(f32) for k in range(4)], axis=1)
        e = 0.5 * (1.0 + lax.erf(z * (2.0**-0.5)))
        zs[t] = z
        cdf[t] = e
        a = (z * e).astype(bf)
        act[t] = a
        loads[8 + t].wait()
        ffn = ffn + nt(a, wv[8 + t])
    xh2, s2 = norm_of(y1 + ffn + pv[1])
    lob[...] = (xh2 * pv[4] + pv[5]).astype(bf)
    los = [send(lob, LO.at[p.x], p.px(k)[0]) for k in AXES]
    loo = pltpu.make_async_copy(lob, LO.at[p.x], ls.at[12])
    loo.start()
    g = cot[...].astype(f32)
    put(4, down_sum(g * xh2))
    put(5, down_sum(g))
    dh2 = norm_back(g, xh2, s2, pv[4])
    put(1, down_sum(dh2))
    dh2b = dh2.astype(bf)
    dh2t = dh2.T.astype(bf)
    y1t = y1.T.astype(bf)
    parts = [Reducer(p, send, o, r) for o, r in zip(MID, red)]
    for t in range(4):
        store_pieces(nn(dh2t, act[t]), t, ga, gb)
        parts[0].begin_at(ga, t)
        parts[1].begin_at(gb, t)
    dy1 = dh2
    outs = []
    for t in range(4):
        da = nn(dh2b, wv[8 + t]).astype(bf).astype(f32)
        z = zs[t]
        dz = da * (cdf[t] + z * (jnp.exp(-0.5 * z * z) * ((2.0 * math.pi) ** -0.5)))
        put(6 + t, down_sum(dz))
        dzb = dz.astype(bf)
        if t >= 2:
            outs[t - 2].wait()
        gs[t % 2] = nn(y1t, dzb).astype(bf)
        cp = pltpu.make_async_copy(gs.at[t % 2], gup.at[t], os.at[t % 2])
        cp.start()
        outs.append(cp)
        dy1 = dy1 + nt(dzb, wv[4 + t])
        if t == 0:
            for part in parts:
                part.first()
    put(2, down_sum(dy1 * xh1))
    put(3, down_sum(dy1))
    d1 = norm_back(dy1, xh1, s1, pv[2])
    dh1[...] = d1
    put(0, down_sum(d1))
    d1b = d1.astype(bf)
    d1t = d1.T.astype(bf)
    for j in range(8):
        dcm[j] = nn(d1b, wo[j]).astype(bf)
    sw = [send(dcm.at[(c + k) % 8], DC.at[c], {"ctx": (c + k) % 8}) for k in range(1, 8)]
    swo = pltpu.make_async_copy(dcm.at[c], DC.at[c], ls.at[2])
    swo.start()
    for t in range(4):
        a, b = nn(d1t, cm[2 * t]), nn(d1t, cm[2 * t + 1])
        go[t] = jnp.concatenate([a[:, :64], a[:, 64:] + b[:, 64:], b[:, :64]], axis=1).astype(bf)
    for part in parts:
        part.gathered(part.c1, part.s1, part.acc, part.r1, 0)
    for cp in los + sw:
        cp.wait_recv()
    for cp in outs[2:] + [swo, loo]:
        cp.wait()
    for cp in send.all:
        cp.wait_send()


def middle(w, cms, xs, cots, vec, cid):
    vm = pltpu.VMEM
    sd = jax.ShapeDtypeStruct
    anywhere, here = pl.BlockSpec(memory_space=pl.ANY), pl.BlockSpec(memory_space=vm)
    left = [shape_of([d for d in "xyz" if d != o[0]]) for o in MID]
    seven = (4, 2, 2, 2, 4, 24)
    return pl.pallas_call(
        mid_kernel,
        out_shape=(
            sd((4, BLK, 768), bf),
            sd((BLK, 768), f32),
            sd((4, 768, 768), bf),
            sd((4, 768, 192), bf),
            sd((8, BLK, 128), bf),
            sd((60, 128), f32),
            sd((*left[0], 24, 384), bf),
            sd((*left[1], 24, 384), bf),
        ),
        in_specs=[anywhere] * 4 + [here],
        out_specs=[anywhere, here, anywhere, here, anywhere, here, here, here],
        scratch_shapes=sum([reducer_scratch(o, 384)[:3] for o in MID], [])
        + [
            vm((8, BLK, 128), bf),
            vm((12, 768, 768), bf),
            vm((8, 768, 128), bf),
            vm((4, BLK, 768), f32),
            vm((4, BLK, 768), f32),
            vm((4, BLK, 768), bf),
            vm((2, 768, 768), bf),
            vm((*seven, 384), bf),
            vm((*seven, 384), bf),
            vm((BLK, 768), bf),
            vm((8, BLK, 128), bf),
            vm((BLK, 768), bf),
            vm((BLK, 768), bf),
            pltpu.SemaphoreType.DMA((40,)),
            pltpu.SemaphoreType.DMA((40,)),
            pltpu.SemaphoreType.DMA((15,)),
            pltpu.SemaphoreType.DMA((2,)),
        ],
        compiler_params=params(cid, MIDMB),
    )(w, cms, xs, cots, vec)


TAIL = ("xyz", "yzx", "zyx")
TAILN = (768, 384, 384)


def tail_kernel(dm, xs, dh1, w, go, gup, vin, n0, n1, R1, R0, R2, V, IG, *refs):
    red, refs = [refs[7 * i : 7 * i + 7] for i in range(3)], refs[21:]
    more, refs = [[None] * 3 + [(n0, n1)[i], *refs[3 * i : 3 * i + 3]] for i in range(2)], refs[6:]
    x, d, wv, ga, gb, igb, acc, vt, vr, ss, rs, ls = refs
    p = Place()
    c = lax.axis_index("ctx")
    core, sib = p.core, p.sib()
    ctx = [{"ctx": (c + k) % 8} for k in range(1, 8)]
    peers = {"x": p.px, "y": p.py, "z": p.pz}
    greet([p.px(k)[0] for k in AXES] + [p.py(k)[0] for k in (1, 3)] + ctx + [sib])
    send = Sender(ss, rs)
    parts = [Reducer(p, send, o, r) for o, r in zip(TAIL, red)]
    parts += [Reducer(p, send, o, r) for o, r in zip(MID, more)]
    parts[0].begin(gup, ls.at[0])
    sw = [send(dm.at[(c + k) % 8], d.at[c], {"ctx": (c + k) % 8}) for k in range(1, 8)]
    swo = pltpu.make_async_copy(dm.at[c], d.at[c], ls.at[1])
    load = pltpu.make_async_copy(w.at[0], wv, ls.at[2])
    swo.start()
    rows = pltpu.make_async_copy(xs.at[p.x], x, ls.at[3])
    rows.start()
    load.start()
    parts[0].first()
    for q in (3, 4):
        parts[q].c2 = parts[q].scatter(parts[q].s1, parts[q].r2, 1)
    rows.wait()
    xt = x[...].astype(f32).T.astype(bf)
    acc[...] = dh1[...]
    swo.wait()
    load.wait()
    for cp in sw:
        cp.wait_recv()
    vt[0, :60] = vin[...]
    for t in range(4):
        a, b = d[2 * t].astype(f32), d[2 * t + 1].astype(f32)
        pre = jnp.concatenate([a[:, :192], a[:, 192:] + b[:, 192:], b[:, :192]], axis=1)
        sums = jnp.concatenate([down_sum(pre), jnp.zeros((1, 64), f32)], axis=1)
        for k in range(5):
            vt[0, 60 + 5 * t + k : 61 + 5 * t + k] = sums[:, 128 * k : 128 * k + 128]
        pre = pre.astype(bf)
        g = jnp.concatenate([nn(xt, pre), go[t].astype(f32)], axis=1)
        store_pieces(g, t, ga, gb)
        parts[1].begin_at(ga, t)
        parts[2].begin_at(gb, t)
        acc[...] += nt(pre, wv[t, :, :576])
    igb[...] = acc[...].astype(bf)
    IG[p.x] = igb[...]
    ig = [send(igb, IG.at[p.x], p.px(k)[0]) for k in AXES]
    cv = send(vt.at[0], vr.at[0, 0], sib)
    parts[1].first()
    parts[2].first()
    cv.wait_recv()
    vt[1] = vt[0] + vr[0, 0]

    def vsend(i, a):
        return [send(vt.at[i], vr.at[i, j - 1], peers[a](j)[0]) for j in AXES]

    def vsum(i, cs):
        for cp in cs:
            cp.wait_recv()
        return vt[i] + vr[i, 0] + vr[i, 1] + vr[i, 2]

    v1 = vsend(1, "z")
    for q in (3, 4):
        parts[q].third()
    parts[0].second()
    vt[2] = vsum(1, v1)
    v2 = vsend(2, "y")
    for q in (1, 2):
        parts[q].second()
    vt[3] = vsum(2, v2)
    v3 = vsend(3, "x")
    for q in (0, 1, 2):
        parts[q].third()
    V[...] = vsum(3, v3)
    for cp in ig:
        cp.wait_recv()
    R1[...] = parts[0].result()
    R2[:, :384] = parts[3].result()
    R2[:, 384:] = parts[4].result()
    R0[:, :384] = parts[1].result()
    R0[:, 384:] = parts[2].result()
    for cp in send.all:
        cp.wait_send()


def finale(dm, xs, dh1, w, go, gup, vin, n0, n1, cid):
    vm = pltpu.VMEM
    sd = jax.ShapeDtypeStruct
    anywhere, here = pl.BlockSpec(memory_space=pl.ANY), pl.BlockSpec(memory_space=vm)
    scratch = sum([reducer_scratch(o, n) for o, n in zip(TAIL, TAILN)], [])
    scratch += sum([reducer_scratch(o, 384)[4:] for o in MID], [])
    seven = (4, 2, 2, 2, 4, 24)
    return pl.pallas_call(
        tail_kernel,
        out_shape=(sd((24, 768), f32), sd((24, 768), f32), sd((24, 768), f32), sd((80, 128), f32), sd((4, BLK, 768), bf)),
        in_specs=[anywhere, anywhere, here, anywhere, here, anywhere, here, here, here],
        out_specs=[here] * 5,
        scratch_shapes=scratch
        + [
            vm((BLK, 768), bf),
            vm((8, BLK, 384), bf),
            vm((4, 768, 768), bf),
            vm((*seven, 384), bf),
            vm((*seven, 384), bf),
            vm((BLK, 768), bf),
            vm((BLK, 768), f32),
            vm((4, 80, 128), f32),
            vm((4, 3, 80, 128), f32),
            pltpu.SemaphoreType.DMA((80,)),
            pltpu.SemaphoreType.DMA((80,)),
            pltpu.SemaphoreType.DMA((4,)),
        ],
        compiler_params=params(cid, TAILMB),
    )(dm, xs, dh1, w, go, gup.reshape(*seven, 768), vin, n0, n1)


def finish_kernel(r1, r0, r2, v, g, R1, PG, OG, R2, PB, UB, B0, B1, B2, B3, B4, B5, IG):
    x, fc = lax.axis_index("tp"), lax.axis_index("fsdp") * 8 + lax.axis_index("ctx")
    IG[...] = g[...].astype(f32)
    R1[...] = r1[...]
    for i, out in enumerate((B0, B1, B2, B3, B4, B5)):
        row = jnp.concatenate([v[6 * i + k : 6 * i + k + 1] for k in range(6)], axis=1)
        row = pltpu.roll(jnp.broadcast_to(row, (8, 768)), (768 - 24 * fc) % 768, 1)
        out[...] = row[:1, :24]
    UB[...] = jnp.concatenate([v[pl.ds(36 + 6 * x + k, 1)] for k in range(6)], axis=1)
    b = jnp.concatenate([v[pl.ds(60 + 5 * x + k, 1)] for k in range(5)], axis=1)
    PB[...] = jnp.concatenate([jnp.concatenate([b[:, head(AT[k, h])] for h in range(3)], axis=1) for k in (0, 2)], axis=0)
    R2[...] = r2[...].T
    p = r0[...]
    for k in range(3):
        PG[k] = jnp.concatenate([p[:, head(AT[k, h])] for h in range(3)], axis=1)
    OG[...] = jnp.concatenate([p[:, head(9 + TURN[h])] for h in range(3)], axis=1).T


def finish(*args):
    sd = jax.ShapeDtypeStruct
    here = pl.BlockSpec(memory_space=pltpu.VMEM)
    shapes = [(24, 768), (3, 24, 192), (192, 24), (768, 24), (2, 192), (1, 768), *[(1, 24)] * 6, (4, BLK, 768)]
    return pl.pallas_call(
        finish_kernel,
        out_shape=tuple(sd(s, f32) for s in shapes),
        in_specs=[here] * 5,
        out_specs=[here] * 13,
        compiler_params=params(mb=24),
    )(*args)


def shards(
    layer_input,
    segment_ids,
    proj_weight,
    proj_bias,
    out_weight,
    out_bias,
    first_gain,
    first_shift,
    up_weight,
    up_bias,
    down_weight,
    down_bias,
    second_gain,
    second_shift,
    cotangent,
):
    tp = lax.axis_index("tp")
    out_t = out_weight.T

    p0 = jnp.concatenate([proj_weight[k, :, head(h)] for k, h in NINE] + [out_t[:, head(h)] for h in TURN], axis=1)
    rows = [out_bias, down_bias, first_gain, first_shift, second_gain, second_shift, proj_bias[0], proj_bias[1]]
    row = lax.broadcasted_iota(jnp.int32, (16, 192), 0)
    vec = jnp.zeros((16, 192), bf)
    for i, v in enumerate(rows + [up_bias[192 * k : 192 * k + 192] for k in range(4)]):
        vec = jnp.where(row == i, v[None], vec)
    seg = lax.dynamic_index_in_dim(segment_ids, tp, 0, keepdims=False).reshape(2, 128)
    w, vec, r, docs = front(p0, up_weight, down_weight.T, vec, layer_input, seg, 1)
    w = w.reshape(3, 4, 768, 768)
    cmsg, acc, qa = attend(docs, r)
    layer_output, dh1, gup, go, dc, sums, n0, n1 = middle(w, cmsg, layer_input, cotangent, vec, 2)
    dmsg = unattend(docs, r, dc, acc, qa)
    done = finale(dmsg, layer_input, dh1, w, go, gup, sums, n0, n1, 3)
    r1, proj, out_grad, r2, pb, ub, b0, b1, b2, b3, b4, b5, input_grad = finish(*done)
    ob, db, g1, s1, g2, s2 = [b.reshape(24) for b in (b0, b1, b2, b3, b4, b5)]
    return (layer_output, input_grad, proj, pb, out_grad, ob, g1, s1, r1, ub.reshape(768), r2, db, g2, s2)


def solution(mesh):
    placed = (
        P("fsdp", "ctx", None),
        P("fsdp", "ctx"),
        P(None, "fsdp", "tp"),
        P(None, "tp"),
        P("tp", "fsdp"),
        P("fsdp"),
        P("fsdp"),
        P("fsdp"),
        P("fsdp", "tp"),
        P("tp"),
        P("tp", "fsdp"),
        P("fsdp"),
        P("fsdp"),
        P("fsdp"),
        P("fsdp", "ctx", None),
    )
    return jax.shard_map(
        shards,
        mesh=mesh,
        in_specs=placed,
        out_specs=(
            P("fsdp", "ctx", None),
            P("fsdp", "ctx", None),
            P(None, ("fsdp", "ctx"), "tp"),
            P(None, "tp"),
            P("tp", ("fsdp", "ctx")),
            P(("fsdp", "ctx")),
            P(("fsdp", "ctx")),
            P(("fsdp", "ctx")),
            P(("fsdp", "ctx"), "tp"),
            P("tp"),
            P("tp", ("fsdp", "ctx")),
            P(("fsdp", "ctx")),
            P(("fsdp", "ctx")),
            P(("fsdp", "ctx")),
        ),
        check_vma=False,
    )
```

```python
import functools
import math

import jax
import jax.numpy as jnp
from jax import lax
from jax.experimental import pallas as pl
from jax.experimental.pallas import tpu as pltpu
from jax.sharding import PartitionSpec as P

HEAD_DIM = 64
NORM_EPS = 1e-12

MESH = pl.DeviceIdType.MESH
bf=jnp.bfloat16; f32=jnp.float32

class Place:
    def __init__(self):
        self.x=lax.axis_index("tp"); f=lax.axis_index("fsdp"); c=lax.axis_index("ctx")
        self.yl=f//2; self.core=f%2; self.yh=c//4; self.z=c%4
        self.y=self.yh*2+self.yl
    def px(self,k):
        q=(self.x+k)%4
        return {"tp":q}, q
    def pz(self,k):
        q=(self.z+k)%4
        return {"ctx":self.yh*4+q}, q
    def py(self,k):
        q=(self.y+k)%4
        return {"fsdp":(q%2)*2+self.core,"ctx":(q//2)*4+self.z}, (q%2,q//2)
    def sib(self):
        return {"fsdp":self.yl*2+1-self.core}

def greet(devs):
    bar=pltpu.get_barrier_semaphore()
    for d in devs: pl.semaphore_signal(bar,inc=1,device_id=d,device_id_type=MESH)
    pl.semaphore_wait(bar,len(devs))

def rcopy(src,dst,ss,rs,dev):
    return pltpu.make_async_remote_copy(src_ref=src,dst_ref=dst,send_sem=ss,recv_sem=rs,device_id=dev,device_id_type=MESH)


DIMS = {"x": (4,), "y": (2, 2), "z": (4,)}
ORDER = ("xyz", "yzx", "zxy")


def shape_of(axes):
    return sum([DIMS[d] for d in "xyz" if d in axes], ())


def split_index(i, shape):
    out = []
    for s in reversed(shape):
        out.insert(0, i % s)
        i = i // s
    return tuple(out)


def pick(ref, axis, q, left):
    at = []
    for d in "xyz":
        if d in left:
            at += list(q if d == "y" else (q,)) if d == axis else [slice(None)] * len(DIMS[d])
    return ref.at[tuple(at)]


def total(dst, first, others, shape):
    outer = shape[: max(0, len(shape) - 2)] if len(shape) != 2 or shape == (4, 4) else ()
    outer = shape[:1] if shape == (4, 4) else outer

    def block(at):
        at = at + (Ellipsis,)
        if len(others) == 1:
            dst[at] = first[at] + others[0][at]
        else:
            a = first[at].astype(f32)
            for o in others:
                a = a + o[at].astype(f32)
            dst[at] = a.astype(dst.dtype)

    if outer:

        @pl.loop(0, math.prod(outer))
        def _(i):
            block(split_index(i, outer))
    else:
        block(())


SQ = HEAD_DIM ** -0.5
FAR = float(2.0 ** 100)
BLK = 256


def nt(a, b):
    return lax.dot_general(a, b, (((1,), (1,)), ((), ())), preferred_element_type=f32)


def nn(a, b):
    return jnp.dot(a, b, preferred_element_type=f32)


def params(cid=None, mb=48):
    return pltpu.CompilerParams(collective_id=cid, has_side_effects=cid is not None, vmem_limit_bytes=mb << 20)


NINE = ((0, 0), (1, 0), (2, 0), (2, 2), (0, 2), (1, 2), (0, 1), (1, 1), (2, 1))
AT = {kh: i for i, kh in enumerate(NINE)}
TURN = (0, 2, 1)
TAILMB, MIDMB, FRONTMB = 48, 50, 60


def head(h):
    return slice(64 * h, 64 * h + 64)


class Sender:
    def __init__(self, ss, rs):
        self.ss, self.rs, self.all = ss, rs, []

    def __call__(self, src, dst, dev):
        i = len(self.all)
        c = rcopy(src, dst, self.ss.at[i], self.rs.at[i], dev)
        c.start()
        self.all.append(c)
        return c


AXES = (1, 2, 3)


class Spread:
    def __init__(self, p, send, own, to, rx, ry, rz):
        self.p, self.send, self.own, self.to = p, send, own, to
        self.rx, self.ry, self.rz = rx, ry, rz
        self.half = ry[0] + pl.multiple_of(p.yh * (ry[1] // 2), 8), ry[1] // 2
        self.quarter = rz[0] + pl.multiple_of(p.z * (rz[1] // 4), 8), rz[1] // 4

    def rows(self, what):
        a, n = what
        return pl.ds(a if isinstance(a, int) else pl.multiple_of(a, 8), n)

    def out(self, t, yl, what):
        return self.to.at[t, yl, self.p.core, self.rows(what)]

    def pass_on(self, t, yl, what, devs):
        return [self.send(self.out(t, yl, what), self.out(t, yl, what), d) for d in devs]

    def start(self):
        p = self.p
        nb = {"fsdp": (1 - p.yl) * 2 + p.core}
        mine = lambda what: self.own.at[self.rows(what)]
        push = lambda what, devs: [self.send(mine(what), self.out(p.x, p.yl, what), d) for d in devs]
        xs = [p.px(k)[0] for k in AXES]
        self.nz = push(self.quarter, [nb])[0] if self.rz[1] else None
        self.nx = push(self.rx, [nb])[0]
        self.xy = push(self.half, xs)
        self.xz = push(self.quarter, xs)
        self.yy = push(self.half, [p.py(k)[0] for k in (1, 3)])

    def second(self):
        p = self.p
        xs = [p.px(k)[0] for k in AXES]
        ys = [p.py(k)[0] for k in AXES]
        zs = [p.pz(k)[0] for k in AXES]
        self.nz.wait_recv()
        self.xz2 = self.pass_on(p.x, 1 - p.yl, self.quarter, xs)
        self.zz = self.pass_on(p.x, 1 - p.yl, self.quarter, zs)
        self.xx = [self.send(self.own.at[self.rows(self.rx)], self.out(p.x, p.yl, self.rx), d) for d in xs]
        self.nx.wait_recv()
        self.xx2 = self.pass_on(p.x, 1 - p.yl, self.rx, xs)
        for k in AXES:
            t = (p.x + 4 - k) % 4
            self.xy[k - 1].wait_recv()
            self.yy += self.pass_on(t, p.yl, self.half, ys)
            self.xz[k - 1].wait_recv()
            self.zz += self.pass_on(t, p.yl, self.quarter, zs)
        for k in AXES:
            t = (p.x + 4 - k) % 4
            self.xz2[k - 1].wait_recv()
            self.zz += self.pass_on(t, 1 - p.yl, self.quarter, zs)

    def finish(self):
        for c in self.yy + self.zz + self.xx + self.xx2:
            c.wait_recv()


def front_kernel(pw, ow, p1, p2, vec, xs, seg, W, V, R, S, po, m, x, p0, ss, rs, ls):
    ot = ow[...].astype(f32).T.astype(bf)
    p0[...] = jnp.concatenate([pw[k, :, head(h)] for k, h in NINE] + [ot[:, head(h)] for h in TURN], axis=1)
    p = Place()
    c = lax.axis_index("ctx")
    core, sib = p.core, p.sib()
    ctx = [{"ctx": (c + k) % 8} for k in range(1, 8)]
    greet([p.px(k)[0] for k in AXES] + [p.py(k)[0] for k in (1, 3)] + ctx + [sib])
    send = Sender(ss, rs)
    own = pltpu.make_async_copy(p0, po.at[p.x, p.yl, core], ls.at[0])
    mine = pltpu.make_async_copy(vec, V.at[p.x, p.yl, core], ls.at[1])
    rows = pltpu.make_async_copy(xs.at[p.x], x, ls.at[2])
    up = pltpu.make_async_copy(p1, W.at[1, p.x, p.yl, core], ls.at[4])
    down = pltpu.make_async_copy(p2, W.at[2, p.x, p.yl, core], ls.at[5])
    for cp in (own, mine, rows, up, down):
        cp.start()
    nb = {"fsdp": (1 - p.yl) * 2 + core}
    first = Spread(p, send, p0, po, (0, 64), (64, 64), (128, 64))
    first.start()
    vn = send(vec, V.at[p.x, p.yl, core], nb)
    vx = [send(vec, V.at[p.x, p.yl, core], p.px(k)[0]) for k in AXES]
    sg = [send(seg, S.at[c], d) for d in ctx]
    sgo = pltpu.make_async_copy(seg, S.at[c], ls.at[3])
    sgo.start()
    d0 = [send(p0, po.at[p.x, p.yl, core], sib)]
    dv = [send(vec, V.at[p.x, p.yl, core], sib)]
    first.second()
    vn.wait_recv()
    vx += [send(V.at[p.x, 1 - p.yl, core], V.at[p.x, 1 - p.yl, core], p.px(k)[0]) for k in AXES]
    bulk = [
        Spread(p, send, p1, W.at[1], (0, 32), (32, 96), (128, 64)),
        Spread(p, send, p2, W.at[2], (0, 64), (64, 96), (160, 32)),
    ]
    for b in bulk:
        b.start()
    first.finish()
    for cp in vx:
        cp.wait_recv()
    own.wait()
    mine.wait()
    d0.append(send(po.at[p.x, 1 - p.yl, core], po.at[p.x, 1 - p.yl, core], sib))
    dv.append(send(V.at[p.x, 1 - p.yl, core], V.at[p.x, 1 - p.yl, core], sib))
    for k in AXES:
        t = (p.x + k) % 4
        d0.append(send(po.at[t, :, core], po.at[t, :, core], sib))
        dv.append(send(V.at[t, :, core], V.at[t, :, core], sib))
    for b in bulk:
        b.second()
    for cp in d0 + dv:
        cp.wait_recv()
    rows.wait()
    back = pltpu.make_async_copy(po, W.at[0], ls.at[0])
    back.start()

    @pl.loop(0, 4)
    def _(t):
        qv = V[t, 0, 0].astype(f32)
        b = [jnp.zeros((1, 64), f32) if k == 1 else qv[6 + k // 2 : 7 + k // 2, head(h)] for k, h in NINE]
        b = jnp.concatenate(b + [jnp.zeros((1, 192), f32)], axis=1)
        r = (nn(x[...], po[t].reshape(768, 768)) + b).astype(bf)
        m[2 * t] = r[:, :384]
        m[2 * t + 1] = jnp.concatenate([r[:, 384:576], r[:, 192:384]], axis=1)

    sw = [send(m.at[(c + k) % 8], R.at[c], {"ctx": (c + k) % 8}) for k in range(1, 8)]
    swo = pltpu.make_async_copy(m.at[c], R.at[c], ls.at[2])
    swo.start()
    for b in bulk:
        b.finish()
    up.wait()
    down.wait()
    dw = []
    for k in range(4):
        t = (p.x + k) % 4
        dw.append(send(W.at[pl.ds(1, 2), t, :, core], W.at[pl.ds(1, 2), t, :, core], sib))
    for cp in sg + sw + dw:
        cp.wait_recv()
    for cp in send.all:
        cp.wait_send()
    for cp in (back, swo, sgo):
        cp.wait()


def front(pw, ow, p1, p2, vec, xs, seg, cid):
    sd = jax.ShapeDtypeStruct
    vm = pltpu.VMEM
    anywhere, here = pl.BlockSpec(memory_space=pl.ANY), pl.BlockSpec(memory_space=vm)
    count = 192
    return pl.pallas_call(
        front_kernel,
        out_shape=(
            sd((3, 4, 2, 2, 192, 768), bf),
            sd((4, 2, 2, 16, 192), bf),
            sd((8, BLK, 384), bf),
            sd((8, 2, 128), jnp.int32),
        ),
        in_specs=[here] * 4 + [anywhere] * 3,
        out_specs=[anywhere, here, anywhere, anywhere],
        scratch_shapes=[
            vm((4, 2, 2, 192, 768), bf),
            vm((8, BLK, 384), bf),
            vm((BLK, 768), bf),
            vm((192, 768), bf),
            pltpu.SemaphoreType.DMA((count,)),
            pltpu.SemaphoreType.DMA((count,)),
            pltpu.SemaphoreType.DMA((6,)),
        ],
        compiler_params=params(cid, FRONTMB),
    )(pw, ow, p1, p2, vec, xs, seg)


LONG = 2048 + BLK
SAFE = 120.0 / SQ
FWD = 8
BWD = 4


def blocks(edge, lst, par, unit):
    n = jnp.int32(0)
    for h in range(2):
        for i in range(8 if h == 0 else 4):
            qi = i if h == 0 else 2 * i + par
            lo, hi = jnp.int32(0), jnp.int32(0)
            for j in range(8):
                lo = lo + (edge[j, 1, 127] < edge[qi, 0, 0]).astype(jnp.int32)
                hi = hi + (edge[j, 0, 0] <= edge[qi, 1, 127]).astype(jnp.int32)

            def put(j, n):
                lst[n] = (h * 8 + qi) * 16 + j
                return n + 1

            n = lax.fori_loop(lo, hi, put, n)
    for k in range(unit - 1):
        lst[n + k] = 8
    return (n + unit - 1) // unit


def triple(code):
    j = code % 16
    i = (code // 16) % 8
    return code // 128, pl.ds(pl.multiple_of(i * BLK, BLK), BLK), pl.ds(pl.multiple_of(j * BLK, BLK), BLK), i


def lanes():
    return lax.broadcasted_iota(jnp.int32, (1, 128), 1)


def three(v, at, lane):
    a = v.astype(bf).astype(f32)
    b = (v - a).astype(bf).astype(f32)
    c = v - a - b
    return jnp.where(lane == at, a, jnp.where(lane == at + 1, b, jnp.where(lane == at + 2, c, 0.0))).astype(bf)


def flat(r, k):
    return r[:, :, 128 * k : 128 * k + 128].reshape(2048, 128)


def turned(v):
    return v.astype(f32).T.astype(bf)


def one_lane(h, lane):
    return lane == (72 if h == 0 else 8)


def doc_rows(docs):
    seg = jnp.concatenate([docs[j, i : i + 1] for j in range(8) for i in range(2)] + [jnp.full((1, BLK), -1)], axis=1)
    row = lax.broadcasted_iota(jnp.int32, (64, 1), 0)
    return seg, jnp.where(((row < 4) & (row != seg)) | ((row >= 8) & (row < 11)), 1.0, 0.0)


def attend_kernel(edge, docs, r, msg, acc, qa, kt, va, top, lst):
    par = lax.axis_index("ctx") % 2
    lane = lanes()
    count = blocks(edge, lst, par, FWD)
    seg, augk = doc_rows(docs)
    row = lax.broadcasted_iota(jnp.int32, (128, 1), 0) - 64
    augq = jnp.where(row == seg[:, :2048], -FAR, 0.0).T.astype(bf)
    augk = augk.astype(bf)
    vv = flat(r, 1)
    safe = jnp.bool_(True)
    for h in range(2):
        qk = flat(r, 2 * h)
        qa[h] = jnp.where(lane < 64, qk * bf(SQ), augq)
        kt[h, :64, :2048] = turned(qk)[64:]
        kt[h, :64, 2048:] = jnp.zeros((64, BLK), bf)
        kt[h, 64:] = augk
        va[h, :2048] = jnp.where((lane < 64) if h == 0 else (lane >= 64), vv, one_lane(h, lane).astype(bf))
        va[h, 2048:] = jnp.zeros((BLK, 128), bf)
        f = qk.astype(f32)
        safe = safe & (jnp.max(jnp.sum(f * f, axis=1, keepdims=True)) < SAFE)
    acc[...] = jnp.zeros_like(acc)

    @pl.when(jnp.logical_not(safe))
    def _():
        top[...] = jnp.full_like(top, -3e38)

        @pl.loop(0, count * FWD)
        def _(n):
            h, at, to, i = triple(lst[n])
            s = jnp.max(nn(qa[h, at], kt[h, :, to]), axis=1, keepdims=True)
            top[h, at] = jnp.maximum(top[h, at], s)

        for h in range(2):
            for i in range(8):
                at = slice(i * BLK, i * BLK + BLK)
                qa[h, at] = qa[h, at] + three(-top[h, at, :1], 72, lane)

    @pl.loop(0, count)
    def _(n):
        tr = [triple(lst[n * FWD + u]) for u in range(FWD)]
        ps = [nn(qa[h, at], kt[h, :, to]) for h, at, to, _ in tr]
        ps = [jnp.exp(p).astype(bf) for p in ps]
        got = [(h, at, nn(p, va[h, to])) for p, (h, at, to, _) in zip(ps, tr)]
        for h, at, o in got:
            acc[h, at] += o

    for i in range(8):
        at = slice(i * BLK, i * BLK + BLK)
        a = acc[0, at] * (1.0 / acc[0, at, 72:73])
        b = acc[1, at] * (1.0 / acc[1, at, 8:9])
        b = jnp.where(par == i % 2, b, 0.0)
        msg[i] = jnp.where(lane < 64, a, b).astype(bf)


def attend(docs, r):
    vm = pltpu.VMEM
    sd = jax.ShapeDtypeStruct
    return pl.pallas_call(
        attend_kernel,
        out_shape=(sd((8, BLK, 128), bf), sd((2, 2048, 128), f32), sd((2, 2048, 128), bf)),
        in_specs=[pl.BlockSpec(memory_space=pltpu.SMEM)] + [pl.BlockSpec(memory_space=vm)] * 2,
        out_specs=[pl.BlockSpec(memory_space=vm)] * 3,
        scratch_shapes=[
            vm((2, 128, LONG), bf),
            vm((2, LONG, 128), bf),
            vm((2, 2048, 128), f32),
            pltpu.SMEM((128,), jnp.int32),
        ],
        compiler_params=params(),
    )(docs, docs, r)


def unattend_kernel(edge, docs, r, dc, acc, qa, out, ka, va, kt, ga, gz, qz, dkv, dqt, lst):
    par = lax.axis_index("ctx") % 2
    lane = lanes()
    count = blocks(edge, lst, par, BWD)
    vv, gg = flat(r, 1), flat(dc, 0)
    tops = doc_rows(docs)[1].T.astype(bf)
    for h in range(2):
        qk = flat(r, 2 * h)
        low = (lane < 64) if h == 0 else (lane >= 64)
        at = 72 if h == 0 else 8
        kt[h, :, :2048] = turned(qk)[64:]
        kt[h, :, 2048:] = jnp.zeros((64, BLK), bf)
        ka[h, :2048] = jnp.concatenate([qk[:, 64:], tops[:2048]], axis=1)
        ka[h, 2048:] = jnp.concatenate([jnp.zeros((BLK, 64), bf), tops[2048:]], axis=1)
        ones = ((lane >= at) & (lane < at + 3)).astype(bf)
        va[h, :2048] = jnp.where(low, vv, ones)
        va[h, 2048:] = jnp.zeros((BLK, 128), bf)
        inv = 1.0 / acc[h, :, at : at + 1]
        g = jnp.where(low, gg.astype(f32), 0.0)
        g = (g * inv).astype(bf)
        delta = jnp.sum(g.astype(f32) * acc[h], axis=1, keepdims=True) * inv
        gz[h] = g
        ga[h] = g + three(-delta, at, lane)
        q = jnp.where(lane < 64, qa[h], bf(0))
        qz[h] = pltpu.roll(q.astype(f32), 64, 1).astype(bf) if h == 0 else q
    dqt[...] = jnp.zeros_like(dqt)
    dkv[...] = jnp.zeros_like(dkv)

    @pl.loop(0, count)
    def _(n):
        tr = [triple(lst[n * BWD + u]) for u in range(BWD)]
        ps = [nt(ka[h, to], qa[h, at]) for h, at, to, _ in tr]
        dp = [nt(va[h, to], ga[h, at]) for h, at, to, _ in tr]
        ps = [jnp.exp(p) for p in ps]
        ds = [(p * d).astype(bf) for p, d in zip(ps, dp)]
        ps = [p.astype(bf) for p in ps]
        kv = [nn(p, gz[h, at]) + nn(d, qz[h, at]) for p, d, (h, at, to, _) in zip(ps, ds, tr)]
        dq = [nn(kt[h, :, to], d) for d, (h, at, to, _) in zip(ds, tr)]
        got = [(h, at, to, a, b) for a, b, (h, at, to, _) in zip(kv, dq, tr)]
        for h, at, to, kv, dq in got:
            dkv[h, to] += kv
            dqt[h, :, at] += dq

    for i in range(8):
        a = slice(i * BLK, i * BLK + BLK)
        q0, q1 = [jnp.concatenate([(dqt[h, :, a] * SQ).T] * 2, axis=1) for h in range(2)]
        q1 = jnp.where(par == i % 2, q1, 0.0)
        kv0, kv1 = dkv[0, a], dkv[1, a]
        out[i, :, :128] = jnp.where(lane < 64, q0, kv0).astype(bf)
        out[i, :, 128:256] = jnp.where(lane < 64, kv0, kv1).astype(bf)
        out[i, :, 256:] = jnp.where(lane < 64, q1, pltpu.roll(kv1, 64, 1)).astype(bf)


def unattend(docs, r, dc, acc, qa):
    vm = pltpu.VMEM
    return pl.pallas_call(
        unattend_kernel,
        out_shape=jax.ShapeDtypeStruct((8, BLK, 384), bf),
        in_specs=[pl.BlockSpec(memory_space=pltpu.SMEM)] + [pl.BlockSpec(memory_space=vm)] * 5,
        out_specs=pl.BlockSpec(memory_space=vm),
        scratch_shapes=[
            vm((2, LONG, 128), bf),
            vm((2, LONG, 128), bf),
            vm((2, 64, LONG), bf),
            vm((2, 2048, 128), bf),
            vm((2, 2048, 128), bf),
            vm((2, 2048, 128), bf),
            vm((2, LONG, 128), f32),
            vm((2, 64, 2048), f32),
            pltpu.SMEM((128,), jnp.int32),
        ],
        compiler_params=params(),
    )(docs, docs, r, dc, acc, qa)


class Reducer:
    def __init__(self, p, send, order, refs):
        self.p, self.send, self.order = p, send, order
        self.acc, self.cor, self.r1, self.s1, self.r2, self.s2, self.r3 = refs
        self.peers = {"x": p.px, "y": p.py, "z": p.pz}
        self.here = {"x": p.x, "y": (p.yl, p.yh), "z": p.z}
        self.left = [[d for d in "xyz" if d not in order[:n]] for n in range(3)]

    def begin(self, src, sem):
        self.c0 = [self.send(src.at[:, :, 1 - self.p.core], self.cor, self.p.sib())]
        self.own = pltpu.make_async_copy(src.at[:, :, self.p.core], self.acc, sem)
        self.own.start()
        self.mine = self.acc

    def begin_at(self, src, t):
        self.c0 = ([] if t == 0 else self.c0) + [self.send(src.at[t, :, 1 - self.p.core], self.cor.at[t], self.p.sib())]
        self.own, self.mine = None, src.at[:, :, self.p.core]

    def scatter(self, src, into, n):
        a = self.order[n]
        return [
            self.send(pick(src, a, self.peers[a](j)[1], self.left[n]), into.at[j - 1], self.peers[a](j)[0]) for j in AXES
        ]

    def first(self):
        for c in self.c0:
            c.wait_recv()
        if self.own is not None:
            self.own.wait()
        total(self.acc, self.mine, [self.cor], shape_of("xyz"))
        self.c1 = self.scatter(self.acc, self.r1, 0)

    def gathered(self, copies, out, src, got, n):
        for c in copies:
            c.wait_recv()
        a = self.order[n]
        total(out, pick(src, a, self.here[a], self.left[n]), [got.at[j] for j in range(3)], shape_of(self.left[n + 1]))

    def second(self):
        self.gathered(self.c1, self.s1, self.acc, self.r1, 0)
        self.c2 = self.scatter(self.s1, self.r2, 1)

    def third(self):
        self.gathered(self.c2, self.s2, self.s1, self.r2, 1)
        self.c3 = self.scatter(self.s2, self.r3, 2)

    def result(self):
        for c in self.c3:
            c.wait_recv()
        a = self.order[2]
        m = pick(self.s2, a, self.here[a], self.left[2])[...].astype(f32)
        for j in range(3):
            m = m + self.r3[j].astype(f32)
        return m


def reducer_scratch(order, n):
    vm = pltpu.VMEM
    one, two = shape_of([d for d in "xyz" if d != order[0]]), shape_of(order[2])
    whole = (*shape_of("xyz"), 24, n)
    shapes = [whole, whole, (3, *one, 24, n), (*one, 24, n), (3, *two, 24, n), (*two, 24, n), (3, 24, n)]
    return [vm(s, bf) for s in shapes]


MID = ("yzx", "zyx", "xyz")
MIDN = 256


def norm_of(v):
    d = v - jnp.mean(v, axis=-1, keepdims=True)
    s = lax.rsqrt(jnp.mean(d * d, axis=-1, keepdims=True) + NORM_EPS)
    return d * s, s


def norm_back(g, xhat, s, gain):
    e = g * gain
    return s * (e - jnp.mean(e, axis=-1, keepdims=True) - xhat * jnp.mean(e * xhat, axis=-1, keepdims=True))


def down_sum(v):
    return jnp.sum(v, axis=0, keepdims=True)


def store_pieces(g, t, outs):
    n = 768 // len(outs)
    for i in range(32):
        at = (t, i // 16, i // 8 % 2, i // 4 % 2, i % 4)
        piece = g[24 * i : 24 * i + 24].astype(bf)
        for k, out in enumerate(outs):
            out[at] = piece[:, n * k : n * k + n]


def mid_kernel(w, cms, xs, cots, vec, LO, dh1, gup, go, DC, sums, o0, o1, o2, *refs):
    red = [[*refs[3 * i : 3 * i + 3], (o0, o1, o2)[i], None, None, None] for i in range(3)]
    refs = refs[9:]
    cm, wv, wo, zs, cdf, act, gs, ga, gb, gc, lob, dcm, x, cot, ss, rs, ls, os = refs
    p = Place()
    c = lax.axis_index("ctx")
    ctx = [{"ctx": (c + k) % 8} for k in range(1, 8)]
    greet([p.px(k)[0] for k in AXES] + [p.py(k)[0] for k in (1, 3)] + ctx + [p.sib()])
    send = Sender(ss, rs)

    def put(i, row):
        for k in range(6):
            sums[6 * i + k : 6 * i + k + 1] = row[:, 128 * k : 128 * k + 128]

    sw = [send(cms.at[(c + k) % 8], cm.at[c], {"ctx": (c + k) % 8}) for k in range(1, 8)]
    swo = pltpu.make_async_copy(cms.at[c], cm.at[c], ls.at[12])
    swo.start()
    ins = [pltpu.make_async_copy(a.at[p.x], b, ls.at[n]) for a, b, n in ((xs, x, 13), (cots, cot, 14))]
    loads = []
    for k in range(3):
        for t in range(4):
            cp = pltpu.make_async_copy(w.at[k, t], wv.at[k * 4 + t], ls.at[k * 4 + t])
            cp.start()
            loads.append(cp)
    for cp in ins:
        cp.start()
    fours = [vec[0, f // 2, f % 2].astype(f32) for f in range(4)]
    pv = [jnp.concatenate([f[i : i + 1] for f in fours], axis=1) for i in range(6)]
    for t in range(4):
        loads[t].wait()
        o = wv[t, :, 576:768]
        wo[2 * t] = o[:, :128]
        wo[2 * t + 1] = jnp.concatenate([o[:, 128:], o[:, 64:128]], axis=1)
    swo.wait()
    for cp in ins:
        cp.wait()
    for cp in sw:
        cp.wait_recv()
    attn = jnp.zeros((BLK, 768), f32)
    for j in range(8):
        attn = attn + nt(cm[j], wo[j])
    h1 = x[...].astype(f32) + attn + pv[0]
    xh1, s1 = norm_of(h1)
    y1 = xh1 * pv[2] + pv[3]
    y1b = y1.astype(bf)
    ffn = jnp.zeros((BLK, 768), f32)
    for t in range(4):
        loads[4 + t].wait()
        z = nn(y1b, wv[4 + t]) + jnp.concatenate([vec[t, 0, 0, 8 + k : 9 + k].astype(f32) for k in range(4)], axis=1)
        e = 0.5 * (1.0 + lax.erf(z * (2.0**-0.5)))
        zs[t] = z
        cdf[t] = e
        a = (z * e).astype(bf)
        act[t] = a
        loads[8 + t].wait()
        ffn = ffn + nt(a, wv[8 + t])
    xh2, s2 = norm_of(y1 + ffn + pv[1])
    lob[...] = (xh2 * pv[4] + pv[5]).astype(bf)
    los = [send(lob, LO.at[p.x], p.px(k)[0]) for k in AXES]
    loo = pltpu.make_async_copy(lob, LO.at[p.x], ls.at[12])
    loo.start()
    g = cot[...].astype(f32)
    put(4, down_sum(g * xh2))
    put(5, down_sum(g))
    dh2 = norm_back(g, xh2, s2, pv[4])
    put(1, down_sum(dh2))
    dh2b = dh2.astype(bf)
    dh2t = dh2.T.astype(bf)
    y1t = y1.T.astype(bf)
    parts = [Reducer(p, send, o, r) for o, r in zip(MID, red)]
    for t in range(4):
        store_pieces(nn(dh2t, act[t]), t, (ga, gb, gc))
        for part, g3 in zip(parts, (ga, gb, gc)):
            part.begin_at(g3, t)
    dy1 = dh2
    outs = []
    for t in range(4):
        da = nn(dh2b, wv[8 + t]).astype(bf).astype(f32)
        z = zs[t]
        dz = da * (cdf[t] + z * (jnp.exp(-0.5 * z * z) * ((2.0 * math.pi) ** -0.5)))
        put(6 + t, down_sum(dz))
        dzb = dz.astype(bf)
        if t >= 2:
            outs[t - 2].wait()
        gs[t % 2] = nn(y1t, dzb).astype(bf)
        cp = pltpu.make_async_copy(gs.at[t % 2], gup.at[t], os.at[t % 2])
        cp.start()
        outs.append(cp)
        dy1 = dy1 + nt(dzb, wv[4 + t])
        if t == 0:
            for part in parts:
                part.first()
    put(2, down_sum(dy1 * xh1))
    put(3, down_sum(dy1))
    d1 = norm_back(dy1, xh1, s1, pv[2])
    dh1[...] = d1
    put(0, down_sum(d1))
    d1b = d1.astype(bf)
    d1t = d1.T.astype(bf)
    for j in range(8):
        dcm[j] = nn(d1b, wo[j]).astype(bf)
    sw = [send(dcm.at[(c + k) % 8], DC.at[c], {"ctx": (c + k) % 8}) for k in range(1, 8)]
    swo = pltpu.make_async_copy(dcm.at[c], DC.at[c], ls.at[2])
    swo.start()
    for t in range(4):
        a, b = nn(d1t, cm[2 * t]), nn(d1t, cm[2 * t + 1])
        go[t] = jnp.concatenate([a[:, :64], a[:, 64:] + b[:, 64:], b[:, :64]], axis=1).astype(bf)
    for part in parts:
        part.gathered(part.c1, part.s1, part.acc, part.r1, 0)
    for cp in los + sw:
        cp.wait_recv()
    for cp in outs[2:] + [swo, loo]:
        cp.wait()
    for cp in send.all:
        cp.wait_send()


def middle(w, cms, xs, cots, vec, cid):
    vm = pltpu.VMEM
    sd = jax.ShapeDtypeStruct
    anywhere, here = pl.BlockSpec(memory_space=pl.ANY), pl.BlockSpec(memory_space=vm)
    left = [shape_of([d for d in "xyz" if d != o[0]]) for o in MID]
    seven = (4, 2, 2, 2, 4, 24)
    return pl.pallas_call(
        mid_kernel,
        out_shape=(
            sd((4, BLK, 768), bf),
            sd((BLK, 768), f32),
            sd((4, 768, 768), bf),
            sd((4, 768, 192), bf),
            sd((8, BLK, 128), bf),
            sd((60, 128), f32),
            *[sd((*s, 24, MIDN), bf) for s in left],
        ),
        in_specs=[anywhere] * 4 + [here],
        out_specs=[anywhere, here, anywhere, here, anywhere, here, here, here, here],
        scratch_shapes=sum([reducer_scratch(o, MIDN)[:3] for o in MID], [])
        + [
            vm((8, BLK, 128), bf),
            vm((12, 768, 768), bf),
            vm((8, 768, 128), bf),
            vm((4, BLK, 768), f32),
            vm((4, BLK, 768), f32),
            vm((4, BLK, 768), bf),
            vm((2, 768, 768), bf),
            vm((*seven, MIDN), bf),
            vm((*seven, MIDN), bf),
            vm((*seven, MIDN), bf),
            vm((BLK, 768), bf),
            vm((8, BLK, 128), bf),
            vm((BLK, 768), bf),
            vm((BLK, 768), bf),
            pltpu.SemaphoreType.DMA((48,)),
            pltpu.SemaphoreType.DMA((48,)),
            pltpu.SemaphoreType.DMA((15,)),
            pltpu.SemaphoreType.DMA((2,)),
        ],
        compiler_params=params(cid, MIDMB),
    )(w, cms, xs, cots, vec)


TAIL = ("xyz", "yzx", "zyx")
TAILN = (768, 384, 384)


def tail_kernel(dm, xs, dh1, w, go, gup, vin, n0, n1, n2, R1, R0, R2, V, IG, *refs):
    red, refs = [refs[7 * i : 7 * i + 7] for i in range(3)], refs[21:]
    more, refs = [[None] * 3 + [(n0, n1, n2)[i], *refs[3 * i : 3 * i + 3]] for i in range(3)], refs[9:]
    x, d, wv, ga, gb, igb, acc, vt, vr, ss, rs, ls = refs
    p = Place()
    c = lax.axis_index("ctx")
    core, sib = p.core, p.sib()
    ctx = [{"ctx": (c + k) % 8} for k in range(1, 8)]
    peers = {"x": p.px, "y": p.py, "z": p.pz}
    greet([p.px(k)[0] for k in AXES] + [p.py(k)[0] for k in (1, 3)] + ctx + [sib])
    send = Sender(ss, rs)
    parts = [Reducer(p, send, o, r) for o, r in zip(TAIL, red)]
    parts += [Reducer(p, send, o, r) for o, r in zip(MID, more)]
    parts[0].begin(gup, ls.at[0])
    sw = [send(dm.at[(c + k) % 8], d.at[c], {"ctx": (c + k) % 8}) for k in range(1, 8)]
    swo = pltpu.make_async_copy(dm.at[c], d.at[c], ls.at[1])
    load = pltpu.make_async_copy(w.at[0], wv, ls.at[2])
    swo.start()
    rows = pltpu.make_async_copy(xs.at[p.x], x, ls.at[3])
    rows.start()
    load.start()
    parts[0].first()
    rows.wait()
    xt = x[...].astype(f32).T.astype(bf)
    acc[...] = dh1[...]
    swo.wait()
    load.wait()
    for cp in sw:
        cp.wait_recv()
    for q in (3, 4, 5):
        parts[q].c2 = parts[q].scatter(parts[q].s1, parts[q].r2, 1)
    vt[0, :60] = vin[...]
    for t in range(4):
        a, b = d[2 * t].astype(f32), d[2 * t + 1].astype(f32)
        pre = jnp.concatenate([a[:, :192], a[:, 192:] + b[:, 192:], b[:, :192]], axis=1)
        sums = jnp.concatenate([down_sum(pre), jnp.zeros((1, 64), f32)], axis=1)
        for k in range(5):
            vt[0, 60 + 5 * t + k : 61 + 5 * t + k] = sums[:, 128 * k : 128 * k + 128]
        pre = pre.astype(bf)
        g = jnp.concatenate([nn(xt, pre), go[t].astype(f32)], axis=1)
        store_pieces(g, t, (ga, gb))
        parts[1].begin_at(ga, t)
        parts[2].begin_at(gb, t)
        acc[...] += nt(pre, wv[t, :, :576])
    igb[...] = acc[...].astype(bf)
    IG[p.x] = igb[...]
    ig = [send(igb, IG.at[p.x], p.px(k)[0]) for k in AXES]
    cv = send(vt.at[0], vr.at[0, 0], sib)
    parts[1].first()
    parts[2].first()
    cv.wait_recv()
    vt[1] = vt[0] + vr[0, 0]

    def vsend(i, a):
        return [send(vt.at[i], vr.at[i, j - 1], peers[a](j)[0]) for j in AXES]

    def vsum(i, cs):
        for cp in cs:
            cp.wait_recv()
        return vt[i] + vr[i, 0] + vr[i, 1] + vr[i, 2]

    v1 = vsend(1, "z")
    for q in (3, 4, 5):
        parts[q].third()
    parts[0].second()
    vt[2] = vsum(1, v1)
    v2 = vsend(2, "y")
    for q in (1, 2):
        parts[q].second()
    vt[3] = vsum(2, v2)
    v3 = vsend(3, "x")
    for q in (0, 1, 2):
        parts[q].third()
    V[...] = vsum(3, v3)
    for cp in ig:
        cp.wait_recv()
    R1[...] = parts[0].result()
    for q in range(3):
        R2[:, MIDN * q : MIDN * q + MIDN] = parts[3 + q].result()
    R0[:, :384] = parts[1].result()
    R0[:, 384:] = parts[2].result()
    for cp in send.all:
        cp.wait_send()


def finale(dm, xs, dh1, w, go, gup, vin, n0, n1, n2, cid):
    vm = pltpu.VMEM
    sd = jax.ShapeDtypeStruct
    anywhere, here = pl.BlockSpec(memory_space=pl.ANY), pl.BlockSpec(memory_space=vm)
    scratch = sum([reducer_scratch(o, n) for o, n in zip(TAIL, TAILN)], [])
    scratch += sum([reducer_scratch(o, MIDN)[4:] for o in MID], [])
    seven = (4, 2, 2, 2, 4, 24)
    return pl.pallas_call(
        tail_kernel,
        out_shape=(sd((24, 768), f32), sd((24, 768), f32), sd((24, 768), f32), sd((80, 128), f32), sd((4, BLK, 768), bf)),
        in_specs=[anywhere, anywhere, here, anywhere, here, anywhere, here, here, here, here],
        out_specs=[here] * 5,
        scratch_shapes=scratch
        + [
            vm((BLK, 768), bf),
            vm((8, BLK, 384), bf),
            vm((4, 768, 768), bf),
            vm((*seven, 384), bf),
            vm((*seven, 384), bf),
            vm((BLK, 768), bf),
            vm((BLK, 768), f32),
            vm((4, 80, 128), f32),
            vm((4, 3, 80, 128), f32),
            pltpu.SemaphoreType.DMA((96,)),
            pltpu.SemaphoreType.DMA((96,)),
            pltpu.SemaphoreType.DMA((5,)),
        ],
        compiler_params=params(cid, TAILMB),
    )(dm, xs, dh1, w, go, gup.reshape(*seven, 768), vin, n0, n1, n2)


def finish_kernel(r1, r0, r2, v, g, R1, PG, OG, R2, PB, UB, B0, B1, B2, B3, B4, B5, IG):
    x, fc = lax.axis_index("tp"), lax.axis_index("fsdp") * 8 + lax.axis_index("ctx")
    IG[...] = g[...].astype(f32)
    R1[...] = r1[...]
    for i, out in enumerate((B0, B1, B2, B3, B4, B5)):
        row = jnp.concatenate([v[6 * i + k : 6 * i + k + 1] for k in range(6)], axis=1)
        row = pltpu.roll(jnp.broadcast_to(row, (8, 768)), (768 - 24 * fc) % 768, 1)
        out[...] = row[:1, :24]
    for k in range(6):
        UB[k : k + 1] = v[pl.ds(36 + 6 * x + k, 1)]
    b = jnp.concatenate([v[pl.ds(60 + 5 * x + k, 1)] for k in range(5)], axis=1)
    PB[...] = jnp.concatenate([jnp.concatenate([b[:, head(AT[k, h])] for h in range(3)], axis=1) for k in (0, 2)], axis=0)
    R2[...] = r2[...]
    p = r0[...]
    for k in range(3):
        PG[k] = jnp.concatenate([p[:, head(AT[k, h])] for h in range(3)], axis=1)
    OG[...] = jnp.concatenate([p[:, head(9 + TURN[h])] for h in range(3)], axis=1)


def finish(*args):
    sd = jax.ShapeDtypeStruct
    here = pl.BlockSpec(memory_space=pltpu.VMEM)
    shapes = [(24, 768), (3, 24, 192), (24, 192), (24, 768), (2, 192), (6, 128), *[(1, 24)] * 6, (4, BLK, 768)]
    return pl.pallas_call(
        finish_kernel,
        out_shape=tuple(sd(s, f32) for s in shapes),
        in_specs=[here] * 5,
        out_specs=[here] * 13,
        compiler_params=params(mb=24),
    )(*args)


def shards(
    layer_input,
    segment_ids,
    proj_weight,
    proj_bias,
    out_weight,
    out_bias,
    first_gain,
    first_shift,
    up_weight,
    up_bias,
    down_weight,
    down_bias,
    second_gain,
    second_shift,
    cotangent,
):
    tp = lax.axis_index("tp")
    rows = [out_bias, down_bias, first_gain, first_shift, second_gain, second_shift, proj_bias[0], proj_bias[1]]
    row = lax.broadcasted_iota(jnp.int32, (16, 192), 0)
    vec = jnp.zeros((16, 192), bf)
    for i, v in enumerate(rows + [up_bias[192 * k : 192 * k + 192] for k in range(4)]):
        vec = jnp.where(row == i, v[None], vec)
    seg = lax.dynamic_index_in_dim(segment_ids, tp, 0, keepdims=False).reshape(2, 128)
    w, vec, r, docs = front(proj_weight, out_weight, up_weight, down_weight.T, vec, layer_input, seg, 1)
    w = w.reshape(3, 4, 768, 768)
    cmsg, acc, qa = attend(docs, r)
    layer_output, dh1, gup, go, dc, sums, *firsts = middle(w, cmsg, layer_input, cotangent, vec, 2)
    dmsg = unattend(docs, r, dc, acc, qa)
    done = finale(dmsg, layer_input, dh1, w, go, gup, sums, *firsts, 3)
    r1, proj, out_grad, r2, pb, ub, b0, b1, b2, b3, b4, b5, input_grad = finish(*done)
    ob, db, g1, s1, g2, s2 = [b.reshape(24) for b in (b0, b1, b2, b3, b4, b5)]
    return (layer_output, input_grad, proj, pb, out_grad.T, ob, g1, s1, r1, ub.reshape(768), r2.T, db, g2, s2)


def solution(mesh):
    placed = (
        P("fsdp", "ctx", None),
        P("fsdp", "ctx"),
        P(None, "fsdp", "tp"),
        P(None, "tp"),
        P("tp", "fsdp"),
        P("fsdp"),
        P("fsdp"),
        P("fsdp"),
        P("fsdp", "tp"),
        P("tp"),
        P("tp", "fsdp"),
        P("fsdp"),
        P("fsdp"),
        P("fsdp"),
        P("fsdp", "ctx", None),
    )
    return jax.shard_map(
        shards,
        mesh=mesh,
        in_specs=placed,
        out_specs=(
            P("fsdp", "ctx", None),
            P("fsdp", "ctx", None),
            P(None, ("fsdp", "ctx"), "tp"),
            P(None, "tp"),
            P("tp", ("fsdp", "ctx")),
            P(("fsdp", "ctx")),
            P(("fsdp", "ctx")),
            P(("fsdp", "ctx")),
            P(("fsdp", "ctx"), "tp"),
            P("tp"),
            P("tp", ("fsdp", "ctx")),
            P(("fsdp", "ctx")),
            P(("fsdp", "ctx")),
            P(("fsdp", "ctx")),
        ),
        check_vma=False,
    )
```

```python
import functools
import math

import jax
import jax.numpy as jnp
from jax import lax
from jax.experimental import pallas as pl
from jax.experimental.pallas import tpu as pltpu
from jax.sharding import PartitionSpec as P

HEAD_DIM = 64
NORM_EPS = 1e-12

MESH = pl.DeviceIdType.MESH
bf=jnp.bfloat16; f32=jnp.float32

class Place:
    def __init__(self):
        self.x=lax.axis_index("tp"); f=lax.axis_index("fsdp"); c=lax.axis_index("ctx")
        self.yl=f//2; self.core=f%2; self.yh=c//4; self.z=c%4
        self.y=self.yh*2+self.yl
    def px(self,k):
        q=(self.x+k)%4
        return {"tp":q}, q
    def pz(self,k):
        q=(self.z+k)%4
        return {"ctx":self.yh*4+q}, q
    def py(self,k):
        q=(self.y+k)%4
        return {"fsdp":(q%2)*2+self.core,"ctx":(q//2)*4+self.z}, (q%2,q//2)
    def sib(self):
        return {"fsdp":self.yl*2+1-self.core}

def others(p):
    steps = ((1, 2), (1, 1), (1, 3), (1, 0), (0, 2), (0, 1), (0, 3))
    return [((p.yh + a) % 2) * 4 + (p.z + b) % 4 for a, b in steps]


def greet(devs, work=None):
    bar=pltpu.get_barrier_semaphore()
    for d in devs: pl.semaphore_signal(bar,inc=1,device_id=d,device_id_type=MESH)
    if work is not None:
        work()
    pl.semaphore_wait(bar,len(devs))

def rcopy(src,dst,ss,rs,dev):
    return pltpu.make_async_remote_copy(src_ref=src,dst_ref=dst,send_sem=ss,recv_sem=rs,device_id=dev,device_id_type=MESH)


DIMS = {"x": (4,), "y": (2, 2), "z": (4,)}
ORDER = ("xyz", "yzx", "zxy")


def shape_of(axes):
    return sum([DIMS[d] for d in "xyz" if d in axes], ())


def split_index(i, shape):
    out = []
    for s in reversed(shape):
        out.insert(0, i % s)
        i = i // s
    return tuple(out)


def pick(ref, axis, q, left):
    at = []
    for d in "xyz":
        if d in left:
            at += list(q if d == "y" else (q,)) if d == axis else [slice(None)] * len(DIMS[d])
    return ref.at[tuple(at)]


def total(dst, first, others, shape):
    outer = shape[: max(0, len(shape) - 2)] if len(shape) != 2 or shape == (4, 4) else ()
    outer = shape[:1] if shape == (4, 4) else outer

    def block(at):
        at = at + (Ellipsis,)
        if len(others) == 1:
            dst[at] = first[at] + others[0][at]
        else:
            a = first[at].astype(f32)
            for o in others:
                a = a + o[at].astype(f32)
            dst[at] = a.astype(dst.dtype)

    if outer:

        @pl.loop(0, math.prod(outer))
        def _(i):
            block(split_index(i, outer))
    else:
        block(())


SQ = HEAD_DIM ** -0.5
FAR = float(2.0 ** 100)
BLK = 256


def nt(a, b):
    return lax.dot_general(a, b, (((1,), (1,)), ((), ())), preferred_element_type=f32)


def nn(a, b):
    return jnp.dot(a, b, preferred_element_type=f32)


def params(cid=None, mb=48):
    return pltpu.CompilerParams(collective_id=cid, has_side_effects=cid is not None, vmem_limit_bytes=mb << 20)


NINE = ((0, 0), (1, 0), (2, 0), (2, 2), (0, 2), (1, 2), (0, 1), (1, 1), (2, 1))
AT = {kh: i for i, kh in enumerate(NINE)}
TURN = (0, 2, 1)
TAILMB, MIDMB, FRONTMB = 48, 50, 60


def head(h):
    return slice(64 * h, 64 * h + 64)


class Sender:
    def __init__(self, ss, rs):
        self.ss, self.rs, self.all = ss, rs, []

    def __call__(self, src, dst, dev):
        i = len(self.all)
        c = rcopy(src, dst, self.ss.at[i], self.rs.at[i], dev)
        c.start()
        self.all.append(c)
        return c


AXES = (1, 2, 3)


class Spread:
    def __init__(self, p, send, own, to, rx, ry, rz):
        self.p, self.send, self.own, self.to = p, send, own, to
        self.rx, self.ry, self.rz = rx, ry, rz
        self.half = ry[0] + pl.multiple_of(p.yh * (ry[1] // 2), 8), ry[1] // 2
        self.quarter = rz[0] + pl.multiple_of(p.z * (rz[1] // 4), 8), rz[1] // 4

    def rows(self, what):
        a, n = what
        return pl.ds(a if isinstance(a, int) else pl.multiple_of(a, 8), n)

    def out(self, t, yl, what):
        return self.to.at[t, yl, self.p.core, self.rows(what)]

    def pass_on(self, t, yl, what, devs):
        return [self.send(self.out(t, yl, what), self.out(t, yl, what), d) for d in devs]

    def start(self):
        p = self.p
        nb = {"fsdp": (1 - p.yl) * 2 + p.core}
        mine = lambda what: self.own.at[self.rows(what)]
        push = lambda what, devs: [self.send(mine(what), self.out(p.x, p.yl, what), d) for d in devs]
        xs = [p.px(k)[0] for k in AXES]
        self.nz = push(self.quarter, [nb])[0] if self.rz[1] else None
        self.nx = push(self.rx, [nb])[0]
        self.xy = push(self.half, xs)
        self.xz = push(self.quarter, xs)
        self.yy = push(self.half, [p.py(k)[0] for k in (1, 3)])

    def second(self):
        p = self.p
        xs = [p.px(k)[0] for k in AXES]
        ys = [p.py(k)[0] for k in AXES]
        zs = [p.pz(k)[0] for k in AXES]
        self.nz.wait_recv()
        self.xz2 = self.pass_on(p.x, 1 - p.yl, self.quarter, xs)
        self.zz = self.pass_on(p.x, 1 - p.yl, self.quarter, zs)
        self.xx = [self.send(self.own.at[self.rows(self.rx)], self.out(p.x, p.yl, self.rx), d) for d in xs]
        self.nx.wait_recv()
        self.xx2 = self.pass_on(p.x, 1 - p.yl, self.rx, xs)
        for k in AXES:
            t = (p.x + 4 - k) % 4
            self.xy[k - 1].wait_recv()
            self.yy += self.pass_on(t, p.yl, self.half, ys)
            self.xz[k - 1].wait_recv()
            self.zz += self.pass_on(t, p.yl, self.quarter, zs)
        for k in AXES:
            t = (p.x + 4 - k) % 4
            self.xz2[k - 1].wait_recv()
            self.zz += self.pass_on(t, 1 - p.yl, self.quarter, zs)

    def finish(self):
        for c in self.yy + self.zz + self.xx + self.xx2:
            c.wait_recv()


def front_kernel(pw, ow, p1, p2, vec, xs, seg, W, V, R, S, po, m, x, p0, ss, rs, ls):
    def pack():
        ot = ow[...].astype(f32).T.astype(bf)
        p0[...] = jnp.concatenate([pw[k, :, head(h)] for k, h in NINE] + [ot[:, head(h)] for h in TURN], axis=1)

    p = Place()
    c = lax.axis_index("ctx")
    core, sib = p.core, p.sib()
    ctx = [{"ctx": q} for q in others(p)]
    greet([p.px(k)[0] for k in AXES] + [p.py(k)[0] for k in (1, 3)] + ctx + [sib], pack)
    send = Sender(ss, rs)
    own = pltpu.make_async_copy(p0, po.at[p.x, p.yl, core], ls.at[0])
    mine = pltpu.make_async_copy(vec, V.at[p.x, p.yl, core], ls.at[1])
    rows = pltpu.make_async_copy(xs.at[p.x], x, ls.at[2])
    up = pltpu.make_async_copy(p1, W.at[1, p.x, p.yl, core], ls.at[4])
    down = pltpu.make_async_copy(p2, W.at[2, p.x, p.yl, core], ls.at[5])
    for cp in (own, mine, rows, up, down):
        cp.start()
    nb = {"fsdp": (1 - p.yl) * 2 + core}
    first = Spread(p, send, p0, po, (0, 64), (64, 64), (128, 64))
    first.start()
    vn = send(vec, V.at[p.x, p.yl, core], nb)
    vx = [send(vec, V.at[p.x, p.yl, core], p.px(k)[0]) for k in AXES]
    sg = [send(seg, S.at[c], d) for d in ctx]
    sgo = pltpu.make_async_copy(seg, S.at[c], ls.at[3])
    sgo.start()
    d0 = [send(p0, po.at[p.x, p.yl, core], sib)]
    dv = [send(vec, V.at[p.x, p.yl, core], sib)]
    first.second()
    vn.wait_recv()
    vx += [send(V.at[p.x, 1 - p.yl, core], V.at[p.x, 1 - p.yl, core], p.px(k)[0]) for k in AXES]
    bulk = [
        Spread(p, send, p1, W.at[1], (0, 32), (32, 96), (128, 64)),
        Spread(p, send, p2, W.at[2], (0, 64), (64, 96), (160, 32)),
    ]
    for b in bulk:
        b.start()
    first.finish()
    for cp in vx:
        cp.wait_recv()
    own.wait()
    mine.wait()
    d0.append(send(po.at[p.x, 1 - p.yl, core], po.at[p.x, 1 - p.yl, core], sib))
    dv.append(send(V.at[p.x, 1 - p.yl, core], V.at[p.x, 1 - p.yl, core], sib))
    for k in AXES:
        t = (p.x + k) % 4
        d0.append(send(po.at[t, :, core], po.at[t, :, core], sib))
        dv.append(send(V.at[t, :, core], V.at[t, :, core], sib))
    for b in bulk:
        b.second()
    for cp in d0 + dv:
        cp.wait_recv()
    rows.wait()
    back = pltpu.make_async_copy(po, W.at[0], ls.at[0])
    back.start()

    @pl.loop(0, 4)
    def _(t):
        qv = V[t, 0, 0].astype(f32)
        b = [jnp.zeros((1, 64), f32) if k == 1 else qv[6 + k // 2 : 7 + k // 2, head(h)] for k, h in NINE]
        b = jnp.concatenate(b + [jnp.zeros((1, 192), f32)], axis=1)
        r = (nn(x[...], po[t].reshape(768, 768)) + b).astype(bf)
        m[2 * t] = r[:, :384]
        m[2 * t + 1] = jnp.concatenate([r[:, 384:576], r[:, 192:384]], axis=1)

    sw = [send(m.at[q], R.at[c], {"ctx": q}) for q in others(p)]
    swo = pltpu.make_async_copy(m.at[c], R.at[c], ls.at[2])
    swo.start()
    for b in bulk:
        b.finish()
    up.wait()
    down.wait()
    dw = []
    for k in range(4):
        t = (p.x + k) % 4
        dw.append(send(W.at[pl.ds(1, 2), t, :, core], W.at[pl.ds(1, 2), t, :, core], sib))
    for cp in sg + sw + dw:
        cp.wait_recv()
    for cp in send.all:
        cp.wait_send()
    for cp in (back, swo, sgo):
        cp.wait()


def front(pw, ow, p1, p2, vec, xs, seg, cid):
    sd = jax.ShapeDtypeStruct
    vm = pltpu.VMEM
    anywhere, here = pl.BlockSpec(memory_space=pl.ANY), pl.BlockSpec(memory_space=vm)
    count = 192
    return pl.pallas_call(
        front_kernel,
        out_shape=(
            sd((3, 4, 2, 2, 192, 768), bf),
            sd((4, 2, 2, 16, 192), bf),
            sd((8, BLK, 384), bf),
            sd((8, 2, 128), jnp.int32),
        ),
        in_specs=[here] * 4 + [anywhere] * 3,
        out_specs=[anywhere, here, anywhere, anywhere],
        scratch_shapes=[
            vm((4, 2, 2, 192, 768), bf),
            vm((8, BLK, 384), bf),
            vm((BLK, 768), bf),
            vm((192, 768), bf),
            pltpu.SemaphoreType.DMA((count,)),
            pltpu.SemaphoreType.DMA((count,)),
            pltpu.SemaphoreType.DMA((6,)),
        ],
        compiler_params=params(cid, FRONTMB),
    )(pw, ow, p1, p2, vec, xs, seg)


LONG = 2048 + BLK
SAFE = 120.0 / SQ
FWD = 8
BWD = 6


def blocks(edge, lst, par, unit):
    n = jnp.int32(0)
    for h in range(2):
        for i in range(8 if h == 0 else 4):
            qi = i if h == 0 else 2 * i + par
            lo, hi = jnp.int32(0), jnp.int32(0)
            for j in range(8):
                lo = lo + (edge[j, 1, 127] < edge[qi, 0, 0]).astype(jnp.int32)
                hi = hi + (edge[j, 0, 0] <= edge[qi, 1, 127]).astype(jnp.int32)

            def put(j, n):
                lst[n] = (h * 8 + qi) * 16 + j
                return n + 1

            n = lax.fori_loop(lo, hi, put, n)
    for k in range(unit - 1):
        lst[n + k] = 8
    return (n + unit - 1) // unit


def triple(code):
    j = code % 16
    i = (code // 16) % 8
    return code // 128, pl.ds(pl.multiple_of(i * BLK, BLK), BLK), pl.ds(pl.multiple_of(j * BLK, BLK), BLK), i


def lanes():
    return lax.broadcasted_iota(jnp.int32, (1, 128), 1)


def three(v, at, lane):
    a = v.astype(bf).astype(f32)
    b = (v - a).astype(bf).astype(f32)
    c = v - a - b
    return jnp.where(lane == at, a, jnp.where(lane == at + 1, b, jnp.where(lane == at + 2, c, 0.0))).astype(bf)


def flat(r, k):
    return r[:, :, 128 * k : 128 * k + 128].reshape(2048, 128)


def turned(v):
    return v.astype(f32).T.astype(bf)


def one_lane(h, lane):
    return lane == (72 if h == 0 else 8)


def doc_rows(docs):
    seg = jnp.concatenate([docs[j, i : i + 1] for j in range(8) for i in range(2)] + [jnp.full((1, BLK), -1)], axis=1)
    row = lax.broadcasted_iota(jnp.int32, (64, 1), 0)
    return seg, jnp.where(((row < 4) & (row != seg)) | ((row >= 8) & (row < 11)), 1.0, 0.0)


def attend_kernel(edge, docs, r, msg, acc, qa, kt, va, top, lst):
    par = lax.axis_index("ctx") % 2
    lane = lanes()
    count = blocks(edge, lst, par, FWD)
    seg, augk = doc_rows(docs)
    row = lax.broadcasted_iota(jnp.int32, (128, 1), 0) - 64
    augq = jnp.where(row == seg[:, :2048], -FAR, 0.0).T.astype(bf)
    augk = augk.astype(bf)
    vv = flat(r, 1)
    safe = jnp.bool_(True)
    for h in range(2):
        qk = flat(r, 2 * h)
        qa[h] = jnp.where(lane < 64, qk * bf(SQ), augq)
        kt[h, :64, :2048] = turned(qk)[64:]
        kt[h, :64, 2048:] = jnp.zeros((64, BLK), bf)
        kt[h, 64:] = augk
        va[h, :2048] = jnp.where((lane < 64) if h == 0 else (lane >= 64), vv, one_lane(h, lane).astype(bf))
        va[h, 2048:] = jnp.zeros((BLK, 128), bf)
        f = qk.astype(f32)
        safe = safe & (jnp.max(jnp.sum(f * f, axis=1, keepdims=True)) < SAFE)
    acc[...] = jnp.zeros_like(acc)

    @pl.when(jnp.logical_not(safe))
    def _():
        top[...] = jnp.full_like(top, -3e38)

        @pl.loop(0, count * FWD)
        def _(n):
            h, at, to, i = triple(lst[n])
            s = jnp.max(nn(qa[h, at], kt[h, :, to]), axis=1, keepdims=True)
            top[h, at] = jnp.maximum(top[h, at], s)

        for h in range(2):
            for i in range(8):
                at = slice(i * BLK, i * BLK + BLK)
                qa[h, at] = qa[h, at] + three(-top[h, at, :1], 72, lane)

    @pl.loop(0, count)
    def _(n):
        tr = [triple(lst[n * FWD + u]) for u in range(FWD)]
        ps = [nn(qa[h, at], kt[h, :, to]) for h, at, to, _ in tr]
        ps = [jnp.exp(p).astype(bf) for p in ps]
        got = [(h, at, nn(p, va[h, to])) for p, (h, at, to, _) in zip(ps, tr)]
        for h, at, o in got:
            acc[h, at] += o

    for i in range(8):
        at = slice(i * BLK, i * BLK + BLK)
        a = acc[0, at] * (1.0 / acc[0, at, 72:73])
        b = acc[1, at] * (1.0 / acc[1, at, 8:9])
        b = jnp.where(par == i % 2, b, 0.0)
        msg[i] = jnp.where(lane < 64, a, b).astype(bf)


def attend(docs, r):
    vm = pltpu.VMEM
    sd = jax.ShapeDtypeStruct
    return pl.pallas_call(
        attend_kernel,
        out_shape=(sd((8, BLK, 128), bf), sd((2, 2048, 128), f32), sd((2, 2048, 128), bf)),
        in_specs=[pl.BlockSpec(memory_space=pltpu.SMEM)] + [pl.BlockSpec(memory_space=vm)] * 2,
        out_specs=[pl.BlockSpec(memory_space=vm)] * 3,
        scratch_shapes=[
            vm((2, 128, LONG), bf),
            vm((2, LONG, 128), bf),
            vm((2, 2048, 128), f32),
            pltpu.SMEM((128,), jnp.int32),
        ],
        compiler_params=params(),
    )(docs, docs, r)


def unattend_kernel(edge, docs, r, dc, acc, qa, out, ka, va, kt, ga, gz, qz, dkv, dqt, lst):
    par = lax.axis_index("ctx") % 2
    lane = lanes()
    count = blocks(edge, lst, par, BWD)
    vv, gg = flat(r, 1), flat(dc, 0)
    tops = doc_rows(docs)[1].T.astype(bf)
    for h in range(2):
        qk = flat(r, 2 * h)
        low = (lane < 64) if h == 0 else (lane >= 64)
        at = 72 if h == 0 else 8
        kt[h, :, :2048] = turned(qk)[64:]
        kt[h, :, 2048:] = jnp.zeros((64, BLK), bf)
        ka[h, :2048] = jnp.concatenate([qk[:, 64:], tops[:2048]], axis=1)
        ka[h, 2048:] = jnp.concatenate([jnp.zeros((BLK, 64), bf), tops[2048:]], axis=1)
        ones = ((lane >= at) & (lane < at + 3)).astype(bf)
        va[h, :2048] = jnp.where(low, vv, ones)
        va[h, 2048:] = jnp.zeros((BLK, 128), bf)
        inv = 1.0 / acc[h, :, at : at + 1]
        g = jnp.where(low, gg.astype(f32), 0.0)
        g = (g * inv).astype(bf)
        delta = jnp.sum(g.astype(f32) * acc[h], axis=1, keepdims=True) * inv
        gz[h] = g
        ga[h] = g + three(-delta, at, lane)
        q = jnp.where(lane < 64, qa[h], bf(0))
        qz[h] = pltpu.roll(q.astype(f32), 64, 1).astype(bf) if h == 0 else q
    dqt[...] = jnp.zeros_like(dqt)
    dkv[...] = jnp.zeros_like(dkv)

    @pl.loop(0, count)
    def _(n):
        tr = [triple(lst[n * BWD + u]) for u in range(BWD)]
        ps = [nt(ka[h, to], qa[h, at]) for h, at, to, _ in tr]
        dp = [nt(va[h, to], ga[h, at]) for h, at, to, _ in tr]
        ps = [jnp.exp(p) for p in ps]
        ds = [(p * d).astype(bf) for p, d in zip(ps, dp)]
        ps = [p.astype(bf) for p in ps]
        kv = [nn(p, gz[h, at]) + nn(d, qz[h, at]) for p, d, (h, at, to, _) in zip(ps, ds, tr)]
        dq = [nn(kt[h, :, to], d) for d, (h, at, to, _) in zip(ds, tr)]
        got = [(h, at, to, a, b) for a, b, (h, at, to, _) in zip(kv, dq, tr)]
        for h, at, to, kv, dq in got:
            dkv[h, to] += kv
            dqt[h, :, at] += dq

    for i in range(8):
        a = slice(i * BLK, i * BLK + BLK)
        q0, q1 = [jnp.concatenate([(dqt[h, :, a] * SQ).T] * 2, axis=1) for h in range(2)]
        q1 = jnp.where(par == i % 2, q1, 0.0)
        kv0, kv1 = dkv[0, a], dkv[1, a]
        out[i, :, :128] = jnp.where(lane < 64, q0, kv0).astype(bf)
        out[i, :, 128:256] = jnp.where(lane < 64, kv0, kv1).astype(bf)
        out[i, :, 256:] = jnp.where(lane < 64, q1, pltpu.roll(kv1, 64, 1)).astype(bf)


def unattend(docs, r, dc, acc, qa):
    vm = pltpu.VMEM
    return pl.pallas_call(
        unattend_kernel,
        out_shape=jax.ShapeDtypeStruct((8, BLK, 384), bf),
        in_specs=[pl.BlockSpec(memory_space=pltpu.SMEM)] + [pl.BlockSpec(memory_space=vm)] * 5,
        out_specs=pl.BlockSpec(memory_space=vm),
        scratch_shapes=[
            vm((2, LONG, 128), bf),
            vm((2, LONG, 128), bf),
            vm((2, 64, LONG), bf),
            vm((2, 2048, 128), bf),
            vm((2, 2048, 128), bf),
            vm((2, 2048, 128), bf),
            vm((2, LONG, 128), f32),
            vm((2, 64, 2048), f32),
            pltpu.SMEM((128,), jnp.int32),
        ],
        compiler_params=params(),
    )(docs, docs, r, dc, acc, qa)


class Reducer:
    def __init__(self, p, send, order, refs):
        self.p, self.send, self.order = p, send, order
        self.acc, self.cor, self.r1, self.s1, self.r2, self.s2, self.r3 = refs
        self.peers = {"x": p.px, "y": p.py, "z": p.pz}
        self.here = {"x": p.x, "y": (p.yl, p.yh), "z": p.z}
        self.left = [[d for d in "xyz" if d not in order[:n]] for n in range(3)]

    def begin(self, src, sem):
        self.c0 = [self.send(src.at[:, :, 1 - self.p.core], self.cor, self.p.sib())]
        self.own = pltpu.make_async_copy(src.at[:, :, self.p.core], self.acc, sem)
        self.own.start()
        self.mine = self.acc

    def begin_at(self, src, t):
        self.c0 = ([] if t == 0 else self.c0) + [self.send(src.at[t, :, 1 - self.p.core], self.cor.at[t], self.p.sib())]
        self.own, self.mine = None, src.at[:, :, self.p.core]

    def scatter(self, src, into, n):
        a = self.order[n]
        return [
            self.send(pick(src, a, self.peers[a](j)[1], self.left[n]), into.at[j - 1], self.peers[a](j)[0]) for j in AXES
        ]

    def first(self):
        for c in self.c0:
            c.wait_recv()
        if self.own is not None:
            self.own.wait()
        total(self.acc, self.mine, [self.cor], shape_of("xyz"))
        self.c1 = self.scatter(self.acc, self.r1, 0)

    def gathered(self, copies, out, src, got, n):
        for c in copies:
            c.wait_recv()
        a = self.order[n]
        total(out, pick(src, a, self.here[a], self.left[n]), [got.at[j] for j in range(3)], shape_of(self.left[n + 1]))

    def second(self):
        self.gathered(self.c1, self.s1, self.acc, self.r1, 0)
        self.c2 = self.scatter(self.s1, self.r2, 1)

    def third(self):
        self.gathered(self.c2, self.s2, self.s1, self.r2, 1)
        self.c3 = self.scatter(self.s2, self.r3, 2)

    def result(self):
        for c in self.c3:
            c.wait_recv()
        a = self.order[2]
        m = pick(self.s2, a, self.here[a], self.left[2])[...].astype(f32)
        for j in range(3):
            m = m + self.r3[j].astype(f32)
        return m


def reducer_scratch(order, n):
    vm = pltpu.VMEM
    one, two = shape_of([d for d in "xyz" if d != order[0]]), shape_of(order[2])
    whole = (*shape_of("xyz"), 24, n)
    shapes = [whole, whole, (3, *one, 24, n), (*one, 24, n), (3, *two, 24, n), (*two, 24, n), (3, 24, n)]
    return [vm(s, bf) for s in shapes]


MID = ("yzx", "zyx", "xyz")
MIDN = 256


def norm_of(v):
    d = v - jnp.mean(v, axis=-1, keepdims=True)
    s = lax.rsqrt(jnp.mean(d * d, axis=-1, keepdims=True) + NORM_EPS)
    return d * s, s


def norm_back(g, xhat, s, gain):
    e = g * gain
    return s * (e - jnp.mean(e, axis=-1, keepdims=True) - xhat * jnp.mean(e * xhat, axis=-1, keepdims=True))


def down_sum(v):
    return jnp.sum(v, axis=0, keepdims=True)


def store_pieces(g, t, outs):
    n = 768 // len(outs)
    for i in range(32):
        at = (t, i // 16, i // 8 % 2, i // 4 % 2, i % 4)
        piece = g[24 * i : 24 * i + 24].astype(bf)
        for k, out in enumerate(outs):
            out[at] = piece[:, n * k : n * k + n]


def mid_kernel(w, cms, xs, cots, vec, LO, dh1, gup, go, DC, sums, o0, o1, o2, *refs):
    red = [[*refs[3 * i : 3 * i + 3], (o0, o1, o2)[i], None, None, None] for i in range(3)]
    refs = refs[9:]
    cm, wv, wo, zs, cdf, act, gs, ga, gb, gc, lob, dcm, x, cot, ss, rs, ls, os = refs
    p = Place()
    c = lax.axis_index("ctx")
    ctx = [{"ctx": q} for q in others(p)]
    greet([p.px(k)[0] for k in AXES] + [p.py(k)[0] for k in (1, 3)] + ctx + [p.sib()])
    send = Sender(ss, rs)

    def put(i, row):
        for k in range(6):
            sums[6 * i + k : 6 * i + k + 1] = row[:, 128 * k : 128 * k + 128]

    sw = [send(cms.at[q], cm.at[c], {"ctx": q}) for q in others(p)]
    swo = pltpu.make_async_copy(cms.at[c], cm.at[c], ls.at[12])
    swo.start()
    ins = [pltpu.make_async_copy(a.at[p.x], b, ls.at[n]) for a, b, n in ((xs, x, 13), (cots, cot, 14))]
    loads = []
    for k in range(3):
        for t in range(4):
            cp = pltpu.make_async_copy(w.at[k, t], wv.at[k * 4 + t], ls.at[k * 4 + t])
            cp.start()
            loads.append(cp)
    for cp in ins:
        cp.start()
    fours = [vec[0, f // 2, f % 2].astype(f32) for f in range(4)]
    pv = [jnp.concatenate([f[i : i + 1] for f in fours], axis=1) for i in range(6)]
    for t in range(4):
        loads[t].wait()
        o = wv[t, :, 576:768]
        wo[2 * t] = o[:, :128]
        wo[2 * t + 1] = jnp.concatenate([o[:, 128:], o[:, 64:128]], axis=1)
    swo.wait()
    for cp in ins:
        cp.wait()
    for cp in sw:
        cp.wait_recv()
    attn = jnp.zeros((BLK, 768), f32)
    for j in range(8):
        attn = attn + nt(cm[j], wo[j])
    h1 = x[...].astype(f32) + attn + pv[0]
    xh1, s1 = norm_of(h1)
    y1 = xh1 * pv[2] + pv[3]
    y1b = y1.astype(bf)
    ffn = jnp.zeros((BLK, 768), f32)
    for t in range(4):
        loads[4 + t].wait()
        z = nn(y1b, wv[4 + t]) + jnp.concatenate([vec[t, 0, 0, 8 + k : 9 + k].astype(f32) for k in range(4)], axis=1)
        e = 0.5 * (1.0 + lax.erf(z * (2.0**-0.5)))
        zs[t] = z
        cdf[t] = e
        a = (z * e).astype(bf)
        act[t] = a
        loads[8 + t].wait()
        ffn = ffn + nt(a, wv[8 + t])
    xh2, s2 = norm_of(y1 + ffn + pv[1])
    lob[...] = (xh2 * pv[4] + pv[5]).astype(bf)
    los = [send(lob, LO.at[p.x], p.px(k)[0]) for k in AXES]
    loo = pltpu.make_async_copy(lob, LO.at[p.x], ls.at[12])
    loo.start()
    g = cot[...].astype(f32)
    put(4, down_sum(g * xh2))
    put(5, down_sum(g))
    dh2 = norm_back(g, xh2, s2, pv[4])
    put(1, down_sum(dh2))
    dh2b = dh2.astype(bf)
    dh2t = dh2.T.astype(bf)
    y1t = y1.T.astype(bf)
    parts = [Reducer(p, send, o, r) for o, r in zip(MID, red)]
    for t in range(4):
        store_pieces(nn(dh2t, act[t]), t, (ga, gb, gc))
        for part, g3 in zip(parts, (ga, gb, gc)):
            part.begin_at(g3, t)
    dy1 = dh2
    outs = []
    for t in range(4):
        da = nn(dh2b, wv[8 + t]).astype(bf).astype(f32)
        z = zs[t]
        dz = da * (cdf[t] + z * (jnp.exp(-0.5 * z * z) * ((2.0 * math.pi) ** -0.5)))
        put(6 + t, down_sum(dz))
        dzb = dz.astype(bf)
        if t >= 2:
            outs[t - 2].wait()
        gs[t % 2] = nn(y1t, dzb).astype(bf)
        cp = pltpu.make_async_copy(gs.at[t % 2], gup.at[t], os.at[t % 2])
        cp.start()
        outs.append(cp)
        dy1 = dy1 + nt(dzb, wv[4 + t])
        if t == 0:
            for part in parts:
                part.first()
    put(2, down_sum(dy1 * xh1))
    put(3, down_sum(dy1))
    d1 = norm_back(dy1, xh1, s1, pv[2])
    dh1[...] = d1
    put(0, down_sum(d1))
    d1b = d1.astype(bf)
    d1t = d1.T.astype(bf)
    for j in range(8):
        dcm[j] = nn(d1b, wo[j]).astype(bf)
    sw = [send(dcm.at[q], DC.at[c], {"ctx": q}) for q in others(p)]
    swo = pltpu.make_async_copy(dcm.at[c], DC.at[c], ls.at[2])
    swo.start()
    for t in range(4):
        a, b = nn(d1t, cm[2 * t]), nn(d1t, cm[2 * t + 1])
        go[t] = jnp.concatenate([a[:, :64], a[:, 64:] + b[:, 64:], b[:, :64]], axis=1).astype(bf)
    for part in parts:
        part.gathered(part.c1, part.s1, part.acc, part.r1, 0)
    for cp in los + sw:
        cp.wait_recv()
    for cp in outs[2:] + [swo, loo]:
        cp.wait()
    for cp in send.all:
        cp.wait_send()


def middle(w, cms, xs, cots, vec, cid):
    vm = pltpu.VMEM
    sd = jax.ShapeDtypeStruct
    anywhere, here = pl.BlockSpec(memory_space=pl.ANY), pl.BlockSpec(memory_space=vm)
    left = [shape_of([d for d in "xyz" if d != o[0]]) for o in MID]
    seven = (4, 2, 2, 2, 4, 24)
    return pl.pallas_call(
        mid_kernel,
        out_shape=(
            sd((4, BLK, 768), bf),
            sd((BLK, 768), f32),
            sd((4, 768, 768), bf),
            sd((4, 768, 192), bf),
            sd((8, BLK, 128), bf),
            sd((60, 128), f32),
            *[sd((*s, 24, MIDN), bf) for s in left],
        ),
        in_specs=[anywhere] * 4 + [here],
        out_specs=[anywhere, here, anywhere, here, anywhere, here, here, here, here],
        scratch_shapes=sum([reducer_scratch(o, MIDN)[:3] for o in MID], [])
        + [
            vm((8, BLK, 128), bf),
            vm((12, 768, 768), bf),
            vm((8, 768, 128), bf),
            vm((4, BLK, 768), f32),
            vm((4, BLK, 768), f32),
            vm((4, BLK, 768), bf),
            vm((2, 768, 768), bf),
            vm((*seven, MIDN), bf),
            vm((*seven, MIDN), bf),
            vm((*seven, MIDN), bf),
            vm((BLK, 768), bf),
            vm((8, BLK, 128), bf),
            vm((BLK, 768), bf),
            vm((BLK, 768), bf),
            pltpu.SemaphoreType.DMA((48,)),
            pltpu.SemaphoreType.DMA((48,)),
            pltpu.SemaphoreType.DMA((15,)),
            pltpu.SemaphoreType.DMA((2,)),
        ],
        compiler_params=params(cid, MIDMB),
    )(w, cms, xs, cots, vec)


TAIL = ("xyz", "yzx", "zyx")
TAILN = (768, 384, 384)


def tail_kernel(dm, xs, dh1, w, go, gup, vin, n0, n1, n2, R1, R0, R2, V, IG, *refs):
    red, refs = [refs[7 * i : 7 * i + 7] for i in range(3)], refs[21:]
    more, refs = [[None] * 3 + [(n0, n1, n2)[i], *refs[3 * i : 3 * i + 3]] for i in range(3)], refs[9:]
    x, d, wv, ga, gb, igb, acc, vt, vr, ss, rs, ls = refs
    p = Place()
    c = lax.axis_index("ctx")
    core, sib = p.core, p.sib()
    ctx = [{"ctx": q} for q in others(p)]
    peers = {"x": p.px, "y": p.py, "z": p.pz}
    greet([p.px(k)[0] for k in AXES] + [p.py(k)[0] for k in (1, 3)] + ctx + [sib])
    send = Sender(ss, rs)
    parts = [Reducer(p, send, o, r) for o, r in zip(TAIL, red)]
    parts += [Reducer(p, send, o, r) for o, r in zip(MID, more)]
    parts[0].begin(gup, ls.at[0])
    sw = [send(dm.at[q], d.at[c], {"ctx": q}) for q in others(p)]
    swo = pltpu.make_async_copy(dm.at[c], d.at[c], ls.at[1])
    load = pltpu.make_async_copy(w.at[0], wv, ls.at[2])
    swo.start()
    rows = pltpu.make_async_copy(xs.at[p.x], x, ls.at[3])
    rows.start()
    load.start()
    parts[0].first()
    rows.wait()
    xt = x[...].astype(f32).T.astype(bf)
    acc[...] = dh1[...]
    swo.wait()
    load.wait()
    for cp in sw:
        cp.wait_recv()
    for q in (3, 4, 5):
        parts[q].c2 = parts[q].scatter(parts[q].s1, parts[q].r2, 1)
    vt[0, :60] = vin[...]
    for t in range(4):
        a, b = d[2 * t].astype(f32), d[2 * t + 1].astype(f32)
        pre = jnp.concatenate([a[:, :192], a[:, 192:] + b[:, 192:], b[:, :192]], axis=1)
        sums = jnp.concatenate([down_sum(pre), jnp.zeros((1, 64), f32)], axis=1)
        for k in range(5):
            vt[0, 60 + 5 * t + k : 61 + 5 * t + k] = sums[:, 128 * k : 128 * k + 128]
        pre = pre.astype(bf)
        g = jnp.concatenate([nn(xt, pre), go[t].astype(f32)], axis=1)
        store_pieces(g, t, (ga, gb))
        parts[1].begin_at(ga, t)
        parts[2].begin_at(gb, t)
        acc[...] += nt(pre, wv[t, :, :576])
    igb[...] = acc[...].astype(bf)
    IG[p.x] = igb[...]
    ig = [send(igb, IG.at[p.x], p.px(k)[0]) for k in AXES]
    cv = send(vt.at[0], vr.at[0, 0], sib)
    parts[1].first()
    parts[2].first()
    cv.wait_recv()
    vt[1] = vt[0] + vr[0, 0]

    def vsend(i, a):
        return [send(vt.at[i], vr.at[i, j - 1], peers[a](j)[0]) for j in AXES]

    def vsum(i, cs):
        for cp in cs:
            cp.wait_recv()
        return vt[i] + vr[i, 0] + vr[i, 1] + vr[i, 2]

    v1 = vsend(1, "z")
    for q in (3, 4, 5):
        parts[q].third()
    parts[0].second()
    vt[2] = vsum(1, v1)
    v2 = vsend(2, "y")
    for q in (1, 2):
        parts[q].second()
    vt[3] = vsum(2, v2)
    v3 = vsend(3, "x")
    for q in (0, 1, 2):
        parts[q].third()
    V[...] = vsum(3, v3)
    for cp in ig:
        cp.wait_recv()
    R1[...] = parts[0].result()
    for q in range(3):
        R2[:, MIDN * q : MIDN * q + MIDN] = parts[3 + q].result()
    R0[:, :384] = parts[1].result()
    R0[:, 384:] = parts[2].result()
    for cp in send.all:
        cp.wait_send()


def finale(dm, xs, dh1, w, go, gup, vin, n0, n1, n2, cid):
    vm = pltpu.VMEM
    sd = jax.ShapeDtypeStruct
    anywhere, here = pl.BlockSpec(memory_space=pl.ANY), pl.BlockSpec(memory_space=vm)
    scratch = sum([reducer_scratch(o, n) for o, n in zip(TAIL, TAILN)], [])
    scratch += sum([reducer_scratch(o, MIDN)[4:] for o in MID], [])
    seven = (4, 2, 2, 2, 4, 24)
    return pl.pallas_call(
        tail_kernel,
        out_shape=(sd((24, 768), f32), sd((24, 768), f32), sd((24, 768), f32), sd((80, 128), f32), sd((4, BLK, 768), bf)),
        in_specs=[anywhere, anywhere, here, anywhere, here, anywhere, here, here, here, here],
        out_specs=[here] * 5,
        scratch_shapes=scratch
        + [
            vm((BLK, 768), bf),
            vm((8, BLK, 384), bf),
            vm((4, 768, 768), bf),
            vm((*seven, 384), bf),
            vm((*seven, 384), bf),
            vm((BLK, 768), bf),
            vm((BLK, 768), f32),
            vm((4, 80, 128), f32),
            vm((4, 3, 80, 128), f32),
            pltpu.SemaphoreType.DMA((96,)),
            pltpu.SemaphoreType.DMA((96,)),
            pltpu.SemaphoreType.DMA((5,)),
        ],
        compiler_params=params(cid, TAILMB),
    )(dm, xs, dh1, w, go, gup.reshape(*seven, 768), vin, n0, n1, n2)


def finish_kernel(r1, r0, r2, v, g, R1, PG, OG, R2, PB, UB, B0, B1, B2, B3, B4, B5, IG):
    x, fc = lax.axis_index("tp"), lax.axis_index("fsdp") * 8 + lax.axis_index("ctx")
    IG[...] = g[...].astype(f32)
    R1[...] = r1[...]
    for i, out in enumerate((B0, B1, B2, B3, B4, B5)):
        row = jnp.concatenate([v[6 * i + k : 6 * i + k + 1] for k in range(6)], axis=1)
        row = pltpu.roll(jnp.broadcast_to(row, (8, 768)), (768 - 24 * fc) % 768, 1)
        out[...] = row[:1, :24]
    for k in range(6):
        UB[k : k + 1] = v[pl.ds(36 + 6 * x + k, 1)]
    b = jnp.concatenate([v[pl.ds(60 + 5 * x + k, 1)] for k in range(5)], axis=1)
    PB[...] = jnp.concatenate([jnp.concatenate([b[:, head(AT[k, h])] for h in range(3)], axis=1) for k in (0, 2)], axis=0)
    R2[...] = r2[...]
    p = r0[...]
    for k in range(3):
        PG[k] = jnp.concatenate([p[:, head(AT[k, h])] for h in range(3)], axis=1)
    OG[...] = jnp.concatenate([p[:, head(9 + TURN[h])] for h in range(3)], axis=1)


def finish(*args):
    sd = jax.ShapeDtypeStruct
    here = pl.BlockSpec(memory_space=pltpu.VMEM)
    shapes = [(24, 768), (3, 24, 192), (24, 192), (24, 768), (2, 192), (6, 128), *[(1, 24)] * 6, (4, BLK, 768)]
    return pl.pallas_call(
        finish_kernel,
        out_shape=tuple(sd(s, f32) for s in shapes),
        in_specs=[here] * 5,
        out_specs=[here] * 13,
        compiler_params=params(mb=24),
    )(*args)


def shards(
    layer_input,
    segment_ids,
    proj_weight,
    proj_bias,
    out_weight,
    out_bias,
    first_gain,
    first_shift,
    up_weight,
    up_bias,
    down_weight,
    down_bias,
    second_gain,
    second_shift,
    cotangent,
):
    tp = lax.axis_index("tp")
    rows = [out_bias, down_bias, first_gain, first_shift, second_gain, second_shift, proj_bias[0], proj_bias[1]]
    row = lax.broadcasted_iota(jnp.int32, (16, 192), 0)
    vec = jnp.zeros((16, 192), bf)
    for i, v in enumerate(rows + [up_bias[192 * k : 192 * k + 192] for k in range(4)]):
        vec = jnp.where(row == i, v[None], vec)
    seg = lax.dynamic_index_in_dim(segment_ids, tp, 0, keepdims=False).reshape(2, 128)
    w, vec, r, docs = front(proj_weight, out_weight, up_weight, down_weight.T, vec, layer_input, seg, 1)
    w = w.reshape(3, 4, 768, 768)
    cmsg, acc, qa = attend(docs, r)
    layer_output, dh1, gup, go, dc, sums, *firsts = middle(w, cmsg, layer_input, cotangent, vec, 2)
    dmsg = unattend(docs, r, dc, acc, qa)
    done = finale(dmsg, layer_input, dh1, w, go, gup, sums, *firsts, 3)
    r1, proj, out_grad, r2, pb, ub, b0, b1, b2, b3, b4, b5, input_grad = finish(*done)
    ob, db, g1, s1, g2, s2 = [b.reshape(24) for b in (b0, b1, b2, b3, b4, b5)]
    return (layer_output, input_grad, proj, pb, out_grad.T, ob, g1, s1, r1, ub.reshape(768), r2.T, db, g2, s2)


def solution(mesh):
    placed = (
        P("fsdp", "ctx", None),
        P("fsdp", "ctx"),
        P(None, "fsdp", "tp"),
        P(None, "tp"),
        P("tp", "fsdp"),
        P("fsdp"),
        P("fsdp"),
        P("fsdp"),
        P("fsdp", "tp"),
        P("tp"),
        P("tp", "fsdp"),
        P("fsdp"),
        P("fsdp"),
        P("fsdp"),
        P("fsdp", "ctx", None),
    )
    return jax.shard_map(
        shards,
        mesh=mesh,
        in_specs=placed,
        out_specs=(
            P("fsdp", "ctx", None),
            P("fsdp", "ctx", None),
            P(None, ("fsdp", "ctx"), "tp"),
            P(None, "tp"),
            P("tp", ("fsdp", "ctx")),
            P(("fsdp", "ctx")),
            P(("fsdp", "ctx")),
            P(("fsdp", "ctx")),
            P(("fsdp", "ctx"), "tp"),
            P("tp"),
            P("tp", ("fsdp", "ctx")),
            P(("fsdp", "ctx")),
            P(("fsdp", "ctx")),
            P(("fsdp", "ctx")),
        ),
        check_vma=False,
    )
```

```python
import functools
import math

import jax
import jax.numpy as jnp
from jax import lax
from jax.experimental import pallas as pl
from jax.experimental.pallas import tpu as pltpu
from jax.sharding import PartitionSpec as P

HEAD_DIM = 64
NORM_EPS = 1e-12

MESH = pl.DeviceIdType.MESH
bf=jnp.bfloat16; f32=jnp.float32

class Place:
    def __init__(self):
        self.x=lax.axis_index("tp"); f=lax.axis_index("fsdp"); c=lax.axis_index("ctx")
        self.yl=f//2; self.core=f%2; self.yh=c//4; self.z=c%4
        self.y=self.yh*2+self.yl
    def px(self,k):
        q=(self.x+k)%4
        return {"tp":q}, q
    def pz(self,k):
        q=(self.z+k)%4
        return {"ctx":self.yh*4+q}, q
    def py(self,k):
        q=(self.y+k)%4
        return {"fsdp":(q%2)*2+self.core,"ctx":(q//2)*4+self.z}, (q%2,q//2)
    def sib(self):
        return {"fsdp":self.yl*2+1-self.core}

def others(p):
    steps = ((1, 2), (1, 1), (1, 3), (1, 0), (0, 2), (0, 1), (0, 3))
    return [((p.yh + a) % 2) * 4 + (p.z + b) % 4 for a, b in steps]


def greet(devs, work=None):
    bar=pltpu.get_barrier_semaphore()
    for d in devs: pl.semaphore_signal(bar,inc=1,device_id=d,device_id_type=MESH)
    if work is not None:
        work()
    pl.semaphore_wait(bar,len(devs))

def rcopy(src,dst,ss,rs,dev):
    return pltpu.make_async_remote_copy(src_ref=src,dst_ref=dst,send_sem=ss,recv_sem=rs,device_id=dev,device_id_type=MESH)


DIMS = {"x": (4,), "y": (2, 2), "z": (4,)}
ORDER = ("xyz", "yzx", "zxy")


def shape_of(axes):
    return sum([DIMS[d] for d in "xyz" if d in axes], ())


def split_index(i, shape):
    out = []
    for s in reversed(shape):
        out.insert(0, i % s)
        i = i // s
    return tuple(out)


def pick(ref, axis, q, left):
    at = []
    for d in "xyz":
        if d in left:
            at += list(q if d == "y" else (q,)) if d == axis else [slice(None)] * len(DIMS[d])
    return ref.at[tuple(at)]


def total(dst, first, others, shape):
    outer = shape[: max(0, len(shape) - 2)] if len(shape) != 2 or shape == (4, 4) else ()
    outer = shape[:1] if shape == (4, 4) else outer

    def block(at):
        at = at + (Ellipsis,)
        if len(others) == 1:
            dst[at] = first[at] + others[0][at]
        else:
            a = first[at].astype(f32)
            for o in others:
                a = a + o[at].astype(f32)
            dst[at] = a.astype(dst.dtype)

    if outer:

        @pl.loop(0, math.prod(outer))
        def _(i):
            block(split_index(i, outer))
    else:
        block(())


SQ = HEAD_DIM ** -0.5
FAR = float(2.0 ** 100)
BLK = 256


def nt(a, b):
    return lax.dot_general(a, b, (((1,), (1,)), ((), ())), preferred_element_type=f32)


def nn(a, b):
    return jnp.dot(a, b, preferred_element_type=f32)


def params(cid=None, mb=48):
    return pltpu.CompilerParams(collective_id=cid, has_side_effects=cid is not None, vmem_limit_bytes=mb << 20)


NINE = ((0, 0), (1, 0), (2, 0), (2, 2), (0, 2), (1, 2), (0, 1), (1, 1), (2, 1))
AT = {kh: i for i, kh in enumerate(NINE)}
TURN = (0, 2, 1)
TAILMB, MIDMB, FRONTMB = 48, 50, 60


def head(h):
    return slice(64 * h, 64 * h + 64)


class Sender:
    def __init__(self, ss, rs):
        self.ss, self.rs, self.all = ss, rs, []

    def __call__(self, src, dst, dev):
        i = len(self.all)
        c = rcopy(src, dst, self.ss.at[i], self.rs.at[i], dev)
        c.start()
        self.all.append(c)
        return c


AXES = (1, 2, 3)


class Spread:
    def __init__(self, p, send, own, to, rx, ry, rz):
        self.p, self.send, self.own, self.to = p, send, own, to
        self.rx, self.ry, self.rz = rx, ry, rz
        self.half = ry[0] + pl.multiple_of(p.yh * (ry[1] // 2), 8), ry[1] // 2
        self.quarter = rz[0] + pl.multiple_of(p.z * (rz[1] // 4), 8), rz[1] // 4

    def rows(self, what):
        a, n = what
        return pl.ds(a if isinstance(a, int) else pl.multiple_of(a, 8), n)

    def out(self, t, yl, what):
        return self.to.at[t, yl, self.p.core, self.rows(what)]

    def pass_on(self, t, yl, what, devs):
        return [self.send(self.out(t, yl, what), self.out(t, yl, what), d) for d in devs]

    def start(self):
        p = self.p
        nb = {"fsdp": (1 - p.yl) * 2 + p.core}
        mine = lambda what: self.own.at[self.rows(what)]
        push = lambda what, devs: [self.send(mine(what), self.out(p.x, p.yl, what), d) for d in devs]
        xs = [p.px(k)[0] for k in AXES]
        self.nz = push(self.quarter, [nb])[0] if self.rz[1] else None
        self.nx = push(self.rx, [nb])[0]
        self.xy = push(self.half, xs)
        self.xz = push(self.quarter, xs)
        self.yy = push(self.half, [p.py(k)[0] for k in (1, 3)])

    def second(self):
        p = self.p
        xs = [p.px(k)[0] for k in AXES]
        ys = [p.py(k)[0] for k in AXES]
        zs = [p.pz(k)[0] for k in AXES]
        self.nz.wait_recv()
        self.xz2 = self.pass_on(p.x, 1 - p.yl, self.quarter, xs)
        self.zz = self.pass_on(p.x, 1 - p.yl, self.quarter, zs)
        self.xx = [self.send(self.own.at[self.rows(self.rx)], self.out(p.x, p.yl, self.rx), d) for d in xs]
        self.nx.wait_recv()
        self.xx2 = self.pass_on(p.x, 1 - p.yl, self.rx, xs)
        for k in AXES:
            t = (p.x + 4 - k) % 4
            self.xy[k - 1].wait_recv()
            self.yy += self.pass_on(t, p.yl, self.half, ys)
            self.xz[k - 1].wait_recv()
            self.zz += self.pass_on(t, p.yl, self.quarter, zs)
        for k in AXES:
            t = (p.x + 4 - k) % 4
            self.xz2[k - 1].wait_recv()
            self.zz += self.pass_on(t, 1 - p.yl, self.quarter, zs)

    def finish(self):
        for c in self.yy + self.zz + self.xx + self.xx2:
            c.wait_recv()


def front_kernel(pw, ow, p1, p2, vec, xs, seg, W, V, R, S, po, m, x, p0, ss, rs, ls):
    def pack():
        ot = ow[...].astype(f32).T.astype(bf)
        p0[...] = jnp.concatenate([pw[k, :, head(h)] for k, h in NINE] + [ot[:, head(h)] for h in TURN], axis=1)

    p = Place()
    c = lax.axis_index("ctx")
    core, sib = p.core, p.sib()
    ctx = [{"ctx": q} for q in others(p)]
    greet([p.px(k)[0] for k in AXES] + [p.py(k)[0] for k in (1, 3)] + ctx + [sib], pack)
    send = Sender(ss, rs)
    own = pltpu.make_async_copy(p0, po.at[p.x, p.yl, core], ls.at[0])
    mine = pltpu.make_async_copy(vec, V.at[p.x, p.yl, core], ls.at[1])
    rows = pltpu.make_async_copy(xs.at[p.x], x, ls.at[2])
    up = pltpu.make_async_copy(p1, W.at[1, p.x, p.yl, core], ls.at[4])
    down = pltpu.make_async_copy(p2, W.at[2, p.x, p.yl, core], ls.at[5])
    for cp in (own, mine, rows, up, down):
        cp.start()
    nb = {"fsdp": (1 - p.yl) * 2 + core}
    first = Spread(p, send, p0, po, (0, 64), (64, 64), (128, 64))
    first.start()
    vn = send(vec, V.at[p.x, p.yl, core], nb)
    vx = [send(vec, V.at[p.x, p.yl, core], p.px(k)[0]) for k in AXES]
    sg = [send(seg, S.at[c], d) for d in ctx]
    sgo = pltpu.make_async_copy(seg, S.at[c], ls.at[3])
    sgo.start()
    d0 = [send(p0, po.at[p.x, p.yl, core], sib)]
    dv = [send(vec, V.at[p.x, p.yl, core], sib)]
    first.second()
    vn.wait_recv()
    vx += [send(V.at[p.x, 1 - p.yl, core], V.at[p.x, 1 - p.yl, core], p.px(k)[0]) for k in AXES]
    bulk = [
        Spread(p, send, p1, W.at[1], (0, 32), (32, 96), (128, 64)),
        Spread(p, send, p2, W.at[2], (0, 64), (64, 96), (160, 32)),
    ]
    for b in bulk:
        b.start()
    first.finish()
    for cp in vx:
        cp.wait_recv()
    own.wait()
    mine.wait()
    d0.append(send(po.at[p.x, 1 - p.yl, core], po.at[p.x, 1 - p.yl, core], sib))
    dv.append(send(V.at[p.x, 1 - p.yl, core], V.at[p.x, 1 - p.yl, core], sib))
    for k in AXES:
        t = (p.x + k) % 4
        d0.append(send(po.at[t, :, core], po.at[t, :, core], sib))
        dv.append(send(V.at[t, :, core], V.at[t, :, core], sib))
    for b in bulk:
        b.second()
    for cp in d0 + dv:
        cp.wait_recv()
    rows.wait()
    back = pltpu.make_async_copy(po, W.at[0], ls.at[0])
    back.start()

    @pl.loop(0, 4)
    def _(t):
        qv = V[t, 0, 0].astype(f32)
        b = [jnp.zeros((1, 64), f32) if k == 1 else qv[6 + k // 2 : 7 + k // 2, head(h)] for k, h in NINE]
        b = jnp.concatenate(b + [jnp.zeros((1, 192), f32)], axis=1)
        r = (nn(x[...], po[t].reshape(768, 768)) + b).astype(bf)
        m[2 * t] = r[:, :384]
        m[2 * t + 1] = jnp.concatenate([r[:, 384:576], r[:, 192:384]], axis=1)

    sw = [send(m.at[q], R.at[c], {"ctx": q}) for q in others(p)]
    swo = pltpu.make_async_copy(m.at[c], R.at[c], ls.at[2])
    swo.start()
    for b in bulk:
        b.finish()
    up.wait()
    down.wait()
    dw = []
    for k in range(4):
        t = (p.x + k) % 4
        dw.append(send(W.at[pl.ds(1, 2), t, :, core], W.at[pl.ds(1, 2), t, :, core], sib))
    for cp in sg + sw + dw:
        cp.wait_recv()
    for cp in send.all:
        cp.wait_send()
    for cp in (back, swo, sgo):
        cp.wait()


def front(pw, ow, p1, p2, vec, xs, seg, cid):
    sd = jax.ShapeDtypeStruct
    vm = pltpu.VMEM
    anywhere, here = pl.BlockSpec(memory_space=pl.ANY), pl.BlockSpec(memory_space=vm)
    count = 192
    return pl.pallas_call(
        front_kernel,
        out_shape=(
            sd((3, 4, 2, 2, 192, 768), bf),
            sd((4, 2, 2, 16, 192), bf),
            sd((8, BLK, 384), bf),
            sd((8, 2, 128), jnp.int32),
        ),
        in_specs=[here] * 4 + [anywhere] * 3,
        out_specs=[anywhere, here, anywhere, anywhere],
        scratch_shapes=[
            vm((4, 2, 2, 192, 768), bf),
            vm((8, BLK, 384), bf),
            vm((BLK, 768), bf),
            vm((192, 768), bf),
            pltpu.SemaphoreType.DMA((count,)),
            pltpu.SemaphoreType.DMA((count,)),
            pltpu.SemaphoreType.DMA((6,)),
        ],
        compiler_params=params(cid, FRONTMB),
    )(pw, ow, p1, p2, vec, xs, seg)


LONG = 2048 + BLK
SAFE = 120.0 / SQ
FWD = 8
BWD = 8


def blocks(edge, lst, par, unit):
    n = jnp.int32(0)
    for h in range(2):
        for i in range(8 if h == 0 else 4):
            qi = i if h == 0 else 2 * i + par
            lo, hi = jnp.int32(0), jnp.int32(0)
            for j in range(8):
                lo = lo + (edge[j, 1, 127] < edge[qi, 0, 0]).astype(jnp.int32)
                hi = hi + (edge[j, 0, 0] <= edge[qi, 1, 127]).astype(jnp.int32)

            def put(j, n):
                lst[n] = (h * 8 + qi) * 16 + j
                return n + 1

            n = lax.fori_loop(lo, hi, put, n)
    for k in range(unit - 1):
        lst[n + k] = 8
    return (n + unit - 1) // unit


def triple(code):
    j = code % 16
    i = (code // 16) % 8
    return code // 128, pl.ds(pl.multiple_of(i * BLK, BLK), BLK), pl.ds(pl.multiple_of(j * BLK, BLK), BLK), i


def lanes():
    return lax.broadcasted_iota(jnp.int32, (1, 128), 1)


def three(v, at, lane):
    a = v.astype(bf).astype(f32)
    b = (v - a).astype(bf).astype(f32)
    c = v - a - b
    return jnp.where(lane == at, a, jnp.where(lane == at + 1, b, jnp.where(lane == at + 2, c, 0.0))).astype(bf)


def flat(r, k):
    return r[:, :, 128 * k : 128 * k + 128].reshape(2048, 128)


def turned(v):
    return v.astype(f32).T.astype(bf)


def one_lane(h, lane):
    return lane == (72 if h == 0 else 8)


def doc_rows(docs):
    seg = jnp.concatenate([docs[j, i : i + 1] for j in range(8) for i in range(2)] + [jnp.full((1, BLK), -1)], axis=1)
    row = lax.broadcasted_iota(jnp.int32, (64, 1), 0)
    return seg, jnp.where(((row < 4) & (row != seg)) | ((row >= 8) & (row < 11)), 1.0, 0.0)


def attend_kernel(edge, docs, r, msg, acc, qa, kt, va, top, lst):
    par = lax.axis_index("ctx") % 2
    lane = lanes()
    count = blocks(edge, lst, par, FWD)
    seg, augk = doc_rows(docs)
    row = lax.broadcasted_iota(jnp.int32, (128, 1), 0) - 64
    augq = jnp.where(row == seg[:, :2048], -FAR, 0.0).T.astype(bf)
    augk = augk.astype(bf)
    vv = flat(r, 1)
    safe = jnp.bool_(True)
    for h in range(2):
        qk = flat(r, 2 * h)
        qa[h] = jnp.where(lane < 64, qk * bf(SQ), augq)
        kt[h, :64, :2048] = turned(qk)[64:]
        kt[h, :64, 2048:] = jnp.zeros((64, BLK), bf)
        kt[h, 64:] = augk
        va[h, :2048] = jnp.where((lane < 64) if h == 0 else (lane >= 64), vv, one_lane(h, lane).astype(bf))
        va[h, 2048:] = jnp.zeros((BLK, 128), bf)
        f = qk.astype(f32)
        safe = safe & (jnp.max(jnp.sum(f * f, axis=1, keepdims=True)) < SAFE)
    acc[...] = jnp.zeros_like(acc)

    @pl.when(jnp.logical_not(safe))
    def _():
        top[...] = jnp.full_like(top, -3e38)

        @pl.loop(0, count * FWD)
        def _(n):
            h, at, to, i = triple(lst[n])
            s = jnp.max(nn(qa[h, at], kt[h, :, to]), axis=1, keepdims=True)
            top[h, at] = jnp.maximum(top[h, at], s)

        for h in range(2):
            for i in range(8):
                at = slice(i * BLK, i * BLK + BLK)
                qa[h, at] = qa[h, at] + three(-top[h, at, :1], 72, lane)

    @pl.loop(0, count)
    def _(n):
        tr = [triple(lst[n * FWD + u]) for u in range(FWD)]
        ps = [nn(qa[h, at], kt[h, :, to]) for h, at, to, _ in tr]
        ps = [jnp.exp(p).astype(bf) for p in ps]
        got = [(h, at, nn(p, va[h, to])) for p, (h, at, to, _) in zip(ps, tr)]
        for h, at, o in got:
            acc[h, at] += o

    for i in range(8):
        at = slice(i * BLK, i * BLK + BLK)
        a = acc[0, at] * (1.0 / acc[0, at, 72:73])
        b = acc[1, at] * (1.0 / acc[1, at, 8:9])
        b = jnp.where(par == i % 2, b, 0.0)
        msg[i] = jnp.where(lane < 64, a, b).astype(bf)


def attend(docs, r):
    vm = pltpu.VMEM
    sd = jax.ShapeDtypeStruct
    return pl.pallas_call(
        attend_kernel,
        out_shape=(sd((8, BLK, 128), bf), sd((2, 2048, 128), f32), sd((2, 2048, 128), bf)),
        in_specs=[pl.BlockSpec(memory_space=pltpu.SMEM)] + [pl.BlockSpec(memory_space=vm)] * 2,
        out_specs=[pl.BlockSpec(memory_space=vm)] * 3,
        scratch_shapes=[
            vm((2, 128, LONG), bf),
            vm((2, LONG, 128), bf),
            vm((2, 2048, 128), f32),
            pltpu.SMEM((128,), jnp.int32),
        ],
        compiler_params=params(),
    )(docs, docs, r)


def unattend_kernel(edge, docs, r, dc, acc, qa, out, ka, va, kt, ga, gz, qz, dkv, dqt, lst):
    par = lax.axis_index("ctx") % 2
    lane = lanes()
    count = blocks(edge, lst, par, BWD)
    vv, gg = flat(r, 1), flat(dc, 0)
    tops = doc_rows(docs)[1].T.astype(bf)
    for h in range(2):
        qk = flat(r, 2 * h)
        low = (lane < 64) if h == 0 else (lane >= 64)
        at = 72 if h == 0 else 8
        kt[h, :, :2048] = turned(qk)[64:]
        kt[h, :, 2048:] = jnp.zeros((64, BLK), bf)
        ka[h, :2048] = jnp.concatenate([qk[:, 64:], tops[:2048]], axis=1)
        ka[h, 2048:] = jnp.concatenate([jnp.zeros((BLK, 64), bf), tops[2048:]], axis=1)
        ones = ((lane >= at) & (lane < at + 3)).astype(bf)
        va[h, :2048] = jnp.where(low, vv, ones)
        va[h, 2048:] = jnp.zeros((BLK, 128), bf)
        inv = 1.0 / acc[h, :, at : at + 1]
        g = jnp.where(low, gg.astype(f32), 0.0)
        g = (g * inv).astype(bf)
        delta = jnp.sum(g.astype(f32) * acc[h], axis=1, keepdims=True) * inv
        gz[h] = g
        ga[h] = g + three(-delta, at, lane)
        q = jnp.where(lane < 64, qa[h], bf(0))
        qz[h] = pltpu.roll(q.astype(f32), 64, 1).astype(bf) if h == 0 else q
    dqt[...] = jnp.zeros_like(dqt)
    dkv[...] = jnp.zeros_like(dkv)

    @pl.loop(0, count)
    def _(n):
        tr = [triple(lst[n * BWD + u]) for u in range(BWD)]
        ps = [nt(ka[h, to], qa[h, at]) for h, at, to, _ in tr]
        dp = [nt(va[h, to], ga[h, at]) for h, at, to, _ in tr]
        ps = [jnp.exp(p) for p in ps]
        ds = [(p * d).astype(bf) for p, d in zip(ps, dp)]
        ps = [p.astype(bf) for p in ps]
        kv = [nn(p, gz[h, at]) + nn(d, qz[h, at]) for p, d, (h, at, to, _) in zip(ps, ds, tr)]
        dq = [nn(kt[h, :, to], d) for d, (h, at, to, _) in zip(ds, tr)]
        got = [(h, at, to, a, b) for a, b, (h, at, to, _) in zip(kv, dq, tr)]
        for h, at, to, kv, dq in got:
            dkv[h, to] += kv
            dqt[h, :, at] += dq

    for i in range(8):
        a = slice(i * BLK, i * BLK + BLK)
        q0, q1 = [jnp.concatenate([(dqt[h, :, a] * SQ).T] * 2, axis=1) for h in range(2)]
        q1 = jnp.where(par == i % 2, q1, 0.0)
        kv0, kv1 = dkv[0, a], dkv[1, a]
        out[i, :, :128] = jnp.where(lane < 64, q0, kv0).astype(bf)
        out[i, :, 128:256] = jnp.where(lane < 64, kv0, kv1).astype(bf)
        out[i, :, 256:] = jnp.where(lane < 64, q1, pltpu.roll(kv1, 64, 1)).astype(bf)


def unattend(docs, r, dc, acc, qa):
    vm = pltpu.VMEM
    return pl.pallas_call(
        unattend_kernel,
        out_shape=jax.ShapeDtypeStruct((8, BLK, 384), bf),
        in_specs=[pl.BlockSpec(memory_space=pltpu.SMEM)] + [pl.BlockSpec(memory_space=vm)] * 5,
        out_specs=pl.BlockSpec(memory_space=vm),
        scratch_shapes=[
            vm((2, LONG, 128), bf),
            vm((2, LONG, 128), bf),
            vm((2, 64, LONG), bf),
            vm((2, 2048, 128), bf),
            vm((2, 2048, 128), bf),
            vm((2, 2048, 128), bf),
            vm((2, LONG, 128), f32),
            vm((2, 64, 2048), f32),
            pltpu.SMEM((128,), jnp.int32),
        ],
        compiler_params=params(),
    )(docs, docs, r, dc, acc, qa)


class Reducer:
    def __init__(self, p, send, order, refs):
        self.p, self.send, self.order = p, send, order
        self.acc, self.cor, self.r1, self.s1, self.r2, self.s2, self.r3 = refs
        self.peers = {"x": p.px, "y": p.py, "z": p.pz}
        self.here = {"x": p.x, "y": (p.yl, p.yh), "z": p.z}
        self.left = [[d for d in "xyz" if d not in order[:n]] for n in range(3)]

    def begin(self, src, sem):
        self.c0 = [self.send(src.at[:, :, 1 - self.p.core], self.cor, self.p.sib())]
        self.own = pltpu.make_async_copy(src.at[:, :, self.p.core], self.acc, sem)
        self.own.start()
        self.mine = self.acc

    def begin_at(self, src, t):
        self.c0 = ([] if t == 0 else self.c0) + [self.send(src.at[t, :, 1 - self.p.core], self.cor.at[t], self.p.sib())]
        self.own, self.mine = None, src.at[:, :, self.p.core]

    def scatter(self, src, into, n):
        a = self.order[n]
        return [
            self.send(pick(src, a, self.peers[a](j)[1], self.left[n]), into.at[j - 1], self.peers[a](j)[0]) for j in AXES
        ]

    def first(self):
        for c in self.c0:
            c.wait_recv()
        if self.own is not None:
            self.own.wait()
        total(self.acc, self.mine, [self.cor], shape_of("xyz"))
        self.c1 = self.scatter(self.acc, self.r1, 0)

    def gathered(self, copies, out, src, got, n):
        for c in copies:
            c.wait_recv()
        a = self.order[n]
        total(out, pick(src, a, self.here[a], self.left[n]), [got.at[j] for j in range(3)], shape_of(self.left[n + 1]))

    def second(self):
        self.gathered(self.c1, self.s1, self.acc, self.r1, 0)
        self.c2 = self.scatter(self.s1, self.r2, 1)

    def third(self):
        self.gathered(self.c2, self.s2, self.s1, self.r2, 1)
        self.c3 = self.scatter(self.s2, self.r3, 2)

    def result(self):
        for c in self.c3:
            c.wait_recv()
        a = self.order[2]
        m = pick(self.s2, a, self.here[a], self.left[2])[...].astype(f32)
        for j in range(3):
            m = m + self.r3[j].astype(f32)
        return m


def reducer_scratch(order, n):
    vm = pltpu.VMEM
    one, two = shape_of([d for d in "xyz" if d != order[0]]), shape_of(order[2])
    whole = (*shape_of("xyz"), 24, n)
    shapes = [whole, whole, (3, *one, 24, n), (*one, 24, n), (3, *two, 24, n), (*two, 24, n), (3, 24, n)]
    return [vm(s, bf) for s in shapes]


MID = ("yzx", "zyx", "xyz")
MIDN = 256


def norm_of(v):
    d = v - jnp.mean(v, axis=-1, keepdims=True)
    s = lax.rsqrt(jnp.mean(d * d, axis=-1, keepdims=True) + NORM_EPS)
    return d * s, s


def norm_back(g, xhat, s, gain):
    e = g * gain
    return s * (e - jnp.mean(e, axis=-1, keepdims=True) - xhat * jnp.mean(e * xhat, axis=-1, keepdims=True))


def down_sum(v):
    return jnp.sum(v, axis=0, keepdims=True)


def store_pieces(g, t, outs):
    n = 768 // len(outs)
    for i in range(32):
        at = (t, i // 16, i // 8 % 2, i // 4 % 2, i % 4)
        piece = g[24 * i : 24 * i + 24].astype(bf)
        for k, out in enumerate(outs):
            out[at] = piece[:, n * k : n * k + n]


def mid_kernel(w, cms, xs, cots, vec, LO, dh1, gup, go, DC, sums, o0, o1, o2, *refs):
    red = [[*refs[3 * i : 3 * i + 3], (o0, o1, o2)[i], None, None, None] for i in range(3)]
    refs = refs[9:]
    cm, wv, wo, zs, cdf, act, gs, ga, gb, gc, lob, dcm, x, cot, ss, rs, ls, os = refs
    p = Place()
    c = lax.axis_index("ctx")
    ctx = [{"ctx": q} for q in others(p)]
    greet([p.px(k)[0] for k in AXES] + [p.py(k)[0] for k in (1, 3)] + ctx + [p.sib()])
    send = Sender(ss, rs)

    def put(i, row):
        for k in range(6):
            sums[6 * i + k : 6 * i + k + 1] = row[:, 128 * k : 128 * k + 128]

    sw = [send(cms.at[q], cm.at[c], {"ctx": q}) for q in others(p)]
    swo = pltpu.make_async_copy(cms.at[c], cm.at[c], ls.at[12])
    swo.start()
    ins = [pltpu.make_async_copy(a.at[p.x], b, ls.at[n]) for a, b, n in ((xs, x, 13), (cots, cot, 14))]
    loads = []
    for k in range(3):
        for t in range(4):
            cp = pltpu.make_async_copy(w.at[k, t], wv.at[k * 4 + t], ls.at[k * 4 + t])
            cp.start()
            loads.append(cp)
    for cp in ins:
        cp.start()
    fours = [vec[0, f // 2, f % 2].astype(f32) for f in range(4)]
    pv = [jnp.concatenate([f[i : i + 1] for f in fours], axis=1) for i in range(6)]
    for t in range(4):
        loads[t].wait()
        o = wv[t, :, 576:768]
        wo[2 * t] = o[:, :128]
        wo[2 * t + 1] = jnp.concatenate([o[:, 128:], o[:, 64:128]], axis=1)
    swo.wait()
    for cp in ins:
        cp.wait()
    for cp in sw:
        cp.wait_recv()
    attn = jnp.zeros((BLK, 768), f32)
    for j in range(8):
        attn = attn + nt(cm[j], wo[j])
    h1 = x[...].astype(f32) + attn + pv[0]
    xh1, s1 = norm_of(h1)
    y1 = xh1 * pv[2] + pv[3]
    y1b = y1.astype(bf)
    ffn = jnp.zeros((BLK, 768), f32)
    for t in range(4):
        loads[4 + t].wait()
        z = nn(y1b, wv[4 + t]) + jnp.concatenate([vec[t, 0, 0, 8 + k : 9 + k].astype(f32) for k in range(4)], axis=1)
        e = 0.5 * (1.0 + lax.erf(z * (2.0**-0.5)))
        zs[t] = z
        cdf[t] = e
        a = (z * e).astype(bf)
        act[t] = a
        loads[8 + t].wait()
        ffn = ffn + nt(a, wv[8 + t])
    xh2, s2 = norm_of(y1 + ffn + pv[1])
    lob[...] = (xh2 * pv[4] + pv[5]).astype(bf)
    los = [send(lob, LO.at[p.x], p.px(k)[0]) for k in AXES]
    loo = pltpu.make_async_copy(lob, LO.at[p.x], ls.at[12])
    loo.start()
    g = cot[...].astype(f32)
    put(4, down_sum(g * xh2))
    put(5, down_sum(g))
    dh2 = norm_back(g, xh2, s2, pv[4])
    put(1, down_sum(dh2))
    dh2b = dh2.astype(bf)
    dh2t = dh2.T.astype(bf)
    y1t = y1.T.astype(bf)
    parts = [Reducer(p, send, o, r) for o, r in zip(MID, red)]
    for t in range(4):
        store_pieces(nn(dh2t, act[t]), t, (ga, gb, gc))
        for part, g3 in zip(parts, (ga, gb, gc)):
            part.begin_at(g3, t)
    dy1 = dh2
    outs = []
    for t in range(4):
        da = nn(dh2b, wv[8 + t]).astype(bf).astype(f32)
        z = zs[t]
        dz = da * (cdf[t] + z * (jnp.exp(-0.5 * z * z) * ((2.0 * math.pi) ** -0.5)))
        put(6 + t, down_sum(dz))
        dzb = dz.astype(bf)
        if t >= 2:
            outs[t - 2].wait()
        gs[t % 2] = nn(y1t, dzb).astype(bf)
        cp = pltpu.make_async_copy(gs.at[t % 2], gup.at[t], os.at[t % 2])
        cp.start()
        outs.append(cp)
        dy1 = dy1 + nt(dzb, wv[4 + t])
        if t == 0:
            for part in parts:
                part.first()
    put(2, down_sum(dy1 * xh1))
    put(3, down_sum(dy1))
    d1 = norm_back(dy1, xh1, s1, pv[2])
    dh1[...] = d1
    put(0, down_sum(d1))
    d1b = d1.astype(bf)
    d1t = d1.T.astype(bf)
    for j in range(8):
        dcm[j] = nn(d1b, wo[j]).astype(bf)
    sw = [send(dcm.at[q], DC.at[c], {"ctx": q}) for q in others(p)]
    swo = pltpu.make_async_copy(dcm.at[c], DC.at[c], ls.at[2])
    swo.start()
    for t in range(4):
        a, b = nn(d1t, cm[2 * t]), nn(d1t, cm[2 * t + 1])
        go[t] = jnp.concatenate([a[:, :64], a[:, 64:] + b[:, 64:], b[:, :64]], axis=1).astype(bf)
    for part in parts:
        part.gathered(part.c1, part.s1, part.acc, part.r1, 0)
    for cp in los + sw:
        cp.wait_recv()
    for cp in outs[2:] + [swo, loo]:
        cp.wait()
    for cp in send.all:
        cp.wait_send()


def middle(w, cms, xs, cots, vec, cid):
    vm = pltpu.VMEM
    sd = jax.ShapeDtypeStruct
    anywhere, here = pl.BlockSpec(memory_space=pl.ANY), pl.BlockSpec(memory_space=vm)
    left = [shape_of([d for d in "xyz" if d != o[0]]) for o in MID]
    seven = (4, 2, 2, 2, 4, 24)
    return pl.pallas_call(
        mid_kernel,
        out_shape=(
            sd((4, BLK, 768), bf),
            sd((BLK, 768), f32),
            sd((4, 768, 768), bf),
            sd((4, 768, 192), bf),
            sd((8, BLK, 128), bf),
            sd((60, 128), f32),
            *[sd((*s, 24, MIDN), bf) for s in left],
        ),
        in_specs=[anywhere] * 4 + [here],
        out_specs=[anywhere, here, anywhere, here, anywhere, here, here, here, here],
        scratch_shapes=sum([reducer_scratch(o, MIDN)[:3] for o in MID], [])
        + [
            vm((8, BLK, 128), bf),
            vm((12, 768, 768), bf),
            vm((8, 768, 128), bf),
            vm((4, BLK, 768), f32),
            vm((4, BLK, 768), f32),
            vm((4, BLK, 768), bf),
            vm((2, 768, 768), bf),
            vm((*seven, MIDN), bf),
            vm((*seven, MIDN), bf),
            vm((*seven, MIDN), bf),
            vm((BLK, 768), bf),
            vm((8, BLK, 128), bf),
            vm((BLK, 768), bf),
            vm((BLK, 768), bf),
            pltpu.SemaphoreType.DMA((48,)),
            pltpu.SemaphoreType.DMA((48,)),
            pltpu.SemaphoreType.DMA((15,)),
            pltpu.SemaphoreType.DMA((2,)),
        ],
        compiler_params=params(cid, MIDMB),
    )(w, cms, xs, cots, vec)


TAIL = ("xyz", "yzx", "zyx")
TAILN = (768, 384, 384)


def tail_kernel(dm, xs, dh1, w, go, gup, vin, n0, n1, n2, R1, R0, R2, V, IG, *refs):
    red, refs = [refs[7 * i : 7 * i + 7] for i in range(3)], refs[21:]
    more, refs = [[None] * 3 + [(n0, n1, n2)[i], *refs[3 * i : 3 * i + 3]] for i in range(3)], refs[9:]
    x, d, wv, ga, gb, igb, acc, vt, vr, ss, rs, ls = refs
    p = Place()
    c = lax.axis_index("ctx")
    core, sib = p.core, p.sib()
    ctx = [{"ctx": q} for q in others(p)]
    peers = {"x": p.px, "y": p.py, "z": p.pz}
    greet([p.px(k)[0] for k in AXES] + [p.py(k)[0] for k in (1, 3)] + ctx + [sib])
    send = Sender(ss, rs)
    parts = [Reducer(p, send, o, r) for o, r in zip(TAIL, red)]
    parts += [Reducer(p, send, o, r) for o, r in zip(MID, more)]
    sw = [send(dm.at[q], d.at[c], {"ctx": q}) for q in others(p)]
    parts[0].begin(gup, ls.at[0])
    swo = pltpu.make_async_copy(dm.at[c], d.at[c], ls.at[1])
    load = pltpu.make_async_copy(w.at[0], wv, ls.at[2])
    swo.start()
    rows = pltpu.make_async_copy(xs.at[p.x], x, ls.at[3])
    rows.start()
    load.start()
    parts[0].first()
    rows.wait()
    xt = x[...].astype(f32).T.astype(bf)
    acc[...] = dh1[...]
    swo.wait()
    load.wait()
    for cp in sw:
        cp.wait_recv()
    for q in (3, 4, 5):
        parts[q].c2 = parts[q].scatter(parts[q].s1, parts[q].r2, 1)
    vt[0, :60] = vin[...]
    for t in range(4):
        a, b = d[2 * t].astype(f32), d[2 * t + 1].astype(f32)
        pre = jnp.concatenate([a[:, :192], a[:, 192:] + b[:, 192:], b[:, :192]], axis=1)
        sums = jnp.concatenate([down_sum(pre), jnp.zeros((1, 64), f32)], axis=1)
        for k in range(5):
            vt[0, 60 + 5 * t + k : 61 + 5 * t + k] = sums[:, 128 * k : 128 * k + 128]
        pre = pre.astype(bf)
        g = jnp.concatenate([nn(xt, pre), go[t].astype(f32)], axis=1)
        store_pieces(g, t, (ga, gb))
        parts[1].begin_at(ga, t)
        parts[2].begin_at(gb, t)
        acc[...] += nt(pre, wv[t, :, :576])
    igb[...] = acc[...].astype(bf)
    IG[p.x] = igb[...]
    ig = [send(igb, IG.at[p.x], p.px(k)[0]) for k in AXES]
    cv = send(vt.at[0], vr.at[0, 0], sib)
    parts[1].first()
    parts[2].first()
    cv.wait_recv()
    vt[1] = vt[0] + vr[0, 0]

    def vsend(i, a):
        return [send(vt.at[i], vr.at[i, j - 1], peers[a](j)[0]) for j in AXES]

    def vsum(i, cs):
        for cp in cs:
            cp.wait_recv()
        return vt[i] + vr[i, 0] + vr[i, 1] + vr[i, 2]

    v1 = vsend(1, "z")
    for q in (3, 4, 5):
        parts[q].third()
    parts[0].second()
    vt[2] = vsum(1, v1)
    v2 = vsend(2, "y")
    for q in (1, 2):
        parts[q].second()
    vt[3] = vsum(2, v2)
    v3 = vsend(3, "x")
    for q in (0, 1, 2):
        parts[q].third()
    V[...] = vsum(3, v3)
    for cp in ig:
        cp.wait_recv()
    R1[...] = parts[0].result()
    for q in range(3):
        R2[:, MIDN * q : MIDN * q + MIDN] = parts[3 + q].result()
    R0[:, :384] = parts[1].result()
    R0[:, 384:] = parts[2].result()
    for cp in send.all:
        cp.wait_send()


def finale(dm, xs, dh1, w, go, gup, vin, n0, n1, n2, cid):
    vm = pltpu.VMEM
    sd = jax.ShapeDtypeStruct
    anywhere, here = pl.BlockSpec(memory_space=pl.ANY), pl.BlockSpec(memory_space=vm)
    scratch = sum([reducer_scratch(o, n) for o, n in zip(TAIL, TAILN)], [])
    scratch += sum([reducer_scratch(o, MIDN)[4:] for o in MID], [])
    seven = (4, 2, 2, 2, 4, 24)
    return pl.pallas_call(
        tail_kernel,
        out_shape=(sd((24, 768), f32), sd((24, 768), f32), sd((24, 768), f32), sd((80, 128), f32), sd((4, BLK, 768), bf)),
        in_specs=[anywhere, anywhere, here, anywhere, here, anywhere, here, here, here, here],
        out_specs=[here] * 5,
        scratch_shapes=scratch
        + [
            vm((BLK, 768), bf),
            vm((8, BLK, 384), bf),
            vm((4, 768, 768), bf),
            vm((*seven, 384), bf),
            vm((*seven, 384), bf),
            vm((BLK, 768), bf),
            vm((BLK, 768), f32),
            vm((4, 80, 128), f32),
            vm((4, 3, 80, 128), f32),
            pltpu.SemaphoreType.DMA((96,)),
            pltpu.SemaphoreType.DMA((96,)),
            pltpu.SemaphoreType.DMA((5,)),
        ],
        compiler_params=params(cid, TAILMB),
    )(dm, xs, dh1, w, go, gup.reshape(*seven, 768), vin, n0, n1, n2)


def finish_kernel(r1, r0, r2, v, g, R1, PG, OG, R2, PB, UB, B0, B1, B2, B3, B4, B5, IG):
    x, fc = lax.axis_index("tp"), lax.axis_index("fsdp") * 8 + lax.axis_index("ctx")
    IG[...] = g[...].astype(f32)
    R1[...] = r1[...]
    for i, out in enumerate((B0, B1, B2, B3, B4, B5)):
        row = jnp.concatenate([v[6 * i + k : 6 * i + k + 1] for k in range(6)], axis=1)
        row = pltpu.roll(jnp.broadcast_to(row, (8, 768)), (768 - 24 * fc) % 768, 1)
        out[...] = row[:1, :24]
    for k in range(6):
        UB[k : k + 1] = v[pl.ds(36 + 6 * x + k, 1)]
    b = jnp.concatenate([v[pl.ds(60 + 5 * x + k, 1)] for k in range(5)], axis=1)
    PB[...] = jnp.concatenate([jnp.concatenate([b[:, head(AT[k, h])] for h in range(3)], axis=1) for k in (0, 2)], axis=0)
    R2[...] = r2[...]
    p = r0[...]
    for k in range(3):
        PG[k] = jnp.concatenate([p[:, head(AT[k, h])] for h in range(3)], axis=1)
    OG[...] = jnp.concatenate([p[:, head(9 + TURN[h])] for h in range(3)], axis=1)


def finish(*args):
    sd = jax.ShapeDtypeStruct
    here = pl.BlockSpec(memory_space=pltpu.VMEM)
    shapes = [(24, 768), (3, 24, 192), (24, 192), (24, 768), (2, 192), (6, 128), *[(1, 24)] * 6, (4, BLK, 768)]
    return pl.pallas_call(
        finish_kernel,
        out_shape=tuple(sd(s, f32) for s in shapes),
        in_specs=[here] * 5,
        out_specs=[here] * 13,
        compiler_params=params(mb=24),
    )(*args)


def shards(
    layer_input,
    segment_ids,
    proj_weight,
    proj_bias,
    out_weight,
    out_bias,
    first_gain,
    first_shift,
    up_weight,
    up_bias,
    down_weight,
    down_bias,
    second_gain,
    second_shift,
    cotangent,
):
    tp = lax.axis_index("tp")
    rows = [out_bias, down_bias, first_gain, first_shift, second_gain, second_shift, proj_bias[0], proj_bias[1]]
    row = lax.broadcasted_iota(jnp.int32, (16, 192), 0)
    vec = jnp.zeros((16, 192), bf)
    for i, v in enumerate(rows + [up_bias[192 * k : 192 * k + 192] for k in range(4)]):
        vec = jnp.where(row == i, v[None], vec)
    seg = lax.dynamic_index_in_dim(segment_ids, tp, 0, keepdims=False).reshape(2, 128)
    w, vec, r, docs = front(proj_weight, out_weight, up_weight, down_weight.T, vec, layer_input, seg, 1)
    w = w.reshape(3, 4, 768, 768)
    cmsg, acc, qa = attend(docs, r)
    layer_output, dh1, gup, go, dc, sums, *firsts = middle(w, cmsg, layer_input, cotangent, vec, 2)
    dmsg = unattend(docs, r, dc, acc, qa)
    done = finale(dmsg, layer_input, dh1, w, go, gup, sums, *firsts, 3)
    r1, proj, out_grad, r2, pb, ub, b0, b1, b2, b3, b4, b5, input_grad = finish(*done)
    ob, db, g1, s1, g2, s2 = [b.reshape(24) for b in (b0, b1, b2, b3, b4, b5)]
    return (layer_output, input_grad, proj, pb, out_grad.T, ob, g1, s1, r1, ub.reshape(768), r2.T, db, g2, s2)


def solution(mesh):
    placed = (
        P("fsdp", "ctx", None),
        P("fsdp", "ctx"),
        P(None, "fsdp", "tp"),
        P(None, "tp"),
        P("tp", "fsdp"),
        P("fsdp"),
        P("fsdp"),
        P("fsdp"),
        P("fsdp", "tp"),
        P("tp"),
        P("tp", "fsdp"),
        P("fsdp"),
        P("fsdp"),
        P("fsdp"),
        P("fsdp", "ctx", None),
    )
    return jax.shard_map(
        shards,
        mesh=mesh,
        in_specs=placed,
        out_specs=(
            P("fsdp", "ctx", None),
            P("fsdp", "ctx", None),
            P(None, ("fsdp", "ctx"), "tp"),
            P(None, "tp"),
            P("tp", ("fsdp", "ctx")),
            P(("fsdp", "ctx")),
            P(("fsdp", "ctx")),
            P(("fsdp", "ctx")),
            P(("fsdp", "ctx"), "tp"),
            P("tp"),
            P("tp", ("fsdp", "ctx")),
            P(("fsdp", "ctx")),
            P(("fsdp", "ctx")),
            P(("fsdp", "ctx")),
        ),
        check_vma=False,
    )
```
